32 devices in a mesh: dp: 8 (over z, x), mp: 4 (over y, core).
Axes of the slice: x: 2, y: 2, z: 4, core: 2. Of those that a mesh axis runs over, the one named last changes fastest.
Arguments:
- inputs: bfloat16 [16384, 768], P('dp'), may hold values from -6 to 6
- segment_ids: int32 [32, 512], P('dp'), may hold values from 0 to 7, never falling along the last dimension, each value on 1 to 128 neighbouring positions
- cotangent: bfloat16 [16384, 768], P('dp'), may hold values from -6 to 6
- query_weight: bfloat16 [768, 768], P(None, 'mp'), may hold values from -0.3125 to 0.3125
- key_weight: bfloat16 [768, 768], P(None, 'mp'), may hold values from -0.21875 to 0.21875
- value_weight: bfloat16 [768, 768], P(None, 'mp'), may hold values from -0.21875 to 0.21875
- query_bias: float32 [768], P('mp'), may hold values from -3 to 3
- value_bias: float32 [768], P('mp'), may hold values from -3 to 3
- output_weight: bfloat16 [768, 768], P('mp'), may hold values from -0.875 to 0.875
- output_bias: float32 [768], replicated, may hold values from -3 to 3
- middle_gain: float32 [768], replicated, may hold values from 0.5 to 1.5
- middle_shift: float32 [768], replicated, may hold values from -3 to 3
- up_weight: bfloat16 [768, 3072], P(None, 'mp'), may hold values from -0.21875 to 0.21875
- up_bias: float32 [3072], P('mp'), may hold values from -3 to 3
- down_weight: bfloat16 [3072, 768], P('mp'), may hold values from -0.15625 to 0.15625
- down_bias: float32 [768], replicated, may hold values from -3 to 3
- final_gain: float32 [768], replicated, may hold values from 0.5 to 1.5
- final_shift: float32 [768], replicated, may hold values from -3 to 3
Outputs:
- layer_out: bfloat16 [16384, 768], P(('dp', 'mp'))
- input_grad: bfloat16 [16384, 768], P(('dp', 'mp'))
- grad_query_weight: float32 [768, 768], P(None, 'mp')
- grad_key_weight: float32 [768, 768], P(None, 'mp')
- grad_value_weight: float32 [768, 768], P(None, 'mp')
- grad_query_bias: float32 [768], P('mp')
- grad_value_bias: float32 [768], P('mp')
- grad_output_weight: float32 [768, 768], P('mp')
- grad_output_bias: float32 [768], replicated
- grad_middle_gain: float32 [768], replicated
- grad_middle_shift: float32 [768], replicated
- grad_up_weight: float32 [768, 3072], P(None, 'mp')
- grad_up_bias: float32 [3072], P('mp')
- grad_down_weight: float32 [3072, 768], P('mp')
- grad_down_bias: float32 [768], replicated
- grad_final_gain: float32 [768], replicated
- grad_final_shift: float32 [768], replicated
The draws below stay inside these ranges and needn't reach their ends.
Inputs may be any that keep to these rules, and one draw needn't show every extreme that they name: `segment_ids`: in each row of 512 positions the passage numbers 0 to 7 appear in rising order, each on 1 to 128 consecutive positions, one on exactly 128.
All inputs are finite; a program needn't handle non-finite values.
Results may differ from the reference program's by a relative error of at most 0.025.
Values may be sent and summed in bfloat16 or wider, within the bound.
No kernel may reach another device: no remote copies, remote signals or barrier semaphores. Data moves between devices by JAX's collectives and lax.ppermute only.
A program may use at most 128 MiB of HBM per device.

```python
import math
from functools import partial
import jax
import jax.numpy as jnp
import numpy as np
from jax import lax

D = 768
HEAD = 64
FF = 3072
SEQ = 512
SEGS = 8
ROWS = 32
TOKENS = 16384
N_MP = 4


def shard_levels(stream_key, extent, split, least, largest):
    level, own = 1.0, jax.random.fold_in(stream_key, 6)
    for axis_at, parts in split:
        steps = jnp.exp(jax.random.uniform(jax.random.fold_in(own, axis_at), (parts,), jnp.float32, least / len(split), largest / len(split)))
        level = level * jnp.repeat(steps, extent[axis_at] // parts).reshape([-1 if axis == axis_at else 1 for axis in range(len(extent))])
    return level


def split_up(amount, total, most, lean):
    loads = [(1 << 20) // math.isqrt(rank ** lean) + 1 for rank in range(2, amount + 1)]
    surplus, counts = total - most - (amount - 1), [1] * (amount - 1)
    while surplus > 0:
        free = [i for i in range(amount - 1) if counts[i] < most]
        whole, budget = sum([loads[i] for i in free]), surplus
        for i in free:
            addition = min(most - counts[i], max(1, budget * loads[i] // whole), surplus)
            counts[i] = counts[i] + addition
            surplus = surplus - addition
    return np.array([most] + counts)


def uneven(key, count, total, reach, slope):
    if count == 2:
        one = jax.random.randint(key, (), max(1, total - reach), min(reach, total - 1) + 1)
        return jnp.stack([one, total - one])
    sizes = jnp.asarray(split_up(count, total, reach, slope), jnp.int32)
    couples = (count - 1) // 2
    donor, sink = sizes[1:1 + 2 * couples:2], sizes[2:2 + 2 * couples:2]
    room = jnp.minimum(donor - 1, reach - sink)
    passed = jax.random.randint(jax.random.fold_in(key, 1), (couples,), 0, 1 << 20) % (room + 1)
    sizes = sizes.at[1:1 + 2 * couples:2].set(donor - passed).at[2:2 + 2 * couples:2].set(sink + passed)
    return sizes[jax.random.permutation(jax.random.fold_in(key, 2), count)]


def gaussian(own_key, shape, scale, most, cuts=(), dtype=jnp.bfloat16):
    result = scale * jax.random.normal(own_key, shape, jnp.float32)
    if cuts:
        result = result * shard_levels(own_key, shape, cuts, -0.22, 0.18)
    return jnp.clip(result, -most, most).astype(dtype)


def setup_inputs(seed: int = 0) -> dict:
    key_of = jax.random.split(jax.random.key(seed), 19)
    inputs = gaussian(key_of[0], (TOKENS, D), 1.0, 6.0, ((0, 8),))
    segment_ids = jax.vmap(lambda own: jnp.searchsorted(jnp.cumsum(uneven(own, SEGS, SEQ, SEQ // 4, 2)), jnp.arange(SEQ), side="right"))(jax.random.split(key_of[1], ROWS)).reshape((ROWS, SEQ)).astype(jnp.int32)
    cotangent = gaussian(key_of[2], (TOKENS, D), 1.0, 6.0, ((0, 8),))
    query_weight = gaussian(key_of[3], (D, D), (D // 2) ** -0.5, 0.3125, ((1, 4),))
    key_weight = gaussian(key_of[4], (D, D), D ** -0.5, 0.21875, ((1, 4),))
    value_weight = gaussian(key_of[5], (D, D), D ** -0.5, 0.21875, ((1, 4),))
    query_bias = gaussian(key_of[6], (D,), 0.5, 3.0, ((0, 4),), jnp.float32)
    value_bias = gaussian(key_of[7], (D,), 0.5, 3.0, ((0, 4),), jnp.float32)
    output_weight = gaussian(key_of[8], (D, D), (D // 16) ** -0.5, 0.875, ((0, 4),))
    output_bias = gaussian(key_of[9], (D,), 0.5, 3.0, (), jnp.float32)
    middle_gain = jnp.clip(1.0 + 0.1 * jax.random.normal(key_of[10], (D,), jnp.float32), 0.5, 1.5)
    middle_shift = gaussian(key_of[11], (D,), 0.5, 3.0, (), jnp.float32)
    up_weight = gaussian(key_of[12], (D, FF), D ** -0.5, 0.21875, ((1, 4),))
    up_bias = gaussian(key_of[13], (FF,), 0.5, 3.0, ((0, 4),), jnp.float32)
    down_weight = gaussian(key_of[14], (FF, D), (FF // 2) ** -0.5, 0.15625, ((0, 4),))
    down_bias = gaussian(key_of[15], (D,), 0.5, 3.0, (), jnp.float32)
    final_gain = jnp.clip(1.0 + 0.1 * jax.random.normal(key_of[16], (D,), jnp.float32), 0.5, 1.5)
    final_shift = gaussian(key_of[17], (D,), 0.5, 3.0, (), jnp.float32)
    return {"inputs": inputs, "segment_ids": segment_ids, "cotangent": cotangent, "query_weight": query_weight, "key_weight": key_weight, "value_weight": value_weight, "query_bias": query_bias, "value_bias": value_bias, "output_weight": output_weight, "output_bias": output_bias, "middle_gain": middle_gain, "middle_shift": middle_shift, "up_weight": up_weight, "up_bias": up_bias, "down_weight": down_weight, "down_bias": down_bias, "final_gain": final_gain, "final_shift": final_shift}


@jax.custom_vjp
def low(v):
    return lax.optimization_barrier(v.astype(jnp.bfloat16)).astype(jnp.float32)

@jax.custom_vjp
def low_back(v):
    return v

def low_keep(v):
    return (low(v), None)

def low_pass(kept, grad):
    return (grad,)

def back_keep(v):
    return (v, None)

def back_low(kept, grad):
    return (low(grad),)
low.defvjp(low_keep, low_pass)
low_back.defvjp(back_keep, back_low)
EPSILON = 1e-12
ROOT_HALF = 0.7071067811865476
MASKED = -1e+30
HIGH = lax.Precision.HIGHEST

def layer_norm(values, gain, shift):
    centred = values - lax.optimization_barrier(jnp.mean(values, axis=-1, keepdims=True))
    variance = lax.optimization_barrier(jnp.mean(centred * centred, axis=-1, keepdims=True))
    return centred * lax.rsqrt(variance + EPSILON) * gain + shift

def gelu_value(pre_act):
    return 0.5 * pre_act * (1.0 + lax.erf(pre_act * ROOT_HALF))

def attend_reference(head_size, pieces):
    queries, keys_row, values_row, seg_row = pieces
    seq_len, width = queries.shape
    head_shape = (seq_len, width // head_size, head_size)
    raw_scores = jnp.einsum('qhd,khd->hqk', queries.reshape(head_shape), keys_row.reshape(head_shape), precision=HIGH)
    scores = low_back(raw_scores) * head_size ** (-0.5)
    same = seg_row[:, None] == seg_row[None, :]
    scores = jnp.where(same[None], scores, MASKED)
    top = lax.optimization_barrier(jnp.max(scores, axis=-1, keepdims=True))
    expo = jnp.exp(scores - top)
    probs = expo / lax.optimization_barrier(jnp.sum(expo, axis=-1, keepdims=True))
    context = jnp.einsum('hqk,khd->qhd', low(probs), values_row.reshape(head_shape), precision=HIGH)
    return context.reshape(seq_len, width)

def layer_forward(weight_set, entry_rows, seg_block):
    query_weight, key_weight, value_weight, query_bias, value_bias, output_weight, output_bias, middle_gain, middle_shift, up_weight, up_bias, down_weight, down_bias, final_gain, final_shift = weight_set
    rows_here = seg_block.shape[0]
    group_width = D // N_MP
    unit_width = FF // N_MP
    attend = jax.checkpoint(partial(attend_reference, HEAD))
    attn_total = jnp.zeros_like(entry_rows)
    for member in range(N_MP):
        columns = slice(member * group_width, (member + 1) * group_width)
        group_entry = low_back(entry_rows)
        queries = low(low_back(jnp.dot(group_entry, query_weight[:, columns], precision=HIGH) + query_bias[columns]))
        keys_all = low(low_back(jnp.dot(group_entry, key_weight[:, columns], precision=HIGH)))
        values_all = low(low_back(jnp.dot(group_entry, value_weight[:, columns], precision=HIGH) + value_bias[columns]))
        row_shape = (rows_here, SEQ, group_width)
        context = lax.map(attend, (queries.reshape(row_shape), keys_all.reshape(row_shape), values_all.reshape(row_shape), seg_block))
        context = low(low_back(context.reshape(-1, group_width)))
        attn_total = attn_total + low(low_back(jnp.dot(context, output_weight[columns, :], precision=HIGH)))
    middle = attn_total + output_bias + entry_rows
    hidden = layer_norm(middle, middle_gain, middle_shift)
    hidden_low = low(hidden)
    ffn_total = jnp.zeros_like(entry_rows)
    for member in range(N_MP):
        units = slice(member * unit_width, (member + 1) * unit_width)
        group_entry = low_back(hidden_low)
        pre_act = low_back(jnp.dot(group_entry, up_weight[:, units], precision=HIGH) + up_bias[units])
        activ = low(gelu_value(pre_act))
        ffn_total = ffn_total + low(low_back(jnp.dot(activ, down_weight[units, :], precision=HIGH)))
    final = ffn_total + down_bias + hidden
    return layer_norm(final, final_gain, final_shift)

def reference(inputs, segment_ids, cotangent, query_weight, key_weight, value_weight, query_bias, value_bias, output_weight, output_bias, middle_gain, middle_shift, up_weight, up_bias, down_weight, down_bias, final_gain, final_shift):
    weights = tuple((weight_arg.astype(jnp.float32) for weight_arg in (query_weight, key_weight, value_weight, query_bias, value_bias, output_weight, output_bias, middle_gain, middle_shift, up_weight, up_bias, down_weight, down_bias, final_gain, final_shift)))
    rows_total = segment_ids.shape[0]
    block_rows = 8 if rows_total % 8 == 0 else 1
    blocks = rows_total // block_rows
    entries = inputs.astype(jnp.float32).reshape(blocks, block_rows * SEQ, D)
    cot_blocks = cotangent.astype(jnp.float32).reshape(blocks, block_rows * SEQ, D)
    seg_blocks = segment_ids.reshape(blocks, block_rows, SEQ)

    def one_block(totals, pieces):
        entry_block, seg_block, cot_block = pieces

        def run_layer(weight_set, entry_set):
            return layer_forward(weight_set, entry_set, seg_block)
        output, pullback = jax.vjp(run_layer, weights, entry_block)
        grad_weights, grad_entry = pullback(cot_block)
        totals = jax.tree.map(jnp.add, totals, grad_weights)
        return (totals, (output.astype(jnp.bfloat16), grad_entry.astype(jnp.bfloat16)))
    initial = jax.tree.map(jnp.zeros_like, weights)
    totals, (outputs, entry_grads) = lax.scan(one_block, initial, (entries, seg_blocks, cot_blocks))
    grad_query_weight, grad_key_weight, grad_value_weight, grad_query_bias, grad_value_bias, grad_output_weight, grad_output_bias, grad_middle_gain, grad_middle_shift, grad_up_weight, grad_up_bias, grad_down_weight, grad_down_bias, grad_final_gain, grad_final_shift = totals
    return (outputs.reshape(-1, D), entry_grads.reshape(-1, D), grad_query_weight, grad_key_weight, grad_value_weight, grad_query_bias, grad_value_bias, grad_output_weight, grad_output_bias, grad_middle_gain, grad_middle_shift, grad_up_weight, grad_up_bias, grad_down_weight, grad_down_bias, grad_final_gain, grad_final_shift)
```

```python
from functools import partial

import jax
import jax.numpy as jnp
from jax import lax
from jax.experimental import pallas as pl
from jax.experimental.pallas import tpu as pltpu
from jax.sharding import PartitionSpec as P

HEAD = 64
BAND = 128
EPSILON = 1e-12
ROOT_HALF = 0.7071067811865476
INV_ROOT_TAU = 0.3989422804014327
MASKED = -1e30
F32 = jnp.float32
BF16 = jnp.bfloat16
VMEM_LIMIT = 60 * 1024 * 1024


def nn(a, b):
    return lax.dot_general(a, b, (((1,), (0,)), ((), ())), preferred_element_type=F32)


def nt(a, b):
    return lax.dot_general(a, b, (((1,), (1,)), ((), ())), preferred_element_type=F32)


def tn(a, b):
    return lax.dot_general(a, b, (((0,), (0,)), ((), ())), preferred_element_type=F32)


def window(block, seq):
    lo = max(block * BAND - BAND, 0)
    hi = min(block * BAND + 2 * BAND, seq)
    return lo, hi


def params():
    return pltpu.CompilerParams(vmem_limit_bytes=VMEM_LIMIT)


def cost(flops, moved, trans=0):
    return pl.CostEstimate(flops=int(flops), bytes_accessed=int(moved), transcendentals=int(trans))


def whole(shape):
    return pl.BlockSpec(shape, lambda *_: (0,) * len(shape))


def attend_fwd_kernel(base, idx, x_ref, seg_ref, wq, wk, wv, wo, qb, vb, *rest):
    q_ref, k_ref, v_ref, p_ref, ctx_ref, part_ref = rest[-6:]
    seq, width = q_ref.shape[1:]
    row = jnp.bitwise_xor(idx[0], base - 2 * pl.program_id(0))
    x = x_ref[...]
    q_ref[0] = ((nn(x, wq[...]) + qb[...]).astype(BF16) * (HEAD**-0.5)).astype(BF16)
    k_ref[0] = nn(x, wk[...]).astype(BF16)
    v_ref[0] = (nn(x, wv[...]) + vb[...]).astype(BF16)
    seg_row = seg_ref[pl.ds(row, 1), :]
    for i in range(seq // BAND):
        lo, hi = window(i, seq)
        seg_k = jnp.broadcast_to(seg_row[:, lo:hi], (BAND, hi - lo))
        seg_q = jnp.transpose(
            jnp.broadcast_to(seg_row[:, i * BAND : (i + 1) * BAND], (BAND, BAND))
        )
        same = jnp.concatenate([seg_q] * ((hi - lo) // BAND), axis=1) == seg_k
        for h in range(width // HEAD):
            cols = slice(h * HEAD, (h + 1) * HEAD)
            scores = nt(q_ref[0, i * BAND : (i + 1) * BAND, cols], k_ref[0, lo:hi, cols])
            scores = jnp.where(same, scores, MASKED)
            expo = jnp.exp(scores - jnp.max(scores, axis=-1, keepdims=True))
            total = jnp.sum(expo, axis=-1, keepdims=True)
            probs = (expo * (1.0 / total)).astype(BF16)
            p_ref[0, h, i * BAND : (i + 1) * BAND, 0 : hi - lo] = probs
            ctx_ref[0, i * BAND : (i + 1) * BAND, cols] = nn(probs, v_ref[0, lo:hi, cols]).astype(
                BF16
            )
    part_ref[0] = nn(ctx_ref[0], wo[...]).astype(BF16)


def attend_fwd(base, idx, x, seg, wq, wk, wv, wo, qb, vb, kept):
    rows, seq = seg.shape
    d, width = wq.shape
    heads = width // HEAD
    slot = lambda g, s: (base - 2 * g, 0, 0)
    saved = (
        jax.ShapeDtypeStruct((rows, seq, width), BF16),
        jax.ShapeDtypeStruct((rows, seq, width), BF16),
        jax.ShapeDtypeStruct((rows, seq, width), BF16),
        jax.ShapeDtypeStruct((rows, heads, seq, 3 * BAND), BF16),
        jax.ShapeDtypeStruct((rows, seq, width), BF16),
    )
    args = (idx, x, seg, wq, wk, wv, wo, qb, vb)
    specs = [
        pl.BlockSpec((seq, d), lambda g, s: (jnp.bitwise_xor(s[0], base - 2 * g), 0)),
        whole(seg.shape),
        whole(wq.shape),
        whole(wk.shape),
        whole(wv.shape),
        whole(wo.shape),
        whole(qb.shape),
        whole(vb.shape),
    ]
    alias = {}
    if kept is not None:
        alias = {len(args) + i: i for i in range(len(kept))}
        args = args + tuple(kept)
        specs = specs + [pl.BlockSpec(memory_space=pl.ANY)] * len(kept)
    return pl.pallas_call(
        partial(attend_fwd_kernel, base),
        out_shape=saved + (jax.ShapeDtypeStruct((2, seq, d), BF16),),
        grid_spec=pltpu.PrefetchScalarGridSpec(
            num_scalar_prefetch=1,
            grid=(2,),
            in_specs=specs,
            out_specs=[
                pl.BlockSpec((1, seq, width), slot),
                pl.BlockSpec((1, seq, width), slot),
                pl.BlockSpec((1, seq, width), slot),
                pl.BlockSpec((1, heads, seq, 3 * BAND), lambda g, s: (base - 2 * g, 0, 0, 0)),
                pl.BlockSpec((1, seq, width), slot),
                pl.BlockSpec((1, seq, d), lambda g, s: (g, 0, 0)),
            ],
        ),
        input_output_aliases=alias,
        compiler_params=params(),
        cost_estimate=cost(2 * (8 * seq * d * width + 4 * seq * 384 * width), 8e6, 2e6),
        name="attend_fwd",
    )(*args)


def gelu_parts(v):
    half = 0.5 * (1.0 + lax.erf(v * ROOT_HALF))
    return v * half, half + v * jnp.exp(-0.5 * v * v) * INV_ROOT_TAU


def by_rows(total, step, body):
    def one(i, carry):
        body(pl.ds(pl.multiple_of(i * step, step), step))
        return carry

    lax.fori_loop(0, total // step, one, 0)


def up_first_kernel(
    idx, x_ref, pa, pb, pc, ob, gain, shift, u0, u1, b0, b1, hid, nrm, inv, low, act, slope
):
    @pl.when(pl.program_id(0) == 0)
    def _():
        def body(rows):
            middle = (
                pa[0, rows, :].astype(F32)
                + pb[0, rows, :].astype(F32)
                + pc[rows, :].astype(F32)
                + ob[...]
                + x_ref[rows, :].astype(F32)
            )
            centred = middle - jnp.mean(middle, axis=-1, keepdims=True)
            r = lax.rsqrt(jnp.mean(centred * centred, axis=-1, keepdims=True) + EPSILON)
            normed = centred * r
            hidden = normed * gain[...] + shift[...]
            nrm[rows, :] = normed
            inv[rows, :] = jnp.broadcast_to(r, (r.shape[0], 128))
            hid[rows, :] = hidden
            low[rows, :] = hidden.astype(BF16)

        by_rows(low.shape[0], 64, body)

    for r, (u, b) in enumerate(((u0, b0), (u1, b1))):
        value, deriv = gelu_parts(nn(low[...], u[...]) + b[...])
        act[r] = value.astype(BF16)
        slope[r] = deriv.astype(BF16)


def up_first(idx, x, own, recv, other, ob, gain, shift, u0, u1, b0, b1):
    seq, d = other.shape
    units = u0.shape[1]
    tile = 256
    row = pl.BlockSpec((seq, d), lambda n, s: (s[0], 0))
    slot1 = pl.BlockSpec((1, seq, d), lambda n, s: (1, 0, 0))
    wide = pl.BlockSpec((d, tile), lambda n, s: (0, n))
    bias = pl.BlockSpec((1, tile), lambda n, s: (0, n))
    out = pl.BlockSpec((2, seq, tile), lambda n, s: (0, 0, n))
    return pl.pallas_call(
        up_first_kernel,
        out_shape=(
            jax.ShapeDtypeStruct((seq, d), F32),
            jax.ShapeDtypeStruct((seq, d), F32),
            jax.ShapeDtypeStruct((seq, 128), F32),
            jax.ShapeDtypeStruct((seq, d), BF16),
            jax.ShapeDtypeStruct((2, seq, units), BF16),
            jax.ShapeDtypeStruct((2, seq, units), BF16),
        ),
        grid_spec=pltpu.PrefetchScalarGridSpec(
            num_scalar_prefetch=1,
            grid=(units // tile,),
            in_specs=[row, slot1, slot1, whole((seq, d)), whole((1, d)), whole((1, d)), whole((1, d))]
            + [wide, wide, bias, bias],
            out_specs=[whole((seq, d)), whole((seq, d)), whole((seq, 128)), whole((seq, d)), out, out],
        ),
        compiler_params=params(),
        cost_estimate=cost(4 * seq * d * units, 14e6, 4 * seq * units),
        name="up_first",
    )(idx, x, own, recv, other, ob, gain, shift, u0, u1, b0, b1)


def up_second_kernel(low, u0, u1, b0, b1, act, slope):
    for r, (u, b) in enumerate(((u0, b0), (u1, b1))):
        value, deriv = gelu_parts(nn(low[...], u[...]) + b[...])
        act[r] = value.astype(BF16)
        slope[r] = deriv.astype(BF16)


def up_second(low, u0, u1, b0, b1):
    seq, d = low.shape
    units = u0.shape[1]
    tile = 256
    wide = pl.BlockSpec((d, tile), lambda n: (0, n))
    bias = pl.BlockSpec((1, tile), lambda n: (0, n))
    out = pl.BlockSpec((2, seq, tile), lambda n: (0, 0, n))
    return pl.pallas_call(
        up_second_kernel,
        out_shape=(
            jax.ShapeDtypeStruct((2, seq, units), BF16),
            jax.ShapeDtypeStruct((2, seq, units), BF16),
        ),
        grid=(units // tile,),
        in_specs=[whole((seq, d)), wide, wide, bias, bias],
        out_specs=[out, out],
        compiler_params=params(),
        cost_estimate=cost(4 * seq * d * units, 7e6, 4 * seq * units),
        name="up_second",
    )(low, u0, u1, b0, b1)


def down_kernel(
    idx, act01, act23, d0, d1, d2, d3, hid, cot, db, gain, shift, out_ref, gf_ref, gl_ref, vec, acc
):
    d = hid.shape[1]
    step = pl.program_id(0)
    acts = (act01[0], act01[1], act23[0], act23[1])
    total = None
    for a, w in zip(acts, (d0, d1, d2, d3)):
        term = nn(a, w[...])
        total = term if total is None else total + term
    acc[step] = total

    @pl.when(step == pl.num_programs(0) - 1)
    def _():
        vec[...] = jnp.zeros_like(vec)

        def body(rows):
            parts = [acc[n, rows, :] for n in range(acc.shape[0])]
            final = jnp.concatenate(parts, axis=1) + db[...] + hid[rows, :]
            centred = final - jnp.mean(final, axis=-1, keepdims=True)
            r = lax.rsqrt(jnp.mean(centred * centred, axis=-1, keepdims=True) + EPSILON)
            normed = centred * r
            out_ref[rows, :] = (normed * gain[...] + shift[...]).astype(BF16)
            cv = cot[rows, :].astype(F32)
            c = cv * gain[...]
            cn = cv * normed
            grad = r * (
                c
                - jnp.mean(c, axis=-1, keepdims=True)
                - normed * jnp.mean(c * normed, axis=-1, keepdims=True)
            )
            gf_ref[rows, :] = grad
            gl_ref[rows, :] = grad.astype(BF16)
            vec[0:1, :] += jnp.sum(cn, axis=0, keepdims=True)
            vec[1:2, :] += jnp.sum(cv, axis=0, keepdims=True)
            vec[2:3, :] += jnp.sum(grad, axis=0, keepdims=True)

        by_rows(hid.shape[0], 64, body)


def down(idx, act01, act23, ds, hid, cot, db, gain, shift):
    seq, d = hid.shape
    units = act01.shape[2]
    tile = 256
    acts = whole((2, seq, units))
    wide = pl.BlockSpec((units, tile), lambda n, s: (0, n))
    vecs = whole((1, d))
    return pl.pallas_call(
        down_kernel,
        out_shape=(
            jax.ShapeDtypeStruct((seq, d), BF16),
            jax.ShapeDtypeStruct((seq, d), F32),
            jax.ShapeDtypeStruct((seq, d), BF16),
            jax.ShapeDtypeStruct((8, d), F32),
        ),
        grid_spec=pltpu.PrefetchScalarGridSpec(
            num_scalar_prefetch=1,
            grid=(d // tile,),
            in_specs=[acts, acts, wide, wide, wide, wide, whole((seq, d))]
            + [pl.BlockSpec((seq, d), lambda n, s: (s[0], 0)), vecs, vecs, vecs],
            out_specs=[whole((seq, d)), whole((seq, d)), whole((seq, d)), whole((8, d))],
            scratch_shapes=[pltpu.VMEM((d // tile, seq, tile), F32)],
        ),
        compiler_params=params(),
        cost_estimate=cost(8 * seq * d * units, 14e6),
        name="down",
    )(idx, act01, act23, *ds, hid, cot, db, gain, shift)


def back_kernel(
    gl, sl01, sl23, d0, d1, d2, d3, u0, u1, u2, u3, gf, nrm, inv, gain, vecf,
    gp01, gp23, gm_ref, gml_ref, vec, acc
):
    step = pl.program_id(0)

    @pl.when(step == 0)
    def _():
        vec[...] = jnp.zeros_like(vec)
        vec[7:10, :] = vecf[0:3, :]

    tile = sl01.shape[2]
    total = None
    for r, (w_d, w_u) in enumerate(((d0, u0), (d1, u1), (d2, u2), (d3, u3))):
        slope = sl01[r] if r < 2 else sl23[r - 2]
        pre = (nt(gl[...], w_d[...]) * slope.astype(F32)).astype(BF16)
        if r < 2:
            gp01[r] = pre
        else:
            gp23[r - 2] = pre
        sums = jnp.sum(pre.astype(F32), axis=0, keepdims=True)
        vec[r : r + 1, pl.ds(pl.multiple_of(step * tile, tile), tile)] = sums
        term = nt(pre, w_u[...])
        total = term if total is None else total + term

    @pl.when(step == 0)
    def _():
        acc[...] = total

    @pl.when(step > 0)
    def _():
        acc[...] += total

    @pl.when(step == pl.num_programs(0) - 1)
    def _():
        def body(rows):
            grad = acc[rows, :] + gf[rows, :]
            normed = nrm[rows, :]
            r = inv[rows, 0:1]
            c = grad * gain[...]
            gm = r * (
                c
                - jnp.mean(c, axis=-1, keepdims=True)
                - normed * jnp.mean(c * normed, axis=-1, keepdims=True)
            )
            gm_ref[rows, :] = gm
            gml_ref[rows, :] = gm.astype(BF16)
            vec[4:5, :] += jnp.sum(grad * normed, axis=0, keepdims=True)
            vec[5:6, :] += jnp.sum(grad, axis=0, keepdims=True)
            vec[6:7, :] += jnp.sum(gm, axis=0, keepdims=True)

        by_rows(gf.shape[0], 64, body)


def back(gl, sl01, sl23, ds, us, gf, nrm, inv, gain, vecf):
    seq, d = gf.shape
    units = sl01.shape[2]
    tile = 256
    slope = pl.BlockSpec((2, seq, tile), lambda n: (0, 0, n))
    w_d = pl.BlockSpec((tile, d), lambda n: (n, 0))
    w_u = pl.BlockSpec((d, tile), lambda n: (0, n))
    return pl.pallas_call(
        back_kernel,
        out_shape=(
            jax.ShapeDtypeStruct((2, seq, units), BF16),
            jax.ShapeDtypeStruct((2, seq, units), BF16),
            jax.ShapeDtypeStruct((seq, d), F32),
            jax.ShapeDtypeStruct((seq, d), BF16),
            jax.ShapeDtypeStruct((16, d), F32),
        ),
        grid=(units // tile,),
        in_specs=[whole((seq, d)), slope, slope]
        + [w_d] * 4
        + [w_u] * 4
        + [whole((seq, d)), whole((seq, d)), whole((seq, 128)), whole((1, d)), whole((8, d))],
        out_specs=[slope, slope, whole((seq, d)), whole((seq, d)), whole((16, d))],
        scratch_shapes=[pltpu.VMEM((seq, d), F32)],
        compiler_params=params(),
        cost_estimate=cost(16 * seq * d * units, 22e6),
        name="back",
    )(gl, sl01, sl23, *ds, *us, gf, nrm, inv, gain, vecf)


def place(idx, e):
    return jnp.bitwise_xor(e // 4, idx[1]) * 4 + jnp.bitwise_xor(e % 4, idx[2])


def outer_kernel(which, idx, left, lo_pair, hi_pair, *rest):
    flip, picks = which
    add, out = (rest[0], rest[1]) if len(rest) == 2 else (None, rest[0])
    eighth = out.shape[1] // 8
    for j, (pair, at) in enumerate(picks):
        varied = (lo_pair, hi_pair)[pair][at]
        value = tn(varied, left[...]) if flip else tn(left[...], varied)
        for e in range(8):
            dst = pl.ds(pl.multiple_of(place(idx, e) * eighth, 16), eighth)
            piece = value[e * eighth : (e + 1) * eighth]
            if add is not None:
                piece = piece + add[j, dst, :].astype(F32)
            out[j, dst, :] = piece.astype(BF16)


def outer(which, idx, left, lo_pair, hi_pair, add=None):
    seq, d = left.shape
    units = lo_pair.shape[2]
    specs = [whole((seq, d)), whole((2, seq, units)), whole((2, seq, units))]
    args = (idx, left, lo_pair, hi_pair)
    if add is not None:
        specs.append(whole(add.shape))
        args = args + (add,)
    return pl.pallas_call(
        partial(outer_kernel, which),
        out_shape=jax.ShapeDtypeStruct((2, units, d) if which[0] else (2, d, units), BF16),
        grid_spec=pltpu.PrefetchScalarGridSpec(
            num_scalar_prefetch=1,
            grid=(1,),
            in_specs=specs,
            out_specs=whole((2, units, d) if which[0] else (2, d, units)),
        ),
        compiler_params=params(),
        cost_estimate=cost(4 * seq * d * units, 7e6),
        name="outer",
    )(*args)


PICK_31 = ((1, 1), (0, 1))
PICK_20 = ((1, 0), (0, 0))


def attend_bwd_kernel(last, idx, x_ref, ga, gb, q_ref, k_ref, v_ref, p_ref, ctx_ref, wq, wk, wv, wo, *rest):
    if last:
        before, vec_before, part_ref, out_ref, vec, grads, gq, gk, gv = rest
    else:
        part_ref, grads, vec, gq, gk, gv = rest
    step = pl.program_id(0)
    seq, width = q_ref.shape[1:]
    heads = width // HEAD
    blocks = seq // BAND

    @pl.when(step == 0)
    def _():
        if last:
            grads[...] = before[...]
            vec[...] = vec_before[...]
        else:
            grads[...] = jnp.zeros_like(grads)
            vec[...] = jnp.zeros_like(vec)

    gml = jnp.where(step == 0, ga[...], gb[...])
    ctx = ctx_ref[0]
    gctx = nt(gml, wo[...]).astype(BF16)
    for h in range(heads):
        cols = slice(h * HEAD, (h + 1) * HEAD)
        gk_sum = [None] * blocks
        gv_sum = [None] * blocks
        for i in range(blocks):
            lo, hi = window(i, seq)
            rows = slice(i * BAND, (i + 1) * BAND)
            low_probs = p_ref[0, h, rows, 0 : hi - lo]
            probs = low_probs.astype(F32)
            gctx_i = gctx[rows, cols]
            gprobs = nt(gctx_i, v_ref[0, lo:hi, cols])
            dot = jnp.sum(gprobs * probs, axis=-1, keepdims=True)
            gscore = (probs * (gprobs - dot)).astype(BF16)
            gq[rows, cols] = (nn(gscore, k_ref[0, lo:hi, cols]) * (HEAD**-0.5)).astype(BF16)
            gk_i = tn(gscore, q_ref[0, rows, cols])
            gv_i = tn(low_probs, gctx_i)
            for j in range(lo // BAND, hi // BAND):
                at = slice(j * BAND - lo, (j + 1) * BAND - lo)
                gk_sum[j] = gk_i[at] if gk_sum[j] is None else gk_sum[j] + gk_i[at]
                gv_sum[j] = gv_i[at] if gv_sum[j] is None else gv_sum[j] + gv_i[at]
        for j in range(blocks):
            rows = slice(j * BAND, (j + 1) * BAND)
            gk[rows, cols] = gk_sum[j].astype(BF16)
            gv[rows, cols] = gv_sum[j].astype(BF16)
    x = x_ref[...]
    grads[0:width] += tn(gq[...], x)
    grads[width : 2 * width] += tn(gk[...], x)
    grads[2 * width : 3 * width] += tn(gv[...], x)
    grads[3 * width : 4 * width] += tn(ctx, gml)
    vec[0:1, 0:width] += jnp.sum(gq[...].astype(F32), axis=0, keepdims=True)
    vec[1:2, 0:width] += jnp.sum(gv[...].astype(F32), axis=0, keepdims=True)
    part_ref[0] = (nt(gq[...], wq[...]) + nt(gk[...], wk[...]) + nt(gv[...], wv[...])).astype(BF16)

    if last:
        @pl.when(step == 1)
        def _():
            eighth = out_ref.shape[0] // 8
            for e in range(8):
                dst = pl.ds(pl.multiple_of(place(idx, e) * eighth, 16), eighth)
                out_ref[dst, :] = grads[e * eighth : (e + 1) * eighth].astype(BF16)


def attend_bwd(first, idx, x, ga, gb, kept, wq, wk, wv, wo, before=None):
    q, k, v, p, ctx = kept
    rows, seq, width = q.shape
    d = x.shape[1]
    heads = width // HEAD
    last = before is not None
    slot = pl.BlockSpec((1, seq, width), lambda g, s: (first + g, 0, 0))
    specs = [
        pl.BlockSpec((seq, d), lambda g, s: (jnp.bitwise_xor(s[0], first + g), 0)),
        whole((seq, d)),
        whole((seq, d)),
        slot,
        slot,
        slot,
        pl.BlockSpec((1, heads, seq, 3 * BAND), lambda g, s: (first + g, 0, 0, 0)),
        slot,
        whole(wq.shape),
        whole(wk.shape),
        whole(wv.shape),
        whole(wo.shape),
    ]
    args = (idx, x, ga, gb, q, k, v, p, ctx, wq, wk, wv, wo)
    part = jax.ShapeDtypeStruct((2, seq, d), BF16)
    part_spec = pl.BlockSpec((1, seq, d), lambda g, s: (g, 0, 0))
    scratch = [pltpu.VMEM((seq, width), BF16)] * 3
    if last:
        specs += [whole((4 * width, d)), whole((8, d))]
        args += tuple(before)
        shapes = (part, jax.ShapeDtypeStruct((4 * width, d), BF16), jax.ShapeDtypeStruct((8, d), F32))
        outs = [part_spec, whole((4 * width, d)), whole((8, d))]
        scratch = [pltpu.VMEM((4 * width, d), F32)] + scratch
    else:
        shapes = (part, jax.ShapeDtypeStruct((4 * width, d), F32), jax.ShapeDtypeStruct((8, d), F32))
        outs = [part_spec, whole((4 * width, d)), whole((8, d))]
    return pl.pallas_call(
        partial(attend_bwd_kernel, last),
        out_shape=shapes,
        grid_spec=pltpu.PrefetchScalarGridSpec(
            num_scalar_prefetch=1, grid=(2,), in_specs=specs, out_specs=outs, scratch_shapes=scratch
        ),
        compiler_params=params(),
        cost_estimate=cost(2 * (16 * seq * d * width + 8 * seq * 384 * width), 12e6),
        name="attend_bwd",
    )(*args)


def join_kernel(idx, p0, p1, p2, p3, out, sem):
    rows = p0.shape[0]
    copies = []
    for j, piece in enumerate((p0, p1, p2, p3)):
        quarter = jnp.bitwise_xor(idx[1], j // 2) * 2 + jnp.bitwise_xor(
            jnp.bitwise_and(idx[2], 1), j % 2
        )
        dst = out.at[pl.ds(pl.multiple_of(quarter * rows, 16), rows)]
        copies.append(pltpu.make_async_copy(piece, dst, sem.at[j]))
    for c in copies:
        c.start()
    for c in copies:
        c.wait()


def join(idx, pieces):
    rows, d = pieces[0].shape
    anywhere = pl.BlockSpec(memory_space=pl.ANY)
    return pl.pallas_call(
        join_kernel,
        out_shape=jax.ShapeDtypeStruct((4 * rows, d), pieces[0].dtype),
        grid_spec=pltpu.PrefetchScalarGridSpec(
            num_scalar_prefetch=1,
            grid=(1,),
            in_specs=[anywhere] * 4,
            out_specs=anywhere,
            scratch_shapes=[pltpu.SemaphoreType.DMA((4,))],
        ),
        name="join",
    )(idx, *pieces)


def unpack_kernel(slots, attn, idx, *refs):
    n = len(slots)
    outs = refs[n:]
    eighth = refs[0].shape[0] // len(slots[0])
    if attn:
        full = outs[-1]
    else:
        full = outs[0]
    for piece, where in zip(refs[:n], slots):
        for j, pos in enumerate(where):
            dst = pl.ds(pl.multiple_of(place(idx, pos) * eighth, 16), eighth)
            full[dst, :] = piece[j * eighth : (j + 1) * eighth].astype(F32)
    if attn:
        width = full.shape[0] // 4
        for j in range(3):
            outs[j][...] = jnp.transpose(full[j * width : (j + 1) * width])
        outs[3][...] = full[3 * width : 4 * width]


def unpack(idx, pieces, slots, attn):
    d = pieces[0].shape[1]
    total = pieces[0].shape[0] // len(slots[0]) * 8
    if attn:
        width = total // 4
        shapes = [(d, width)] * 3 + [(width, d)]
        scratch = [pltpu.VMEM((total, d), F32)]
    else:
        shapes = [(total, d)]
        scratch = []
    return pl.pallas_call(
        partial(unpack_kernel, slots, attn),
        out_shape=[jax.ShapeDtypeStruct(s, F32) for s in shapes],
        grid_spec=pltpu.PrefetchScalarGridSpec(
            num_scalar_prefetch=1,
            grid=(1,),
            in_specs=[whole(p.shape) for p in pieces],
            out_specs=[whole(s) for s in shapes],
            scratch_shapes=scratch,
        ),
        compiler_params=params(),
        name="unpack",
    )(idx, *pieces)


def finish_kernel(idx, a, b, c, gm, out):
    total = a[0].astype(F32) + b[...].astype(F32) + c[...].astype(F32) + gm[...]
    out[...] = total.astype(BF16)


def over(name, bit):
    size = lax.axis_size(name)
    pairs = [(i, i ^ bit) for i in range(size)]
    return lambda a: lax.ppermute(a, name, pairs)


def local(
    inputs, segment_ids, cotangent, query_weight, key_weight, value_weight, query_bias, value_bias,
    output_weight, output_bias, middle_gain, middle_shift, up_weight, up_bias, down_weight, down_bias,
    final_gain, final_shift,
):
    rows_here, seq = segment_ids.shape
    members = lax.axis_size("mp")
    assert members == 4 and rows_here == 4
    d = inputs.shape[1]
    staged = lax.axis_size("dp") == 8
    me = lax.axis_index("mp")
    spot = lax.axis_index("dp")
    x_bit = spot % 2 if staged else 0 * spot
    z_at = spot // 2 if staged else 0 * spot
    idx = jnp.stack([me, x_bit, z_at]).astype(jnp.int32)
    core, y, both = over("mp", 1), over("mp", 2), over("mp", 3)
    x_swap = over("dp", 1)
    z_swap = {k: over("dp", 2 * k) for k in (1, 2, 3)}
    line = lambda v: v.reshape(1, -1)

    def gather(w, z_first):
        one = core(w)
        if not staged:
            return one, y(w), both(w)
        quarter = w.shape[0] // 4
        mine = lax.dynamic_slice_in_dim(w, (x_bit * 2 + z_at % 2) * quarter, quarter, 0)
        near = y(mine)
        by_x = x_swap(near)
        by_z = z_swap[1](near)
        far = x_swap(by_z) if z_first else z_swap[1](by_x)
        two = join(idx, (near, by_z, by_x, far))
        return one, two, core(two)

    ub = line(up_bias)
    ub1, ub2 = core(ub), y(ub)
    ub3 = core(ub2)
    u1, u2, u3 = gather(up_weight, False)
    d1, d2, d3 = gather(down_weight, True)

    weights = (query_weight, key_weight, value_weight, output_weight)
    fwd = (idx, inputs, segment_ids) + weights + (line(query_bias), line(value_bias))
    *kept, part31 = attend_fwd(3, *fwd, None)
    recv = core(part31)
    *kept, part20 = attend_fwd(2, *fwd, kept)
    other = y(part20[0] + recv[0])
    hidden, normed, inverse, low, act01, slope01 = up_first(
        idx, inputs, part20, recv, other, line(output_bias), line(middle_gain), line(middle_shift),
        up_weight, u1, ub, ub1,
    )
    act23, slope23 = up_second(low, u2, u3, ub2, ub3)
    ds = (down_weight, d1, d2, d3)
    us = (up_weight, u1, u2, u3)
    layer_out, grad_final, grad_low, vec_fin = down(
        idx, act01, act23, ds, hidden, cotangent, line(down_bias), line(final_gain), line(final_shift)
    )

    gd31 = outer((True, PICK_31), idx, grad_low, act01, act23)
    rd = core(gd31)
    gp01, gp23, grad_mid, mid_low, vec = back(
        grad_low, slope01, slope23, ds, us, grad_final, normed, inverse, line(middle_gain), vec_fin
    )
    mid1 = core(mid_low)
    mid2 = y(mid_low)
    sd = outer((True, PICK_20), idx, grad_low, act01, act23, rd)
    gu31 = outer((False, PICK_31), idx, low, gp01, gp23)
    ru = core(gu31)
    part01, *before = attend_bwd(0, idx, inputs, mid_low, mid1, kept, *weights)
    su = outer((False, PICK_20), idx, low, gp01, gp23, ru)
    mid3 = core(mid2)
    part23, ta, vec_att = attend_bwd(2, idx, inputs, mid2, mid3, kept, *weights, before)

    in1, in3 = core(part01[1]), core(part23[1])
    in2 = y(part23[0] + in3)
    input_grad = pl.pallas_call(
        finish_kernel,
        out_shape=jax.ShapeDtypeStruct((seq, d), BF16),
        grid_spec=pltpu.PrefetchScalarGridSpec(
            num_scalar_prefetch=1,
            grid=(1,),
            in_specs=[whole((1, seq, d))] + [whole((seq, d))] * 3,
            out_specs=whole((seq, d)),
        ),
        compiler_params=params(),
        name="finish",
    )(idx, part01, in1, in2, grad_mid)

    def over_dp(t):
        if not staged:
            return (lax.psum(t, "dp"),), (tuple(range(8)),)
        half = t.shape[0] // 2
        a = t[:half] + x_swap(t[half:])
        quarter = half // 4
        s = a[:quarter]
        for k in (1, 2, 3):
            s = s + z_swap[k](a[k * quarter : (k + 1) * quarter])
        rest = [z_swap[k](s) for k in (1, 2, 3)]
        far = x_swap(jnp.concatenate([s] + rest, axis=0))
        return (s, *rest, far), ((0,), (1,), (2,), (3,), (4, 5, 6, 7))

    td = sd[1] + y(sd[0])
    (grad_down,) = unpack(idx, *over_dp(td), False)
    tu = su[1] + y(su[0])
    (grad_up,) = unpack(idx, *over_dp(tu), False)
    grad_q, grad_k, grad_v, grad_o = unpack(idx, *over_dp(ta), True)

    def mixed(v, r, order):
        return v + jnp.concatenate([r[j : j + 1] for j in order] + [r[4:]], axis=0)

    vec = mixed(vec, core(vec), (1, 0, 3, 2))
    vec = mixed(vec, y(vec), (2, 3, 0, 1))
    vec = jnp.concatenate([vec[0:1], vec[4:10], vec_att[0:2]], axis=0)
    vec = jnp.pad(vec, ((0, 7), (0, 0)))
    if staged:
        for swap in (x_swap, z_swap[1], z_swap[2]):
            vec = vec + swap(vec)
    else:
        vec = lax.psum(vec, "dp")
    width = query_bias.shape[0]
    return (
        layer_out, input_grad, grad_q, grad_k, grad_v, vec[7, :width], vec[8, :width], grad_o,
        vec[3], vec[1], vec[2], grad_up, vec[0], grad_down, vec[6], vec[4], vec[5],
    )


def solution(mesh):
    tokens = P("dp", None)
    columns, units, stacked, full = P(None, "mp"), P("mp"), P("mp", None), P()
    shared = P(("dp", "mp"), None)
    placed = (
        tokens, tokens, tokens, columns, columns, columns, units, units, stacked, full, full, full,
        columns, units, stacked, full, full, full,
    )
    given = (
        shared, shared, columns, columns, columns, units, units, stacked, full, full, full,
        columns, units, stacked, full, full, full,
    )
    return jax.shard_map(local, mesh=mesh, in_specs=placed, out_specs=given, check_vma=False)
```

```python
from functools import partial

import jax
import jax.numpy as jnp
from jax import lax
from jax.experimental import pallas as pl
from jax.experimental.pallas import tpu as pltpu
from jax.sharding import PartitionSpec as P

HEAD = 64
BAND = 128
EPSILON = 1e-12
ROOT_HALF = 0.7071067811865476
INV_ROOT_TAU = 0.3989422804014327
MASKED = -1e30
F32 = jnp.float32
BF16 = jnp.bfloat16
MIB = 1024 * 1024
SCALE = 4.0


def nn(a, b):
    return lax.dot_general(a, b, (((1,), (0,)), ((), ())), preferred_element_type=F32)


def nt(a, b):
    return lax.dot_general(a, b, (((1,), (1,)), ((), ())), preferred_element_type=F32)


def tn(a, b):
    return lax.dot_general(a, b, (((0,), (0,)), ((), ())), preferred_element_type=F32)


def window(block, seq):
    lo = max(block * BAND - BAND, 0)
    hi = min(block * BAND + 2 * BAND, seq)
    return lo, hi


def params(mib):
    return pltpu.CompilerParams(vmem_limit_bytes=mib * MIB)


def cost(us):
    return pl.CostEstimate(
        flops=int(us * SCALE * 1.15e9), bytes_accessed=int(us * SCALE * 3.6e6), transcendentals=0
    )


def whole(*shape):
    return pl.BlockSpec(shape, lambda *_: (0,) * len(shape), pipeline_mode=pl.Buffered(1))


def held(*shape):
    return pl.BlockSpec(shape, lambda *_: (0,) * len(shape))


def rows_of_heads(a):
    zero = jnp.zeros((HEAD, a.shape[1]), a.dtype)
    tiles = []
    for h in range(a.shape[0] // HEAD):
        mine = a[h * HEAD : (h + 1) * HEAD]
        if h % 2 == 0 and (h + 1) * HEAD == a.shape[0]:
            tiles.append(mine)
        else:
            tiles.append(jnp.concatenate([mine, zero] if h % 2 == 0 else [zero, mine], axis=0))
    return tiles


def tiles_of_heads(a):
    width = a.shape[1]
    return [a[:, h // 2 * 128 : min(h // 2 * 128 + 128, width)] for h in range(width // HEAD)]


def columns_of_heads(a):
    masked = []
    for h, tile in enumerate(tiles_of_heads(a)):
        if tile.shape[1] == HEAD:
            masked.append(tile)
        else:
            lane = lax.broadcasted_iota(jnp.int32, tile.shape, 1)
            masked.append(jnp.where((lane < HEAD) == (h % 2 == 0), tile, jnp.zeros_like(tile)))
    return masked


def store_tiles(ref, rows, per_head, scale=None):
    for at in range(0, len(per_head), 2):
        total = per_head[at] if at + 1 == len(per_head) else per_head[at] + per_head[at + 1]
        if scale is not None:
            total = total * scale
        lo = at * HEAD
        ref[rows, lo : lo + total.shape[1]] = total.astype(ref.dtype)


def attend_fwd_kernel(base, idx, x_ref, seg_ref, wq, wk, wv, wo, qb, vb,
                      q_ref, k_ref, v_ref, p_ref, ctx_ref, *parts):
    step = pl.program_id(0)
    seq = x_ref.shape[0]
    row = jnp.bitwise_xor(idx[0], base - step)
    x = x_ref[...]
    q = ((nt(x, wq[...]) + qb[...]).astype(BF16) * (HEAD**-0.5)).astype(BF16)
    k_t = nt(wk[...], x).astype(BF16)
    v = (nt(x, wv[...]) + vb[...]).astype(BF16)
    q_ref[0] = jnp.transpose(q)
    k_ref[0] = jnp.transpose(k_t)
    v_ref[0] = jnp.transpose(v)
    q_tiles, k_rows, v_cols = tiles_of_heads(q), rows_of_heads(k_t), columns_of_heads(v)
    heads = range(len(q_tiles))
    seg_row = seg_ref[pl.ds(row, 1), :]
    for i in range(seq // BAND):
        lo, hi = window(i, seq)
        rows = slice(i * BAND, (i + 1) * BAND)
        seg_k = jnp.broadcast_to(seg_row[:, lo:hi], (BAND, hi - lo))
        seg_q = jnp.transpose(jnp.broadcast_to(seg_row[:, rows], (BAND, BAND)))
        same = jnp.concatenate([seg_q] * ((hi - lo) // BAND), axis=1) == seg_k
        scores = [jnp.where(same, nn(q_tiles[h][rows], k_rows[h][:, lo:hi]), MASKED) for h in heads]
        tops = [jnp.max(a, axis=-1, keepdims=True) for a in scores]
        expos = [jnp.exp(a - m) for a, m in zip(scores, tops)]
        scales = [1.0 / jnp.sum(e, axis=-1, keepdims=True) for e in expos]
        probs = [(e * t).astype(BF16) for e, t in zip(expos, scales)]
        for h in heads:
            p_ref[0, h, rows, 0 : hi - lo] = probs[h]
        store_tiles(ctx_ref.at[0], rows, [nn(probs[h], v_cols[h][lo:hi]) for h in heads])
    part = nn(ctx_ref[0], wo[...]).astype(BF16)
    for j, ref in enumerate(parts):

        @pl.when(step == j)
        def _():
            ref[...] = part


def attend_fwd(base, count, idx, x, seg, wq, wk, wv, wo, qb, vb):
    seq = seg.shape[1]
    width, d = wq.shape
    heads = width // HEAD
    slot = lambda g, s: (g, 0, 0)
    natural = pl.BlockSpec((1, seq, width), slot)
    turned = pl.BlockSpec((1, width, seq), slot)
    saved = (
        jax.ShapeDtypeStruct((count, width, seq), BF16),
        jax.ShapeDtypeStruct((count, seq, width), BF16),
        jax.ShapeDtypeStruct((count, width, seq), BF16),
        jax.ShapeDtypeStruct((count, heads, seq, 3 * BAND), BF16),
        jax.ShapeDtypeStruct((count, seq, width), BF16),
    )
    args = (idx, x, seg, wq, wk, wv, wo, qb, vb)
    specs = [
        pl.BlockSpec((seq, d), lambda g, s: (jnp.bitwise_xor(s[0], base - g), 0)),
        whole(*seg.shape),
        whole(width, d),
        whole(width, d),
        whole(width, d),
        whole(width, d),
        whole(1, width),
        whole(1, width),
    ]
    return pl.pallas_call(
        partial(attend_fwd_kernel, base),
        out_shape=saved + (jax.ShapeDtypeStruct((seq, d), BF16),) * count,
        grid_spec=pltpu.PrefetchScalarGridSpec(
            num_scalar_prefetch=1,
            grid=(count,),
            in_specs=specs,
            out_specs=[
                turned,
                natural,
                turned,
                pl.BlockSpec((1, heads, seq, 3 * BAND), lambda g, s: (g, 0, 0, 0)),
                natural,
            ]
            + [held(seq, d)] * count,
        ),
        compiler_params=params(60),
        cost_estimate=cost(3.2 * count),
        name="attend_fwd",
    )(*args)


def gelu_parts(v):
    half = 0.5 * (1.0 + lax.erf(v * ROOT_HALF))
    return v * half, half + v * jnp.exp(-0.5 * v * v) * INV_ROOT_TAU


def by_rows(total, step, body, carry):
    def one(i, c):
        return body(pl.ds(pl.multiple_of(i * step, step), step), c)

    return lax.fori_loop(0, total // step, one, carry, unroll=True)


def fold(a):
    return jnp.sum(a.reshape(a.shape[0] // 8, 8, a.shape[1]), axis=0)


def up_kernel(
    idx, x_ref, pa, pb, pc, ob, gain, shift, u0, u1, u2, u3, b0, b1, b2, b3,
    hid, nrm, inv, low, act, slope,
):
    @pl.when(pl.program_id(0) == 0)
    def _():
        def body(rows, carry):
            middle = (
                pa[rows, :].astype(F32)
                + pb[rows, :].astype(F32)
                + pc[rows, :].astype(F32)
                + ob[...]
                + x_ref[rows, :].astype(F32)
            )
            centred = middle - jnp.mean(middle, axis=-1, keepdims=True)
            r = lax.rsqrt(jnp.mean(centred * centred, axis=-1, keepdims=True) + EPSILON)
            normed = centred * r
            hidden = normed * gain[...] + shift[...]
            nrm[rows, :] = normed
            inv[rows, :] = jnp.broadcast_to(r, (r.shape[0], 128))
            hid[rows, :] = hidden
            low[rows, :] = hidden.astype(BF16)
            return carry

        by_rows(low.shape[0], 64, body, 0)

    for r, (u, b) in enumerate(((u0, b0), (u1, b1), (u2, b2), (u3, b3))):
        value, deriv = gelu_parts(nn(low[...], u[...]) + b[...])
        act[r] = value.astype(BF16)
        slope[r] = deriv.astype(BF16)


def up(idx, x, own, recv, other, ob, gain, shift, us, bs):
    seq, d = other.shape
    units = us[0].shape[1]
    tile = 256
    row = pl.BlockSpec((seq, d), lambda n, s: (s[0], 0), pipeline_mode=pl.Buffered(1))
    wide = pl.BlockSpec((d, tile), lambda n, s: (0, n))
    bias = pl.BlockSpec((1, tile), lambda n, s: (0, n))
    out = pl.BlockSpec((4, seq, tile), lambda n, s: (0, 0, n))
    return pl.pallas_call(
        up_kernel,
        out_shape=(
            jax.ShapeDtypeStruct((seq, d), F32),
            jax.ShapeDtypeStruct((seq, d), F32),
            jax.ShapeDtypeStruct((seq, 128), F32),
            jax.ShapeDtypeStruct((seq, d), BF16),
            jax.ShapeDtypeStruct((4, seq, units), BF16),
            jax.ShapeDtypeStruct((4, seq, units), BF16),
        ),
        grid_spec=pltpu.PrefetchScalarGridSpec(
            num_scalar_prefetch=1,
            grid=(units // tile,),
            in_specs=[row] + [whole(seq, d)] * 3 + [whole(1, d)] * 3 + [wide] * 4 + [bias] * 4,
            out_specs=[held(seq, d), held(seq, d), held(seq, 128), held(seq, d), out, out],
        ),
        compiler_params=params(28),
        cost_estimate=cost(7.3),
        name="up",
    )(idx, x, own, recv, other, ob, gain, shift, *us, *bs)


def down_kernel(idx, act, d0, d1, d2, d3, hid, cot, db, gain, shift, out_ref, gf_ref, gl_ref, vec, acc):
    step = pl.program_id(0)
    total = None
    for r, w in enumerate((d0, d1, d2, d3)):
        term = nn(act[r], w[...])
        total = term if total is None else total + term
    acc[step] = total

    @pl.when(step == pl.num_programs(0) - 1)
    def _():
        def body(rows, carry):
            parts = [acc[n, rows, :] for n in range(acc.shape[0])]
            final = jnp.concatenate(parts, axis=1) + db[...] + hid[rows, :]
            centred = final - jnp.mean(final, axis=-1, keepdims=True)
            r = lax.rsqrt(jnp.mean(centred * centred, axis=-1, keepdims=True) + EPSILON)
            normed = centred * r
            out_ref[rows, :] = (normed * gain[...] + shift[...]).astype(BF16)
            cv = cot[rows, :].astype(F32)
            c = cv * gain[...]
            grad = r * (
                c
                - jnp.mean(c, axis=-1, keepdims=True)
                - normed * jnp.mean(c * normed, axis=-1, keepdims=True)
            )
            gf_ref[rows, :] = grad
            gl_ref[rows, :] = grad.astype(BF16)
            return tuple(a + b for a, b in zip(carry, (fold(cv * normed), fold(cv), fold(grad))))

        zero = jnp.zeros((8, hid.shape[1]), F32)
        sums = by_rows(hid.shape[0], 64, body, (zero, zero, zero))
        vec[...] = jnp.zeros_like(vec)
        for j, total in enumerate(sums):
            vec[j : j + 1, :] = jnp.sum(total, axis=0, keepdims=True)


def down(idx, act, ds, hid, cot, db, gain, shift):
    seq, d = hid.shape
    units = act.shape[2]
    tile = 256
    wide = pl.BlockSpec((units, tile), lambda n, s: (0, n))
    row = pl.BlockSpec((seq, d), lambda n, s: (s[0], 0), pipeline_mode=pl.Buffered(1))
    return pl.pallas_call(
        down_kernel,
        out_shape=(
            jax.ShapeDtypeStruct((seq, d), BF16),
            jax.ShapeDtypeStruct((seq, d), F32),
            jax.ShapeDtypeStruct((seq, d), BF16),
            jax.ShapeDtypeStruct((8, d), F32),
        ),
        grid_spec=pltpu.PrefetchScalarGridSpec(
            num_scalar_prefetch=1,
            grid=(d // tile,),
            in_specs=[whole(4, seq, units)] + [wide] * 4 + [whole(seq, d), row] + [whole(1, d)] * 3,
            out_specs=[held(seq, d), held(seq, d), held(seq, d), held(8, d)],
            scratch_shapes=[pltpu.VMEM((d // tile, seq, tile), F32)],
        ),
        compiler_params=params(24),
        cost_estimate=cost(6.2),
        name="down",
    )(idx, act, *ds, hid, cot, db, gain, shift)


def back_kernel(
    gl, slope, d0, d1, d2, d3, u0, u1, u2, u3, gf, nrm, inv, gain, vecf, gp, gm_ref, gml_ref, vec, acc
):
    step = pl.program_id(0)
    tile = slope.shape[2]
    total = None
    for r, (w_d, w_u) in enumerate(((d0, u0), (d1, u1), (d2, u2), (d3, u3))):
        pre = (nt(gl[...], w_d[...]) * slope[r].astype(F32)).astype(BF16)
        gp[r] = pre
        sums = jnp.sum(pre.astype(F32), axis=0, keepdims=True)
        vec[r : r + 1, pl.ds(pl.multiple_of(step * tile, tile), tile)] = sums
        term = nt(pre, w_u[...])
        total = term if total is None else total + term

    @pl.when(step == 0)
    def _():
        acc[...] = total

    @pl.when(step > 0)
    def _():
        acc[...] += total

    @pl.when(step == pl.num_programs(0) - 1)
    def _():
        def body(rows, carry):
            grad = acc[rows, :] + gf[rows, :]
            normed = nrm[rows, :]
            c = grad * gain[...]
            gm = inv[rows, 0:1] * (
                c
                - jnp.mean(c, axis=-1, keepdims=True)
                - normed * jnp.mean(c * normed, axis=-1, keepdims=True)
            )
            gm_ref[rows, :] = gm
            gml_ref[rows, :] = gm.astype(BF16)
            return tuple(a + b for a, b in zip(carry, (fold(grad * normed), fold(grad), fold(gm))))

        zero = jnp.zeros((8, gf.shape[1]), F32)
        sums = by_rows(gf.shape[0], 64, body, (zero, zero, zero))
        for j, total in enumerate(sums):
            vec[4 + j : 5 + j, :] = jnp.sum(total, axis=0, keepdims=True)
        vec[7:10, :] = vecf[0:3, :]
        vec[10:16, :] = jnp.zeros((6, gf.shape[1]), F32)


def back(gl, slope, ds, us, gf, nrm, inv, gain, vecf):
    seq, d = gf.shape
    units = slope.shape[2]
    tile = 256
    tall = pl.BlockSpec((4, seq, tile), lambda n: (0, 0, n))
    w_d = pl.BlockSpec((tile, d), lambda n: (n, 0))
    w_u = pl.BlockSpec((d, tile), lambda n: (0, n))
    return pl.pallas_call(
        back_kernel,
        out_shape=(
            jax.ShapeDtypeStruct((4, seq, units), BF16),
            jax.ShapeDtypeStruct((seq, d), F32),
            jax.ShapeDtypeStruct((seq, d), BF16),
            jax.ShapeDtypeStruct((16, d), F32),
        ),
        grid=(units // tile,),
        in_specs=[whole(seq, d), tall]
        + [w_d] * 4
        + [w_u] * 4
        + [whole(seq, d), whole(seq, d), whole(seq, 128), whole(1, d), whole(8, d)],
        out_specs=[tall, held(seq, d), held(seq, d), held(16, d)],
        scratch_shapes=[pltpu.VMEM((seq, d), F32)],
        compiler_params=params(28),
        cost_estimate=cost(10.8),
        name="back",
    )(gl, slope, *ds, *us, gf, nrm, inv, gain, vecf)


def place(idx, e, z_major=False):
    first, second = (idx[2], idx[1]) if z_major else (idx[1], idx[2])
    return jnp.bitwise_xor(e // 2, first) * 2 + jnp.bitwise_xor(e % 2, second)


def spread(idx, value, put, z_major=False):
    size = value.shape[0] // 4
    for e in range(4):
        put(place(idx, e, z_major), size, value[e * size : (e + 1) * size])


def slot_rows(slot, size):
    return pl.ds(pl.multiple_of(slot * size, 16), size)


def put_halves(first, second):
    def put(slot, size, piece):
        @pl.when(slot < 2)
        def _():
            first[slot_rows(slot, size), :] = piece.astype(BF16)

        @pl.when(slot >= 2)
        def _():
            second[slot_rows(slot - 2, size), :] = piece.astype(BF16)

    return put


def outer_kernel(flip, split, idx, left, varied, out, *rest):
    step = pl.program_id(0)
    value = tn(varied[0], left[...]) if flip else tn(left[...], varied[0])

    def whole_to(ref):
        def put(slot, size, piece):
            ref[slot_rows(slot, size), :] = piece.astype(BF16)

        spread(idx, value, put)

    @pl.when(step < 2)
    def _():
        whole_to(out.at[step])

    if split:
        @pl.when(step >= 2)
        def _():
            spread(idx, value, put_halves(rest[0].at[step - 2], rest[1].at[step - 2]))

    else:
        @pl.when(step == 2)
        def _():
            whole_to(rest[0])

        @pl.when(step == 3)
        def _():
            spread(idx, value, put_halves(rest[1], rest[2]))


def outer(flip, split, idx, left, varied):
    seq, d = left.shape
    units = varied.shape[2]
    rows, cols = (units, d) if flip else (d, units)
    if split:
        kept = [(2, rows // 2, cols)] * 2
    else:
        kept = [(rows, cols), (rows // 2, cols), (rows // 2, cols)]
    member = lambda g, s: (jnp.where(g < 2, 3 - 2 * g, 6 - 2 * g), 0, 0)
    return pl.pallas_call(
        partial(outer_kernel, flip, split),
        out_shape=[jax.ShapeDtypeStruct(a, BF16) for a in [(2, rows, cols)] + kept],
        grid_spec=pltpu.PrefetchScalarGridSpec(
            num_scalar_prefetch=1,
            grid=(4,),
            in_specs=[whole(seq, d), pl.BlockSpec((1, seq, units), member)],
            out_specs=[whole(*a) for a in [(2, rows, cols)] + kept],
        ),
        compiler_params=params(20),
        cost_estimate=cost(5.5),
        name="outer",
    )(idx, left, varied)


def attend_bwd_kernel(count, later, last, idx, x_ref, *rest):
    gmls, rest = rest[:count], rest[count:]
    q_ref, k_ref, v_ref, p_ref, ctx_ref, wq, wk, wv, wo = rest[:9]
    rest = rest[9:]
    if later:
        before, vec_before = rest[:2]
        rest = rest[2:]
    parts, rest = rest[:count], rest[count:]
    if last:
        qk_first, qk_second, vo_first, vo_second, vec, grads, gq_s, gk_s, gv_s = rest
    else:
        grads, vec, gq_s, gk_s, gv_s = rest
    step = pl.program_id(0)
    seq = x_ref.shape[0]
    width = wq.shape[0]
    blocks = seq // BAND

    @pl.when(step == 0)
    def _():
        if later:
            grads[...] = before[...]
            vec[...] = vec_before[...]
        else:
            grads[...] = jnp.zeros_like(grads)
            vec[...] = jnp.zeros_like(vec)

    gml = gmls[0][...] if count == 1 else jnp.where(step == 0, gmls[0][...], gmls[1][...])
    x, ctx, q_t, k = x_ref[...], ctx_ref[0], q_ref[0], k_ref[0]
    gctx = nt(gml, wo[...]).astype(BF16)
    gctx_t = jnp.transpose(gctx)
    g_tiles, v_rows, k_cols = tiles_of_heads(gctx), rows_of_heads(v_ref[0]), columns_of_heads(k)
    heads = range(len(g_tiles))
    gk = [[None] * blocks for _ in heads]
    gv = [[None] * blocks for _ in heads]
    for i in range(blocks):
        lo, hi = window(i, seq)
        rows = slice(i * BAND, (i + 1) * BAND)
        probs_low = [p_ref[0, h, rows, 0 : hi - lo] for h in heads]
        gprobs = [nn(g_tiles[h][rows], v_rows[h][:, lo:hi]) for h in heads]
        probs = [p.astype(F32) for p in probs_low]
        dots = [jnp.sum(a * b, axis=-1, keepdims=True) for a, b in zip(gprobs, probs)]
        gscores = [(p * (g - t)).astype(BF16) for g, p, t in zip(gprobs, probs, dots)]
        store_tiles(gq_s, rows, [nn(gscores[h], k_cols[h][lo:hi]) for h in heads], HEAD**-0.5)
        for h in heads:
            mine = slice(h * HEAD, (h + 1) * HEAD)
            gk_i = nn(q_t[mine, rows], gscores[h])
            gv_i = nn(gctx_t[mine, rows], probs_low[h])
            for j in range(lo // BAND, hi // BAND):
                at = slice(j * BAND - lo, (j + 1) * BAND - lo)
                gk[h][j] = gk_i[:, at] if gk[h][j] is None else gk[h][j] + gk_i[:, at]
                gv[h][j] = gv_i[:, at] if gv[h][j] is None else gv[h][j] + gv_i[:, at]
    for h in heads:
        mine = slice(h * HEAD, (h + 1) * HEAD)
        for j in range(blocks):
            cols = slice(j * BAND, (j + 1) * BAND)
            gk_s[mine, cols] = gk[h][j].astype(BF16)
            gv_s[mine, cols] = gv[h][j].astype(BF16)
    gq, gk_t, gv_t = gq_s[...], gk_s[...], gv_s[...]
    gv_n = jnp.transpose(gv_t)
    grads[0:width] += tn(gq, x)
    grads[width : 2 * width] += nn(gk_t, x)
    grads[2 * width : 3 * width] += nn(gv_t, x)
    grads[3 * width : 4 * width] += tn(ctx, gml)
    vec[0:1, 0:width] += jnp.sum(gq.astype(F32), axis=0, keepdims=True)
    vec[1:2, 0:width] += jnp.sum(gv_n.astype(F32), axis=0, keepdims=True)
    part = (nn(gq, wq[...]) + nn(jnp.transpose(gk_t), wk[...]) + nn(gv_n, wv[...])).astype(BF16)

    for j, ref in enumerate(parts):

        @pl.when(step == j)
        def _():
            ref[...] = part

    if last:

        @pl.when(step == count - 1)
        def _():
            spread(idx, grads[0 : 2 * width], put_halves(qk_first, qk_second))
            spread(idx, grads[2 * width : 4 * width], put_halves(vo_first, vo_second), True)


def attend_bwd(base, last, idx, x, gmls, kept, wq, wk, wv, wo, before=None):
    q, k, v, p, ctx = kept
    width, d = wq.shape
    seq = gmls[0].shape[0]
    heads = width // HEAD
    count = len(gmls)
    later = before is not None
    slot = lambda g, s: (count - 1 - g, 0, 0)
    natural = pl.BlockSpec((1, seq, width), slot)
    turned = pl.BlockSpec((1, width, seq), slot)
    specs = [
        pl.BlockSpec((seq, d), lambda g, s: (jnp.bitwise_xor(s[0], base + g), 0)),
    ] + [whole(seq, d)] * count + [
        turned,
        natural,
        turned,
        pl.BlockSpec((1, heads, seq, 3 * BAND), lambda g, s: (count - 1 - g, 0, 0, 0)),
        natural,
    ] + [whole(width, d)] * 4
    args = (idx, x, *gmls, q, k, v, p, ctx, wq, wk, wv, wo)
    part = jax.ShapeDtypeStruct((seq, d), BF16)
    small = jax.ShapeDtypeStruct((8, d), F32)
    scratch = [
        pltpu.VMEM((seq, width), BF16),
        pltpu.VMEM((width, seq), BF16),
        pltpu.VMEM((width, seq), BF16),
    ]
    if later:
        specs += [whole(4 * width, d), whole(8, d)]
        args += tuple(before)
    if last:
        shapes = (part,) * count + (jax.ShapeDtypeStruct((width, d), BF16),) * 4 + (small,)
        outs = [held(seq, d)] * count + [held(width, d)] * 4 + [held(8, d)]
        scratch = [pltpu.VMEM((4 * width, d), F32)] + scratch
    else:
        shapes = (part,) * count + (jax.ShapeDtypeStruct((4 * width, d), F32), small)
        outs = [held(seq, d)] * count + [held(4 * width, d), held(8, d)]
    return pl.pallas_call(
        partial(attend_bwd_kernel, count, later, last),
        out_shape=shapes,
        grid_spec=pltpu.PrefetchScalarGridSpec(
            num_scalar_prefetch=1, grid=(count,), in_specs=specs, out_specs=outs, scratch_shapes=scratch
        ),
        compiler_params=params(28),
        cost_estimate=cost(5.0 * count),
        name="attend_bwd",
    )(*args)


def join_kernel(idx, p0, p1, p2, p3, out):
    rows = p0.shape[0]
    for j, piece in enumerate((p0, p1, p2, p3)):
        quarter = jnp.bitwise_xor(idx[1], j // 2) * 2 + jnp.bitwise_xor(
            jnp.bitwise_and(idx[2], 1), j % 2
        )
        out[pl.ds(pl.multiple_of(quarter * rows, 16), rows), :] = piece[...]


def join(idx, pieces):
    rows, d = pieces[0].shape
    return pl.pallas_call(
        join_kernel,
        out_shape=jax.ShapeDtypeStruct((4 * rows, d), pieces[0].dtype),
        grid_spec=pltpu.PrefetchScalarGridSpec(
            num_scalar_prefetch=1,
            grid=(1,),
            in_specs=[whole(rows, d)] * 4,
            out_specs=whole(4 * rows, d),
        ),
        compiler_params=params(6),
        cost_estimate=cost(0.7),
        name="join",
    )(idx, *pieces)


def unpack_kernel(groups, idx, *refs):
    outs = refs[-1 if len(groups) == 1 else -4 :]
    pieces = refs[: len(refs) - len(outs)]
    each = len(pieces) // len(groups)
    for j, z_major in enumerate(groups):
        mine = pieces[j * each : (j + 1) * each]
        size = mine[0].shape[0] * each // 4
        for slot in range(4):
            piece = mine[slot][...] if each == 4 else mine[0][slot * size : (slot + 1) * size]
            at = place(idx, slot, z_major)
            if len(groups) == 1:
                outs[0][slot_rows(at, size), :] = piece.astype(F32)
            else:
                for h in range(2):
                    @pl.when(at // 2 == h)
                    def _():
                        outs[2 * j + h][slot_rows(at % 2, size), :] = piece.astype(F32)


def unpack(idx, groups, pieces):
    d = pieces[0].shape[1]
    total = sum(p.shape[0] for p in pieces)
    shapes = [(total // 4, d)] * 4 if len(groups) == 2 else [(total, d)]
    return pl.pallas_call(
        partial(unpack_kernel, groups),
        out_shape=[jax.ShapeDtypeStruct(s, F32) for s in shapes],
        grid_spec=pltpu.PrefetchScalarGridSpec(
            num_scalar_prefetch=1,
            grid=(1,),
            in_specs=[whole(*p.shape) for p in pieces],
            out_specs=[whole(*s) for s in shapes],
        ),
        compiler_params=params(10),
        cost_estimate=cost(2.1),
        name="unpack",
    )(idx, *pieces)


def mix_kernel(order, v, r, out):
    for j, other in enumerate(order):
        out[j : j + 1, :] = v[j : j + 1, :] + r[other : other + 1, :]
    out[len(order) :, :] = v[len(order) :, :] + r[len(order) :, :]


def settle_kernel(v, r, att, out):
    out[0:1, :] = v[0:1, :] + r[2:3, :]
    out[1:7, :] = v[4:10, :] + r[4:10, :]
    out[7:9, :] = att[0:2, :]
    out[9:16, :] = jnp.zeros_like(out[9:16, :])


def small(kernel, *arrays):
    return pl.pallas_call(
        kernel,
        out_shape=jax.ShapeDtypeStruct(arrays[0].shape, F32),
        compiler_params=params(4),
        cost_estimate=cost(0.5),
        name="small",
    )(*arrays)


def finish_kernel(a, b, c, gm, out):
    total = a[...].astype(F32) + b[...].astype(F32) + c[...].astype(F32) + gm[...]
    out[...] = total.astype(BF16)


def finish(a, b, c, gm):
    seq, d = a.shape
    tile = seq // 4
    part = pl.BlockSpec((tile, d), lambda n: (n, 0))
    return pl.pallas_call(
        finish_kernel,
        out_shape=jax.ShapeDtypeStruct((seq, d), BF16),
        grid=(4,),
        in_specs=[part] * 4,
        out_specs=part,
        compiler_params=params(8),
        cost_estimate=cost(1.7),
        name="finish",
    )(a, b, c, gm)


def over(name, bit):
    size = lax.axis_size(name)
    pairs = [(i, i ^ bit) for i in range(size)]
    return lambda a: lax.ppermute(a, name, pairs)


class Order:
    def __init__(self):
        self.last = ()

    def then(self, a):
        return lax.optimization_barrier((a, self.last))[0]

    def done(self, out):
        self.last = (jax.tree.leaves(out)[-1],)
        return out

    def wait(self, *arrays):
        arrays = self.then(arrays)
        self.last = self.last + tuple(arrays)
        return arrays


def local(
    inputs, segment_ids, cotangent, query_weight, key_weight, value_weight, query_bias, value_bias,
    output_weight, output_bias, middle_gain, middle_shift, up_weight, up_bias, down_weight, down_bias,
    final_gain, final_shift,
):
    rows_here, seq = segment_ids.shape
    members = lax.axis_size("mp")
    assert members == 4 and rows_here == 4
    staged = lax.axis_size("dp") == 8
    me = lax.axis_index("mp")
    spot = lax.axis_index("dp")
    x_bit = jnp.bitwise_and(spot, 1) if staged else 0 * spot
    z_bit = jnp.bitwise_and(jnp.right_shift(spot, 1), 1) if staged else 0 * spot
    idx = jnp.stack([me, x_bit, z_bit]).astype(jnp.int32)
    core, y, both = over("mp", 1), over("mp", 2), over("mp", 3)
    x, z1, z2 = over("dp", 1), over("dp", 2), over("dp", 4)
    line = lambda v: v.reshape(1, -1)
    order = Order()
    then, done, wait = order.then, order.done, order.wait
    kernel = lambda f, *a: done(f(then(idx), *a))

    if staged:
        quarter = up_weight.shape[0] // 4
        at = (x_bit * 2 + z_bit) * quarter
        near_u = y(lax.dynamic_slice_in_dim(up_weight, at, quarter, 0))
        near_d = y(lax.dynamic_slice_in_dim(down_weight, at, quarter, 0))
    u1, d1 = core(up_weight), core(down_weight)
    ub = line(up_bias)
    ub1, ub2 = core(ub), y(ub)

    weights = (query_weight.T, key_weight.T, value_weight.T, output_weight)
    fwd = (inputs, segment_ids) + weights + (line(query_bias), line(value_bias))
    *kept3, part3 = kernel(partial(attend_fwd, 3, 1), *fwd)
    from3 = core(part3)
    *kept2, part2 = kernel(partial(attend_fwd, 2, 1), *fwd)
    if staged:
        (near_u,) = wait(near_u)
        x_u, z_u = x(near_u), z1(near_u)
    u1, d1, ub1, ub2 = wait(u1, d1, ub1, ub2)
    ub3 = core(ub2)
    other = y(done(part2 + then(from3)))
    if staged:
        (near_d,) = wait(near_d)
        x_d, z_d = x(near_d), z1(near_d)
    *kept10, part1, part0 = kernel(partial(attend_fwd, 1, 2), *fwd)
    from1 = core(part1)
    if staged:
        (x_u,) = wait(x_u)
        far_u = z1(x_u)
        z_u, ub3, z_d = wait(z_u, ub3, z_d)
        far_d = x(z_d)
        u2 = kernel(join, (near_u, z_u, x_u, far_u))
        u3 = core(u2)
        d2 = kernel(join, (near_d, z_d, x_d, far_d))
        d3 = core(d2)
    else:
        u2, u3, d2, d3 = y(up_weight), both(up_weight), y(down_weight), both(down_weight)
    us = (up_weight, u1, u2, u3)
    ds = (down_weight, d1, d2, d3)
    hidden, normed, inverse, low, act, slope = kernel(
        up, inputs, part0, from1, other, line(output_bias), line(middle_gain), line(middle_shift),
        us, (ub, ub1, ub2, ub3),
    )
    layer_out, grad_final, grad_low, vec_fin = kernel(
        down, act, ds, hidden, cotangent, line(down_bias), line(final_gain), line(final_shift)
    )

    gd31, first_d, second_d = kernel(partial(outer, True, True), grad_low, act)
    rd = core(gd31)
    gp, grad_mid, mid0, vec = done(
        back(grad_low, slope, ds, us, grad_final, normed, inverse, then(line(middle_gain)), vec_fin)
    )
    mid2, mid1 = y(mid0), core(mid0)
    vec_core = core(vec)
    half = first_d.shape[1]
    rd = then(rd)
    second_d = done(second_d + rd[:, half:])
    got_d = x(second_d) if staged else None
    gu31, far_w, first_u, second_u = kernel(partial(outer, False, False), low, gp)
    ru = core(gu31)
    in0, in1, *before = kernel(partial(attend_bwd, 0, False), inputs, (mid0, mid1), kept10, *weights)
    from_in1 = core(in1)
    (mid2,) = wait(mid2)
    mid3 = core(mid2)
    vec = done(small(partial(mix_kernel, (1, 0, 3, 2)), vec, then(vec_core)))
    vec_y = y(vec)
    ru = then(ru)
    got_u = y(done(far_w + ru[0]))
    in2, *before = kernel(partial(attend_bwd, 2, False), inputs, (mid2,), kept2, *weights, before)
    in3, qk_first, qk_second, vo_first, vo_second, vec_att = kernel(
        partial(attend_bwd, 3, True), inputs, (mid3,), kept3, *weights, before
    )
    width = query_bias.shape[0]

    if staged:
        def halved(base, got):
            got = then(got)
            n = got.shape[0] // 2
            return done((base[n:] + got[n:], base[:n] + got[:n]))[::-1]

        def summed(base, got):
            return done(base + then(got))

        got_qk, got_vo = x(qk_second), z1(vo_second)
        from_in3 = core(in3)
        got_d = then(got_d)
        own_d = first_d[1] + rd[1, :half] + got_d[1]
        more_d = y(done(first_d[0] + rd[0, :half] + got_d[0]))
        from_in2 = y(done(in2 + then(from_in3)))
        keep_qk, send_qk = halved(qk_first, got_qk)
        got_qk = z1(send_qk)
        keep_vo, send_vo = halved(vo_first, got_vo)
        got_vo = x(send_vo)
        vec = done(small(settle_kernel, vec, then(vec_y), vec_att))
        vec_x = x(vec)
        got_u = then(got_u)
        own_u = first_u + ru[1, :half] + got_u[:half]
        got_u = x(done(second_u + ru[1, half:] + got_u[half:]))
        s_qk = summed(keep_qk, got_qk)
        got_qk = z2(s_qk)
        s_vo = summed(keep_vo, got_vo)
        got_vo = z2(s_vo)
        keep_d, send_d = halved(own_d, more_d)
        got_d = z1(send_d)
        vec = summed(vec, vec_x)
        vec_z = z1(vec)
        s_qk = summed(s_qk, got_qk)
        q_qk, p_qk = z1(s_qk), x(s_qk)
        s_vo = summed(s_vo, got_vo)
        q_vo, p_vo = x(s_vo), z1(s_vo)
        keep_u, send_u = halved(own_u, got_u)
        got_u = z1(send_u)
        s_d = summed(keep_d, got_d)
        got_d = z2(s_d)
        (q_qk,) = wait(q_qk)
        r_qk = x(q_qk)
        (q_vo,) = wait(q_vo)
        r_vo = z1(q_vo)
        vec = summed(vec, vec_z)
        vec_z = z2(vec)
        s_u = summed(keep_u, got_u)
        got_u = z2(s_u)
        s_d = summed(s_d, got_d)
        q_d, p_d = z1(s_d), x(s_d)
        input_grad = done(finish(in0, from_in1, then(from_in2), grad_mid))
        s_u = summed(s_u, got_u)
        q_u, p_u = z1(s_u), x(s_u)
        (q_d,) = wait(q_d)
        r_d = x(q_d)
        grad_q, grad_k, grad_v, grad_o = kernel(
            unpack, (False, True), (s_qk, q_qk, p_qk, r_qk, s_vo, q_vo, p_vo, r_vo)
        )
        (q_u,) = wait(q_u)
        r_u = x(q_u)
        vec = summed(vec, vec_z)
        (grad_down,) = kernel(unpack, (False,), (s_d, q_d, p_d, r_d))
        (grad_up,) = kernel(unpack, (False,), (s_u, q_u, p_u, r_u))
    else:
        input_grad = finish(in0, from_in1, y(in2 + core(in3)), grad_mid)
        vec = small(settle_kernel, vec, vec_y, vec_att)
        first_d = first_d + rd[:, :half]
        td = jnp.concatenate([first_d[1], second_d[1]]) + y(
            jnp.concatenate([first_d[0], second_d[0]])
        )
        tu = jnp.concatenate([first_u, second_u]) + ru[1] + got_u
        qk = jnp.concatenate([qk_first, qk_second])
        vo = jnp.concatenate([vo_first, vo_second])
        td, tu, qk, vo, vec = lax.psum((td, tu, qk, vo, vec), "dp")
        (grad_down,) = unpack(idx, (False,), (td,))
        (grad_up,) = unpack(idx, (False,), (tu,))
        grad_q, grad_k, grad_v, grad_o = unpack(idx, (False, True), (qk, vo))

    return (
        layer_out, input_grad, grad_q.T, grad_k.T, grad_v.T, vec[7, :width], vec[8, :width], grad_o,
        vec[3], vec[1], vec[2], grad_up, vec[0], grad_down, vec[6], vec[4], vec[5],
    )


def solution(mesh):
    tokens = P("dp", None)
    columns, units, stacked, full = P(None, "mp"), P("mp"), P("mp", None), P()
    shared = P(("dp", "mp"), None)
    placed = (
        tokens, tokens, tokens, columns, columns, columns, units, units, stacked, full, full, full,
        columns, units, stacked, full, full, full,
    )
    given = (
        shared, shared, columns, columns, columns, units, units, stacked, full, full, full,
        columns, units, stacked, full, full, full,
    )
    return jax.shard_map(local, mesh=mesh, in_specs=placed, out_specs=given, check_vma=False)
```

```python
from functools import partial

import jax
import jax.numpy as jnp
from jax import lax
from jax.experimental import pallas as pl
from jax.experimental.pallas import tpu as pltpu
from jax.sharding import PartitionSpec as P

HEAD = 64
BAND = 128
EPSILON = 1e-12
ROOT_HALF = 0.7071067811865476
INV_ROOT_TAU = 0.3989422804014327
MASKED = -1e30
TAIL = 8
F32 = jnp.float32
BF16 = jnp.bfloat16
MIB = 1024 * 1024
SCALE = 4.0


def nn(a, b):
    return lax.dot_general(a, b, (((1,), (0,)), ((), ())), preferred_element_type=F32)


def nt(a, b):
    return lax.dot_general(a, b, (((1,), (1,)), ((), ())), preferred_element_type=F32)


def tn(a, b):
    return lax.dot_general(a, b, (((0,), (0,)), ((), ())), preferred_element_type=F32)


def window(block, seq):
    lo = max(block * BAND - BAND, 0)
    hi = min(block * BAND + 2 * BAND, seq)
    return lo, hi


def params(mib):
    return pltpu.CompilerParams(vmem_limit_bytes=mib * MIB)


def cost(us):
    return pl.CostEstimate(
        flops=int(us * SCALE * 1.15e9), bytes_accessed=int(us * SCALE * 3.6e6), transcendentals=0
    )


def whole(*shape):
    return pl.BlockSpec(shape, lambda *_: (0,) * len(shape), pipeline_mode=pl.Buffered(1))


def held(*shape):
    return pl.BlockSpec(shape, lambda *_: (0,) * len(shape))


def rows_of_heads(a):
    zero = jnp.zeros((HEAD, a.shape[1]), a.dtype)
    tiles = []
    for h in range(a.shape[0] // HEAD):
        mine = a[h * HEAD : (h + 1) * HEAD]
        if h % 2 == 0 and (h + 1) * HEAD == a.shape[0]:
            tiles.append(mine)
        else:
            tiles.append(jnp.concatenate([mine, zero] if h % 2 == 0 else [zero, mine], axis=0))
    return tiles


def tiles_of_heads(a):
    width = a.shape[1]
    return [a[:, h // 2 * 128 : min(h // 2 * 128 + 128, width)] for h in range(width // HEAD)]


def columns_of_heads(a):
    masked = []
    for h, tile in enumerate(tiles_of_heads(a)):
        if tile.shape[1] == HEAD:
            masked.append(tile)
        else:
            lane = lax.broadcasted_iota(jnp.int32, tile.shape, 1)
            masked.append(jnp.where((lane < HEAD) == (h % 2 == 0), tile, jnp.zeros_like(tile)))
    return masked


def store_tiles(ref, rows, per_head, scale=None):
    for at in range(0, len(per_head), 2):
        total = per_head[at] if at + 1 == len(per_head) else per_head[at] + per_head[at + 1]
        if scale is not None:
            total = total * scale
        lo = at * HEAD
        ref[rows, lo : lo + total.shape[1]] = total.astype(ref.dtype)


def attend_fwd_kernel(base, idx, x_ref, seg_ref, wq, wk, wv, wo, qb, vb,
                      q_ref, k_ref, v_ref, p_ref, ctx_ref, *parts):
    step = pl.program_id(0)
    seq = x_ref.shape[0]
    row = jnp.bitwise_xor(idx[0], base - step)
    x = x_ref[...]
    q = ((nt(x, wq[...]) + qb[...]).astype(BF16) * (HEAD**-0.5)).astype(BF16)
    k_t = nt(wk[...], x).astype(BF16)
    v = (nt(x, wv[...]) + vb[...]).astype(BF16)
    q_ref[0] = jnp.transpose(q)
    k_ref[0] = jnp.transpose(k_t)
    v_ref[0] = jnp.transpose(v)
    q_tiles, k_rows, v_cols = tiles_of_heads(q), rows_of_heads(k_t), columns_of_heads(v)
    heads = range(len(q_tiles))
    seg_row = seg_ref[pl.ds(row, 1), :]
    for i in range(seq // BAND):
        lo, hi = window(i, seq)
        rows = slice(i * BAND, (i + 1) * BAND)
        seg_k = jnp.broadcast_to(seg_row[:, lo:hi], (BAND, hi - lo))
        seg_q = jnp.transpose(jnp.broadcast_to(seg_row[:, rows], (BAND, BAND)))
        same = jnp.concatenate([seg_q] * ((hi - lo) // BAND), axis=1) == seg_k
        scores = [jnp.where(same, nn(q_tiles[h][rows], k_rows[h][:, lo:hi]), MASKED) for h in heads]
        tops = [jnp.max(a, axis=-1, keepdims=True) for a in scores]
        expos = [jnp.exp(a - m) for a, m in zip(scores, tops)]
        scales = [1.0 / jnp.sum(e, axis=-1, keepdims=True) for e in expos]
        probs = [(e * t).astype(BF16) for e, t in zip(expos, scales)]
        for h in heads:
            p_ref[0, h, rows, 0 : hi - lo] = probs[h]
        store_tiles(ctx_ref.at[0], rows, [nn(probs[h], v_cols[h][lo:hi]) for h in heads])
    part = nn(ctx_ref[0], wo[...]).astype(BF16)
    for j, ref in enumerate(parts):

        @pl.when(step == j)
        def _():
            ref[...] = part


def attend_fwd(base, count, idx, x, seg, wq, wk, wv, wo, qb, vb):
    seq = seg.shape[1]
    width, d = wq.shape
    heads = width // HEAD
    slot = lambda g, s: (g, 0, 0)
    natural = pl.BlockSpec((1, seq, width), slot)
    turned = pl.BlockSpec((1, width, seq), slot)
    saved = (
        jax.ShapeDtypeStruct((count, width, seq), BF16),
        jax.ShapeDtypeStruct((count, seq, width), BF16),
        jax.ShapeDtypeStruct((count, width, seq), BF16),
        jax.ShapeDtypeStruct((count, heads, seq, 3 * BAND), BF16),
        jax.ShapeDtypeStruct((count, seq, width), BF16),
    )
    args = (idx, x, seg, wq, wk, wv, wo, qb, vb)
    specs = [
        pl.BlockSpec((seq, d), lambda g, s: (jnp.bitwise_xor(s[0], base - g), 0)),
        whole(*seg.shape),
        whole(width, d),
        whole(width, d),
        whole(width, d),
        whole(width, d),
        whole(1, width),
        whole(1, width),
    ]
    return pl.pallas_call(
        partial(attend_fwd_kernel, base),
        out_shape=saved + (jax.ShapeDtypeStruct((seq, d), BF16),) * count,
        grid_spec=pltpu.PrefetchScalarGridSpec(
            num_scalar_prefetch=1,
            grid=(count,),
            in_specs=specs,
            out_specs=[
                turned,
                natural,
                turned,
                pl.BlockSpec((1, heads, seq, 3 * BAND), lambda g, s: (g, 0, 0, 0)),
                natural,
            ]
            + [held(seq, d)] * count,
        ),
        compiler_params=params(60),
        cost_estimate=cost(3.2 * count),
        name="attend_fwd",
    )(*args)


def gelu_parts(v):
    half = 0.5 * (1.0 + lax.erf(v * ROOT_HALF))
    return v * half, half + v * jnp.exp(-0.5 * v * v) * INV_ROOT_TAU


def by_rows(total, step, body, carry):
    def one(i, c):
        return body(pl.ds(pl.multiple_of(i * step, step), step), c)

    return lax.fori_loop(0, total // step, one, carry, unroll=True)


def fold(a):
    return jnp.sum(a.reshape(a.shape[0] // 8, 8, a.shape[1]), axis=0)


def up_kernel(
    idx, x_ref, pa, pb, pc, ob, gain, shift, u0, u1, u2, u3, b0, b1, b2, b3,
    hid, nrm, inv, low, act, slope,
):
    @pl.when(pl.program_id(0) == 0)
    def _():
        def body(rows, carry):
            middle = (
                pa[rows, :].astype(F32)
                + pb[rows, :].astype(F32)
                + pc[rows, :].astype(F32)
                + ob[...]
                + x_ref[rows, :].astype(F32)
            )
            centred = middle - jnp.mean(middle, axis=-1, keepdims=True)
            r = lax.rsqrt(jnp.mean(centred * centred, axis=-1, keepdims=True) + EPSILON)
            normed = centred * r
            hidden = normed * gain[...] + shift[...]
            nrm[rows, :] = normed
            inv[rows, :] = jnp.broadcast_to(r, (r.shape[0], 128))
            hid[rows, :] = hidden
            low[rows, :] = hidden.astype(BF16)
            return carry

        by_rows(low.shape[0], 64, body, 0)

    for r, (u, b) in enumerate(((u0, b0), (u1, b1), (u2, b2), (u3, b3))):
        value, deriv = gelu_parts(nn(low[...], u[...]) + b[...])
        act[r] = value.astype(BF16)
        slope[r] = deriv.astype(BF16)


def up(idx, x, own, recv, other, ob, gain, shift, us, bs):
    seq, d = other.shape
    units = us[0].shape[1]
    tile = 256
    row = pl.BlockSpec((seq, d), lambda n, s: (s[0], 0), pipeline_mode=pl.Buffered(1))
    wide = pl.BlockSpec((d, tile), lambda n, s: (0, n))
    bias = pl.BlockSpec((1, tile), lambda n, s: (0, n))
    out = pl.BlockSpec((4, seq, tile), lambda n, s: (0, 0, n))
    return pl.pallas_call(
        up_kernel,
        out_shape=(
            jax.ShapeDtypeStruct((seq, d), F32),
            jax.ShapeDtypeStruct((seq, d), F32),
            jax.ShapeDtypeStruct((seq, 128), F32),
            jax.ShapeDtypeStruct((seq, d), BF16),
            jax.ShapeDtypeStruct((4, seq, units), BF16),
            jax.ShapeDtypeStruct((4, seq, units), BF16),
        ),
        grid_spec=pltpu.PrefetchScalarGridSpec(
            num_scalar_prefetch=1,
            grid=(units // tile,),
            in_specs=[row] + [whole(seq, d)] * 3 + [whole(1, d)] * 3 + [wide] * 4 + [bias] * 4,
            out_specs=[held(seq, d), held(seq, d), held(seq, 128), held(seq, d), out, out],
        ),
        compiler_params=params(28),
        cost_estimate=cost(7.3),
        name="up",
    )(idx, x, own, recv, other, ob, gain, shift, *us, *bs)


def down_kernel(idx, act, d0, d1, d2, d3, hid, cot, db, gain, shift, out_ref, gf_ref, gl_ref, vec, acc):
    step = pl.program_id(0)
    total = None
    for r, w in enumerate((d0, d1, d2, d3)):
        term = nn(act[r], w[...])
        total = term if total is None else total + term
    acc[step] = total

    @pl.when(step == pl.num_programs(0) - 1)
    def _():
        def body(rows, carry):
            parts = [acc[n, rows, :] for n in range(acc.shape[0])]
            final = jnp.concatenate(parts, axis=1) + db[...] + hid[rows, :]
            centred = final - jnp.mean(final, axis=-1, keepdims=True)
            r = lax.rsqrt(jnp.mean(centred * centred, axis=-1, keepdims=True) + EPSILON)
            normed = centred * r
            out_ref[rows, :] = (normed * gain[...] + shift[...]).astype(BF16)
            cv = cot[rows, :].astype(F32)
            c = cv * gain[...]
            grad = r * (
                c
                - jnp.mean(c, axis=-1, keepdims=True)
                - normed * jnp.mean(c * normed, axis=-1, keepdims=True)
            )
            gf_ref[rows, :] = grad
            gl_ref[rows, :] = grad.astype(BF16)
            return tuple(a + b for a, b in zip(carry, (fold(cv * normed), fold(cv), fold(grad))))

        zero = jnp.zeros((8, hid.shape[1]), F32)
        sums = by_rows(hid.shape[0], 64, body, (zero, zero, zero))
        vec[...] = jnp.zeros_like(vec)
        for j, total in enumerate(sums):
            vec[j : j + 1, :] = jnp.sum(total, axis=0, keepdims=True)


def down(idx, act, ds, hid, cot, db, gain, shift):
    seq, d = hid.shape
    units = act.shape[2]
    tile = 256
    wide = pl.BlockSpec((units, tile), lambda n, s: (0, n))
    row = pl.BlockSpec((seq, d), lambda n, s: (s[0], 0), pipeline_mode=pl.Buffered(1))
    return pl.pallas_call(
        down_kernel,
        out_shape=(
            jax.ShapeDtypeStruct((seq, d), BF16),
            jax.ShapeDtypeStruct((seq, d), F32),
            jax.ShapeDtypeStruct((seq, d), BF16),
            jax.ShapeDtypeStruct((8, d), F32),
        ),
        grid_spec=pltpu.PrefetchScalarGridSpec(
            num_scalar_prefetch=1,
            grid=(d // tile,),
            in_specs=[whole(4, seq, units)] + [wide] * 4 + [whole(seq, d), row] + [whole(1, d)] * 3,
            out_specs=[held(seq, d), held(seq, d), held(seq, d), held(8, d)],
            scratch_shapes=[pltpu.VMEM((d // tile, seq, tile), F32)],
        ),
        compiler_params=params(24),
        cost_estimate=cost(6.2),
        name="down",
    )(idx, act, *ds, hid, cot, db, gain, shift)


def back_kernel(
    gl, slope, d0, d1, d2, d3, u0, u1, u2, u3, gf, nrm, inv, gain, vecf, gp, gm_ref, gml_ref, vec, acc
):
    step = pl.program_id(0)
    tile = slope.shape[2]
    total = None
    for r, (w_d, w_u) in enumerate(((d0, u0), (d1, u1), (d2, u2), (d3, u3))):
        pre = (nt(gl[...], w_d[...]) * slope[r].astype(F32)).astype(BF16)
        gp[r] = pre
        sums = jnp.sum(pre.astype(F32), axis=0, keepdims=True)
        vec[r : r + 1, pl.ds(pl.multiple_of(step * tile, tile), tile)] = sums
        term = nt(pre, w_u[...])
        total = term if total is None else total + term

    @pl.when(step == 0)
    def _():
        acc[...] = total

    @pl.when(step > 0)
    def _():
        acc[...] += total

    @pl.when(step == pl.num_programs(0) - 1)
    def _():
        def body(rows, carry):
            grad = acc[rows, :] + gf[rows, :]
            normed = nrm[rows, :]
            c = grad * gain[...]
            gm = inv[rows, 0:1] * (
                c
                - jnp.mean(c, axis=-1, keepdims=True)
                - normed * jnp.mean(c * normed, axis=-1, keepdims=True)
            )
            gm_ref[rows, :] = gm
            gml_ref[rows, :] = gm.astype(BF16)
            return tuple(a + b for a, b in zip(carry, (fold(grad * normed), fold(grad), fold(gm))))

        zero = jnp.zeros((8, gf.shape[1]), F32)
        sums = by_rows(gf.shape[0], 64, body, (zero, zero, zero))
        for j, total in enumerate(sums):
            vec[4 + j : 5 + j, :] = jnp.sum(total, axis=0, keepdims=True)
        vec[7:10, :] = vecf[0:3, :]
        vec[10:16, :] = jnp.zeros((6, gf.shape[1]), F32)


def back(gl, slope, ds, us, gf, nrm, inv, gain, vecf):
    seq, d = gf.shape
    units = slope.shape[2]
    tile = 256
    tall = pl.BlockSpec((4, seq, tile), lambda n: (0, 0, n))
    w_d = pl.BlockSpec((tile, d), lambda n: (n, 0))
    w_u = pl.BlockSpec((d, tile), lambda n: (0, n))
    return pl.pallas_call(
        back_kernel,
        out_shape=(
            jax.ShapeDtypeStruct((4, seq, units), BF16),
            jax.ShapeDtypeStruct((seq, d), F32),
            jax.ShapeDtypeStruct((seq, d), BF16),
            jax.ShapeDtypeStruct((16, d), F32),
        ),
        grid=(units // tile,),
        in_specs=[whole(seq, d), tall]
        + [w_d] * 4
        + [w_u] * 4
        + [whole(seq, d), whole(seq, d), whole(seq, 128), whole(1, d), whole(8, d)],
        out_specs=[tall, held(seq, d), held(seq, d), held(16, d)],
        scratch_shapes=[pltpu.VMEM((seq, d), F32)],
        compiler_params=params(28),
        cost_estimate=cost(10.8),
        name="back",
    )(gl, slope, *ds, *us, gf, nrm, inv, gain, vecf)


def place(idx, e, z_major=False):
    first, second = (idx[2], idx[1]) if z_major else (idx[1], idx[2])
    return jnp.bitwise_xor(e // 2, first) * 2 + jnp.bitwise_xor(e % 2, second)


def spread(idx, value, put, z_major=False):
    size = value.shape[0] // 4
    for e in range(4):
        put(place(idx, e, z_major), size, value[e * size : (e + 1) * size])


def slot_rows(slot, size):
    return pl.ds(pl.multiple_of(slot * size, 8), size)


def put_halves(first, second):
    def put(slot, size, piece):
        @pl.when(slot < 2)
        def _():
            first[slot_rows(slot, size), :] = piece.astype(BF16)

        @pl.when(slot >= 2)
        def _():
            second[slot_rows(slot - 2, size), :] = piece.astype(BF16)

    return put


def outer_kernel(flip, z_major, halves, idx, left, varied, out, *kept):
    step = pl.program_id(0)
    value = tn(varied[0], left[...]) if flip else tn(left[...], varied[0])

    def whole_to(ref):
        def put(slot, size, piece):
            ref[slot_rows(slot, size), :] = piece.astype(BF16)

        return put

    @pl.when(step < 2)
    def _():
        spread(idx, value, whole_to(out.at[step]), z_major)

    if not halves:
        first, second = kept

        @pl.when(step >= 2)
        def _():
            spread(idx, value, put_halves(first.at[step - 2], second.at[step - 2]), z_major)

    else:
        far_left, near_first, near_second, first, second = kept
        n = far_left.shape[1]

        @pl.when(step >= 2)
        def _():
            spread(idx, value[:, n:], put_halves(first.at[step - 2], second.at[step - 2]), z_major)

        @pl.when(step == 2)
        def _():
            spread(idx, value[:, :n], whole_to(far_left), z_major)

        @pl.when(step == 3)
        def _():
            spread(idx, value[:, :n], put_halves(near_first, near_second), z_major)


def outer(flip, z_major, halves, idx, left, varied):
    seq, d = left.shape
    units = varied.shape[2]
    rows, cols = (units, d) if flip else (d, units)
    shapes = [(2, rows, cols)]
    if halves:
        cols = cols // 2
        shapes += [(rows, cols), (rows // 2, cols), (rows // 2, cols)]
    shapes += [(2, rows // 2, cols), (2, rows // 2, cols)]
    member = lambda g, s: (jnp.where(g < 2, 3 - 2 * g, 6 - 2 * g), 0, 0)
    return pl.pallas_call(
        partial(outer_kernel, flip, z_major, halves),
        out_shape=[jax.ShapeDtypeStruct(a, BF16) for a in shapes],
        grid_spec=pltpu.PrefetchScalarGridSpec(
            num_scalar_prefetch=1,
            grid=(4,),
            in_specs=[whole(seq, d), pl.BlockSpec((1, seq, units), member)],
            out_specs=[whole(*a) for a in shapes],
        ),
        compiler_params=params(20),
        cost_estimate=cost(5.5),
        name="outer",
    )(idx, left, varied)


def attend_bwd_kernel(count, later, last, idx, x_ref, *rest):
    gmls, rest = rest[:count], rest[count:]
    q_ref, k_ref, v_ref, p_ref, ctx_ref, wq, wk, wv, wo = rest[:9]
    rest = rest[9:]
    if later:
        before, vec_before = rest[:2]
        rest = rest[2:]
    if last:
        shared, shared_y = rest[:2]
        rest = rest[2:]
    parts, rest = rest[:count], rest[count:]
    if last:
        first, second, tail, vec, grads, gq_s, gk_s, gv_s = rest
    else:
        grads, vec, gq_s, gk_s, gv_s = rest
    step = pl.program_id(0)
    seq = x_ref.shape[0]
    width = wq.shape[0]
    blocks = seq // BAND

    @pl.when(step == 0)
    def _():
        if later:
            grads[...] = before[...]
            vec[...] = vec_before[...]
        else:
            grads[...] = jnp.zeros_like(grads)
            vec[...] = jnp.zeros_like(vec)

    gml = gmls[0][...] if count == 1 else jnp.where(step == 0, gmls[0][...], gmls[1][...])
    x, ctx, q_t, k = x_ref[...], ctx_ref[0], q_ref[0], k_ref[0]
    gctx = nt(gml, wo[...]).astype(BF16)
    gctx_t = jnp.transpose(gctx)
    g_tiles, v_rows, k_cols = tiles_of_heads(gctx), rows_of_heads(v_ref[0]), columns_of_heads(k)
    heads = range(len(g_tiles))
    gk = [[None] * blocks for _ in heads]
    gv = [[None] * blocks for _ in heads]
    for i in range(blocks):
        lo, hi = window(i, seq)
        rows = slice(i * BAND, (i + 1) * BAND)
        probs_low = [p_ref[0, h, rows, 0 : hi - lo] for h in heads]
        gprobs = [nn(g_tiles[h][rows], v_rows[h][:, lo:hi]) for h in heads]
        probs = [p.astype(F32) for p in probs_low]
        dots = [jnp.sum(a * b, axis=-1, keepdims=True) for a, b in zip(gprobs, probs)]
        gscores = [(p * (g - t)).astype(BF16) for g, p, t in zip(gprobs, probs, dots)]
        store_tiles(gq_s, rows, [nn(gscores[h], k_cols[h][lo:hi]) for h in heads], HEAD**-0.5)
        for h in heads:
            mine = slice(h * HEAD, (h + 1) * HEAD)
            gk_i = nn(q_t[mine, rows], gscores[h])
            gv_i = nn(gctx_t[mine, rows], probs_low[h])
            for j in range(lo // BAND, hi // BAND):
                at = slice(j * BAND - lo, (j + 1) * BAND - lo)
                gk[h][j] = gk_i[:, at] if gk[h][j] is None else gk[h][j] + gk_i[:, at]
                gv[h][j] = gv_i[:, at] if gv[h][j] is None else gv[h][j] + gv_i[:, at]
    for h in heads:
        mine = slice(h * HEAD, (h + 1) * HEAD)
        for j in range(blocks):
            cols = slice(j * BAND, (j + 1) * BAND)
            gk_s[mine, cols] = gk[h][j].astype(BF16)
            gv_s[mine, cols] = gv[h][j].astype(BF16)
    gq, gk_t, gv_t = gq_s[...], gk_s[...], gv_s[...]
    gv_n = jnp.transpose(gv_t)
    grads[0:width] += tn(gq, x)
    grads[width : 2 * width] += nn(gk_t, x)
    grads[2 * width : 3 * width] += nn(gv_t, x)
    grads[3 * width : 4 * width] += tn(ctx, gml)
    vec[0:1, 0:width] += jnp.sum(gq.astype(F32), axis=0, keepdims=True)
    vec[1:2, 0:width] += jnp.sum(gv_n.astype(F32), axis=0, keepdims=True)
    part = (nn(gq, wq[...]) + nn(jnp.transpose(gk_t), wk[...]) + nn(gv_n, wv[...])).astype(BF16)

    for j, ref in enumerate(parts):

        @pl.when(step == j)
        def _():
            ref[...] = part

    if last:

        @pl.when(step == count - 1)
        def _():
            tail[...] = jnp.zeros_like(tail)
            tail[0:1, :] = shared[0:1, :] + shared_y[2:3, :]
            for j in range(6):
                at = TAIL * ((j + 1) // 3) + (j + 1) % 3
                tail[at : at + 1, :] = shared[4 + j : 5 + j, :] + shared_y[4 + j : 5 + j, :]
            tail[2 * TAIL + 1 : 2 * TAIL + 3, :] = vec[0:2, :]
            for e in range(4):
                body = grads[e * width : (e + 1) * width]
                both = jnp.concatenate([body, tail[e * TAIL : (e + 1) * TAIL]], axis=0)
                put_halves(first, second)(place(idx, e), width + TAIL, both)


def attend_bwd(base, last, idx, x, gmls, kept, wq, wk, wv, wo, before=None, shared=()):
    q, k, v, p, ctx = kept
    width, d = wq.shape
    seq = gmls[0].shape[0]
    heads = width // HEAD
    count = len(gmls)
    later = before is not None
    slot = lambda g, s: (count - 1 - g, 0, 0)
    natural = pl.BlockSpec((1, seq, width), slot)
    turned = pl.BlockSpec((1, width, seq), slot)
    specs = [
        pl.BlockSpec((seq, d), lambda g, s: (jnp.bitwise_xor(s[0], base + g), 0)),
    ] + [whole(seq, d)] * count + [
        turned,
        natural,
        turned,
        pl.BlockSpec((1, heads, seq, 3 * BAND), lambda g, s: (count - 1 - g, 0, 0, 0)),
        natural,
    ] + [whole(width, d)] * 4
    args = (idx, x, *gmls, q, k, v, p, ctx, wq, wk, wv, wo)
    part = jax.ShapeDtypeStruct((seq, d), BF16)
    small = jax.ShapeDtypeStruct((8, d), F32)
    scratch = [
        pltpu.VMEM((seq, width), BF16),
        pltpu.VMEM((width, seq), BF16),
        pltpu.VMEM((width, seq), BF16),
    ]
    if later:
        specs += [whole(4 * width, d), whole(8, d)]
        args += tuple(before)
    if last:
        specs += [whole(16, d)] * 2
        args += tuple(shared)
        half = 2 * (width + TAIL)
        shapes = (part,) * count + (jax.ShapeDtypeStruct((half, d), BF16),) * 2
        outs = [held(seq, d)] * count + [held(half, d)] * 2
        scratch = [
            pltpu.VMEM((4 * TAIL, d), F32), pltpu.VMEM((8, d), F32), pltpu.VMEM((4 * width, d), F32)
        ] + scratch
    else:
        shapes = (part,) * count + (jax.ShapeDtypeStruct((4 * width, d), F32), small)
        outs = [held(seq, d)] * count + [held(4 * width, d), held(8, d)]
    return pl.pallas_call(
        partial(attend_bwd_kernel, count, later, last),
        out_shape=shapes,
        grid_spec=pltpu.PrefetchScalarGridSpec(
            num_scalar_prefetch=1, grid=(count,), in_specs=specs, out_specs=outs, scratch_shapes=scratch
        ),
        compiler_params=params(28),
        cost_estimate=cost(5.0 if later else 10.0),
        name="attend_bwd",
    )(*args)


def join_kernel(idx, *refs):
    pieces, outs = refs[:-2], refs[-2:]
    rows = pieces[0].shape[0]
    for j, piece in enumerate(pieces):
        at = place(idx, j % 4)
        outs[j // 4][slot_rows(at, rows), :] = piece[...]


def join(idx, *pieces):
    rows, d = pieces[0].shape
    return pl.pallas_call(
        join_kernel,
        out_shape=[jax.ShapeDtypeStruct((4 * rows, d), BF16)] * 2,
        grid_spec=pltpu.PrefetchScalarGridSpec(
            num_scalar_prefetch=1,
            grid=(1,),
            in_specs=[whole(rows, d)] * 8,
            out_specs=[whole(4 * rows, d)] * 2,
        ),
        compiler_params=params(8),
        cost_estimate=cost(1.0),
        name="join",
    )(idx, *pieces)


def unpack_kernel(z_major, given, tail, idx, *refs):
    pieces, outs = refs[:given], refs[given:]
    size = pieces[0].shape[0] * given // 4
    body = size - tail
    for slot in range(4):
        piece = pieces[slot][...] if given == 4 else pieces[0][slot * size : (slot + 1) * size]
        at = place(idx, slot, z_major)
        if not tail:
            outs[0][slot_rows(at, size), :] = piece.astype(F32)
        else:
            outs[4][slot_rows(at, tail), :] = piece[body:].astype(F32)
            for j in range(4):

                @pl.when(at == j)
                def _():
                    outs[j][...] = piece[:body].astype(F32)


def unpack(idx, z_major, tail, pieces):
    d = pieces[0].shape[1]
    total = sum(p.shape[0] for p in pieces)
    shapes = [(total // 4 - tail, d)] * 4 + [(4 * tail, d)] if tail else [(total, d)]
    return pl.pallas_call(
        partial(unpack_kernel, z_major, len(pieces), tail),
        out_shape=[jax.ShapeDtypeStruct(a, F32) for a in shapes],
        grid_spec=pltpu.PrefetchScalarGridSpec(
            num_scalar_prefetch=1,
            grid=(1,),
            in_specs=[whole(*p.shape) for p in pieces],
            out_specs=[whole(*a) for a in shapes],
        ),
        compiler_params=params(10),
        cost_estimate=cost(0.0),
        name="unpack",
    )(idx, *pieces)


def mix_kernel(order, v, r, out):
    for j, other in enumerate(order):
        out[j : j + 1, :] = v[j : j + 1, :] + r[other : other + 1, :]
    out[len(order) :, :] = v[len(order) :, :] + r[len(order) :, :]


def small(kernel, *arrays):
    return pl.pallas_call(
        kernel,
        out_shape=jax.ShapeDtypeStruct(arrays[0].shape, F32),
        compiler_params=params(4),
        cost_estimate=cost(0.5),
        name="small",
    )(*arrays)


def block(array, *index, rows=None, cols=None):
    (r, n_r), (c, n_c) = rows or (0, 1), cols or (0, 1)
    shape = (1,) * len(index) + (array.shape[-2] // n_r, array.shape[-1] // n_c)
    return array, shape, index + (r, c)


def add_up_kernel(sizes, idx, *refs):
    outs = refs[sum(sizes) :]
    col = 0
    for size in sizes:
        total = None
        for ref in refs[:size]:
            piece = ref[...]
            piece = piece.reshape(piece.shape[-2:]).astype(F32)
            total = piece if total is None else total + piece
        refs = refs[size:]
        cols = slice(col, col + total.shape[1])
        col += total.shape[1]
        n = outs[0].shape[0]
        for j, out in enumerate(outs):
            out[:, cols] = total[j * n : (j + 1) * n].astype(BF16)


def add_up(idx, pieces, *parts):
    blocks = [b for part in parts for b in part]
    rows = blocks[0][1][-2] // pieces
    cols = sum(part[0][1][-1] for part in parts)
    out = pl.pallas_call(
        partial(add_up_kernel, tuple(len(part) for part in parts)),
        out_shape=[jax.ShapeDtypeStruct((rows, cols), BF16)] * pieces,
        grid_spec=pltpu.PrefetchScalarGridSpec(
            num_scalar_prefetch=1,
            grid=(1,),
            in_specs=[
                pl.BlockSpec(b[1], partial(lambda at, g, s: at, b[2]), pipeline_mode=pl.Buffered(1))
                for b in blocks
            ],
            out_specs=[whole(rows, cols)] * pieces,
        ),
        compiler_params=params(12),
        cost_estimate=cost(0.25),
        name="add_up",
    )(idx, *(b[0] for b in blocks))
    return out if pieces > 1 else out[0]


def finish_kernel(idx, a, b, c, gm, out):
    total = a[...].astype(F32) + b[...].astype(F32) + c[...].astype(F32) + gm[...]
    out[...] = total.astype(BF16)


def finish(idx, a, b, c, gm):
    seq, d = a.shape
    part = pl.BlockSpec((seq // 4, d), lambda n, s: (n, 0))
    return pl.pallas_call(
        finish_kernel,
        out_shape=jax.ShapeDtypeStruct((seq, d), BF16),
        grid_spec=pltpu.PrefetchScalarGridSpec(
            num_scalar_prefetch=1, grid=(4,), in_specs=[part] * 4, out_specs=part
        ),
        compiler_params=params(8),
        cost_estimate=cost(0.0),
        name="finish",
    )(idx, a, b, c, gm)


def over(name, bit):
    size = lax.axis_size(name)
    pairs = [(i, i ^ bit) for i in range(size)]
    return lambda a: lax.ppermute(a, name, pairs)


class Order:
    def __init__(self):
        self.last = ()

    def then(self, a):
        return lax.optimization_barrier((a, self.last))[0]

    def done(self, out):
        self.last = (jax.tree.leaves(out)[-1],)
        return out

    def wait(self, *arrays):
        arrays = self.then(arrays)
        self.last = self.last + tuple(arrays)
        return arrays


def local(
    inputs, segment_ids, cotangent, query_weight, key_weight, value_weight, query_bias, value_bias,
    output_weight, output_bias, middle_gain, middle_shift, up_weight, up_bias, down_weight, down_bias,
    final_gain, final_shift,
):
    rows_here, seq = segment_ids.shape
    members = lax.axis_size("mp")
    assert members == 4 and rows_here == 4
    staged = lax.axis_size("dp") == 8
    me = lax.axis_index("mp")
    spot = lax.axis_index("dp")
    x_bit = jnp.bitwise_and(spot, 1) if staged else 0 * spot
    z_bit = jnp.bitwise_and(jnp.right_shift(spot, 1), 1) if staged else 0 * spot
    idx = jnp.stack([me, x_bit, z_bit]).astype(jnp.int32)
    core, y, both = over("mp", 1), over("mp", 2), over("mp", 3)
    x, z1, z2 = over("dp", 1), over("dp", 2), over("dp", 4)
    line = lambda v: v.reshape(1, -1)
    order = Order()
    then, done, wait = order.then, order.done, order.wait
    kernel = lambda f, *a: done(f(then(idx), *a))

    if staged:
        quarter = up_weight.shape[0] // 4
        at = (x_bit * 2 + z_bit) * quarter
        mine = [lax.dynamic_slice_in_dim(w, at, quarter, 0) for w in (up_weight, down_weight)]
        mine = done(mine)
        near_u, near_d = y(mine[0]), y(mine[1])
    u1, d1 = core(up_weight), core(down_weight)
    ub = line(up_bias)
    ub1, ub2 = core(ub), y(ub)

    weights = (query_weight.T, key_weight.T, value_weight.T, output_weight)
    fwd = (inputs, segment_ids) + weights + (line(query_bias), line(value_bias))
    *kept3, part3 = kernel(partial(attend_fwd, 3, 1), *fwd)
    from3 = core(part3)
    if staged:
        (near_u,) = wait(near_u)
        x_u, z_u = x(near_u), z1(near_u)
    *kept2, part2 = kernel(partial(attend_fwd, 2, 1), *fwd)
    if staged:
        (near_d,) = wait(near_d)
        x_d, z_d = x(near_d), z1(near_d)
    u1, d1, ub1, ub2 = wait(u1, d1, ub1, ub2)
    ub3 = core(ub2)
    other = y(done(part2 + then(from3)))
    if staged:
        x_u, z_u = wait(x_u, z_u)
        far_u = z1(x_u)
    *kept10, part1, part0 = kernel(partial(attend_fwd, 1, 2), *fwd)
    from1 = core(part1)
    if staged:
        z_d, x_d, ub3 = wait(z_d, x_d, ub3)
        far_d = x(z_d)
        (other,) = wait(other)
        far_u, far_d = wait(far_u, far_d)
        u2, d2 = kernel(join, near_u, z_u, x_u, far_u, near_d, z_d, x_d, far_d)
        u3, d3 = core(u2), core(d2)
    else:
        u2, u3, d2, d3 = y(up_weight), both(up_weight), y(down_weight), both(down_weight)
    us = (up_weight, u1, u2, u3)
    ds = (down_weight, d1, d2, d3)
    hidden, normed, inverse, low, act, slope = kernel(
        up, inputs, part0, from1, other, line(output_bias), line(middle_gain), line(middle_shift),
        us, (ub, ub1, ub2, ub3),
    )
    layer_out, grad_final, grad_low, vec_fin = kernel(
        down, act, ds, hidden, cotangent, line(down_bias), line(final_gain), line(final_shift)
    )

    gd31, first_d, second_d = kernel(partial(outer, True, False, False), grad_low, act)
    rd = core(gd31)
    gp, grad_mid, mid0, vec = done(
        back(grad_low, slope, ds, us, grad_final, normed, inverse, then(line(middle_gain)), vec_fin)
    )
    mid2, mid1 = y(mid0), core(mid0)
    vec_core = core(vec)
    half = first_d.shape[1]
    rd = then(rd)
    second_d = done(second_d + rd[:, half:])
    got_d = x(second_d) if staged else None
    gu31, far_l, near_l1, near_l2, first_r, second_r = kernel(
        partial(outer, False, True, True), low, gp
    )
    ru = core(gu31)
    in0, in1, *before = kernel(partial(attend_bwd, 0, False), inputs, (mid0, mid1), kept10, *weights)
    from_in1 = core(in1)
    n = far_l.shape[1]
    ru = then(ru)
    second_r = second_r + ru[:, half:, n:]
    far_l = done(far_l + ru[0, :, :n])
    got_r = z1(second_r) if staged else None
    got_l = y(far_l)
    (mid2,) = wait(mid2)
    mid3 = core(mid2)
    vec = done(small(partial(mix_kernel, (1, 0, 3, 2)), vec, then(vec_core)))
    vec_y = y(vec)
    in2, *before = kernel(partial(attend_bwd, 2, False), inputs, (mid2,), kept2, *weights, before)
    (vec_y,) = wait(vec_y)
    in3, first_a, second_a = kernel(
        partial(attend_bwd, 3, True), inputs, (mid3,), kept3, *weights, before, (vec, vec_y)
    )
    width = query_bias.shape[0]

    if staged:
        top = dict(rows=(0, 2))
        left, right = dict(cols=(0, 2)), dict(cols=(1, 2))
        got_a = x(second_a)
        from_in3 = core(in3)
        more_d = y(
            kernel(add_up, 1, [block(first_d, 0), block(rd, 0, **top), block(got_d, 0)])
        )
        more_r = y(
            kernel(add_up, 1, [block(first_r, 0), block(ru, 0, **top, **right), block(got_r, 0)])
        )
        more_l = z1(
            kernel(
                add_up, 1,
                [block(near_l2), block(ru, 1, rows=(1, 2), **left), block(got_l, rows=(1, 2))],
            )
        )
        keep_a, send_a = kernel(add_up, 2, [block(first_a), block(got_a)])
        got_a = z1(send_a)
        keep_d, send_d = kernel(
            add_up, 2, [block(first_d, 1), block(rd, 1, **top), block(got_d, 1), block(more_d)]
        )
        got_d = z1(send_d)
        keep_u, send_u = kernel(
            add_up, 2,
            [block(near_l1), block(ru, 1, **top, **left), block(got_l, **top), block(more_l)],
            [block(first_r, 1), block(ru, 1, **top, **right), block(got_r, 1), block(more_r)],
        )
        got_u = x(send_u)
        from_in2 = y(kernel(add_up, 1, [block(in2), block(from_in3)]))
        s_a = kernel(add_up, 1, [block(keep_a), block(got_a)])
        got_a = z2(s_a)
        s_d = kernel(add_up, 1, [block(keep_d), block(got_d)])
        got_d = z2(s_d)
        s_u = kernel(add_up, 1, [block(keep_u), block(got_u)])
        got_u = z2(s_u)
        s_a = kernel(add_up, 1, [block(s_a), block(got_a)])
        q_a, p_a = z1(s_a), x(s_a)
        input_grad = kernel(finish, in0, from_in1, from_in2, grad_mid)
        (q_a,) = wait(q_a)
        r_a = x(q_a)
        s_d = kernel(add_up, 1, [block(s_d), block(got_d)])
        q_d, p_d = z1(s_d), x(s_d)
        s_u = kernel(add_up, 1, [block(s_u), block(got_u)])
        q_u, p_u = x(s_u), z1(s_u)
        (q_d,) = wait(q_d)
        r_d = x(q_d)
        grad_q, grad_k, grad_v, grad_o, vecs = kernel(unpack, False, TAIL, (s_a, q_a, p_a, r_a))
        (q_u,) = wait(q_u)
        r_u = z1(q_u)
        (grad_down,) = kernel(unpack, False, 0, (s_d, q_d, p_d, r_d))
        (grad_up,) = kernel(unpack, True, 0, (s_u, q_u, p_u, r_u))
    else:
        input_grad = finish(idx, in0, from_in1, y(in2 + core(in3)), grad_mid)
        td = jnp.concatenate([first_d[1] + rd[1, :half], second_d[1]]) + y(
            jnp.concatenate([first_d[0] + rd[0, :half], second_d[0]])
        )
        tl = jnp.concatenate([near_l1, near_l2]) + ru[1, :, :n] + got_l
        tr = jnp.concatenate([first_r[1] + ru[1, :half, n:], second_r[1]]) + y(
            jnp.concatenate([first_r[0] + ru[0, :half, n:], second_r[0]])
        )
        tu = jnp.concatenate([tl, tr], axis=1)
        ta = jnp.concatenate([first_a, second_a])
        td, tu, ta = lax.psum((td, tu, ta), "dp")
        (grad_down,) = unpack(idx, False, 0, (td,))
        (grad_up,) = unpack(idx, True, 0, (tu,))
        grad_q, grad_k, grad_v, grad_o, vecs = unpack(idx, False, TAIL, (ta,))

    bias_up, gain_mid, shift_mid, bias_out, gain_fin, shift_fin, bias_down, bias_q, bias_v = (
        vecs[TAIL * (j // 3) + j % 3] for j in range(9)
    )
    return (
        layer_out, input_grad, grad_q.T, grad_k.T, grad_v.T, bias_q[:width], bias_v[:width], grad_o,
        bias_out, gain_mid, shift_mid, grad_up, bias_up, grad_down, bias_down, gain_fin, shift_fin,
    )


def solution(mesh):
    tokens = P("dp", None)
    columns, units, stacked, full = P(None, "mp"), P("mp"), P("mp", None), P()
    shared = P(("dp", "mp"), None)
    placed = (
        tokens, tokens, tokens, columns, columns, columns, units, units, stacked, full, full, full,
        columns, units, stacked, full, full, full,
    )
    given = (
        shared, shared, columns, columns, columns, units, units, stacked, full, full, full,
        columns, units, stacked, full, full, full,
    )
    return jax.shard_map(local, mesh=mesh, in_specs=placed, out_specs=given, check_vma=False)
```

```python
from functools import partial

import jax
import jax.numpy as jnp
from jax import lax
from jax.experimental import pallas as pl
from jax.experimental.pallas import tpu as pltpu
from jax.sharding import PartitionSpec as P

HEAD = 64
BAND = 128
EPSILON = 1e-12
ROOT_HALF = 0.7071067811865476
INV_ROOT_TAU = 0.3989422804014327
MASKED = -1e30
TAIL = 8
F32 = jnp.float32
BF16 = jnp.bfloat16
MIB = 1024 * 1024
SCALE = 4.0


def nn(a, b):
    return lax.dot_general(a, b, (((1,), (0,)), ((), ())), preferred_element_type=F32)


def nt(a, b):
    return lax.dot_general(a, b, (((1,), (1,)), ((), ())), preferred_element_type=F32)


def tn(a, b):
    return lax.dot_general(a, b, (((0,), (0,)), ((), ())), preferred_element_type=F32)


def window(block, seq):
    lo = max(block * BAND - BAND, 0)
    hi = min(block * BAND + 2 * BAND, seq)
    return lo, hi


def params(mib):
    return pltpu.CompilerParams(vmem_limit_bytes=mib * MIB)


def cost(us):
    return pl.CostEstimate(
        flops=int(us * SCALE * 1.15e9), bytes_accessed=int(us * SCALE * 3.6e6), transcendentals=0
    )


def whole(*shape):
    return pl.BlockSpec(shape, lambda *_: (0,) * len(shape), pipeline_mode=pl.Buffered(1))


def held(*shape):
    return pl.BlockSpec(shape, lambda *_: (0,) * len(shape))


def rows_of_heads(a):
    zero = jnp.zeros((HEAD, a.shape[1]), a.dtype)
    tiles = []
    for h in range(a.shape[0] // HEAD):
        mine = a[h * HEAD : (h + 1) * HEAD]
        if h % 2 == 0 and (h + 1) * HEAD == a.shape[0]:
            tiles.append(mine)
        else:
            tiles.append(jnp.concatenate([mine, zero] if h % 2 == 0 else [zero, mine], axis=0))
    return tiles


def tiles_of_heads(a):
    width = a.shape[1]
    return [a[:, h // 2 * 128 : min(h // 2 * 128 + 128, width)] for h in range(width // HEAD)]


def columns_of_heads(a):
    masked = []
    for h, tile in enumerate(tiles_of_heads(a)):
        if tile.shape[1] == HEAD:
            masked.append(tile)
        else:
            lane = lax.broadcasted_iota(jnp.int32, tile.shape, 1)
            masked.append(jnp.where((lane < HEAD) == (h % 2 == 0), tile, jnp.zeros_like(tile)))
    return masked


def store_tiles(ref, rows, per_head, scale=None):
    for at in range(0, len(per_head), 2):
        total = per_head[at] if at + 1 == len(per_head) else per_head[at] + per_head[at + 1]
        if scale is not None:
            total = total * scale
        lo = at * HEAD
        ref[rows, lo : lo + total.shape[1]] = total.astype(ref.dtype)


def attend_fwd_kernel(base, idx, x_ref, seg_ref, wq, wk, wv, wo, qb, vb,
                      q_ref, k_ref, v_ref, p_ref, ctx_ref, *parts):
    step = pl.program_id(0)
    seq = x_ref.shape[0]
    row = jnp.bitwise_xor(idx[0], base - step)
    x = x_ref[...]
    q = ((nt(x, wq[...]) + qb[...]).astype(BF16) * (HEAD**-0.5)).astype(BF16)
    k_t = nt(wk[...], x).astype(BF16)
    v = (nt(x, wv[...]) + vb[...]).astype(BF16)
    q_ref[0] = jnp.transpose(q)
    k_ref[0] = jnp.transpose(k_t)
    v_ref[0] = jnp.transpose(v)
    q_tiles, k_rows, v_cols = tiles_of_heads(q), rows_of_heads(k_t), columns_of_heads(v)
    heads = range(len(q_tiles))
    seg_row = seg_ref[pl.ds(row, 1), :]
    for i in range(seq // BAND):
        lo, hi = window(i, seq)
        rows = slice(i * BAND, (i + 1) * BAND)
        seg_k = jnp.broadcast_to(seg_row[:, lo:hi], (BAND, hi - lo))
        seg_q = jnp.transpose(jnp.broadcast_to(seg_row[:, rows], (BAND, BAND)))
        same = jnp.concatenate([seg_q] * ((hi - lo) // BAND), axis=1) == seg_k
        scores = [jnp.where(same, nn(q_tiles[h][rows], k_rows[h][:, lo:hi]), MASKED) for h in heads]
        tops = [jnp.max(a, axis=-1, keepdims=True) for a in scores]
        expos = [jnp.exp(a - m) for a, m in zip(scores, tops)]
        scales = [1.0 / jnp.sum(e, axis=-1, keepdims=True) for e in expos]
        probs = [(e * t).astype(BF16) for e, t in zip(expos, scales)]
        for h in heads:
            p_ref[0, h, rows, 0 : hi - lo] = probs[h]
        store_tiles(ctx_ref.at[0], rows, [nn(probs[h], v_cols[h][lo:hi]) for h in heads])
    part = nn(ctx_ref[0], wo[...]).astype(BF16)
    for j, ref in enumerate(parts):

        @pl.when(step == j)
        def _():
            ref[...] = part


def attend_fwd(base, count, idx, x, seg, wq, wk, wv, wo, qb, vb):
    seq = seg.shape[1]
    width, d = wq.shape
    heads = width // HEAD
    slot = lambda g, s: (g, 0, 0)
    natural = pl.BlockSpec((1, seq, width), slot)
    turned = pl.BlockSpec((1, width, seq), slot)
    saved = (
        jax.ShapeDtypeStruct((count, width, seq), BF16),
        jax.ShapeDtypeStruct((count, seq, width), BF16),
        jax.ShapeDtypeStruct((count, width, seq), BF16),
        jax.ShapeDtypeStruct((count, heads, seq, 3 * BAND), BF16),
        jax.ShapeDtypeStruct((count, seq, width), BF16),
    )
    args = (idx, x, seg, wq, wk, wv, wo, qb, vb)
    specs = [
        pl.BlockSpec((seq, d), lambda g, s: (jnp.bitwise_xor(s[0], base - g), 0)),
        whole(*seg.shape),
        whole(width, d),
        whole(width, d),
        whole(width, d),
        whole(width, d),
        whole(1, width),
        whole(1, width),
    ]
    return pl.pallas_call(
        partial(attend_fwd_kernel, base),
        out_shape=saved + (jax.ShapeDtypeStruct((seq, d), BF16),) * count,
        grid_spec=pltpu.PrefetchScalarGridSpec(
            num_scalar_prefetch=1,
            grid=(count,),
            in_specs=specs,
            out_specs=[
                turned,
                natural,
                turned,
                pl.BlockSpec((1, heads, seq, 3 * BAND), lambda g, s: (g, 0, 0, 0)),
                natural,
            ]
            + [held(seq, d)] * count,
        ),
        compiler_params=params(60 if base == 3 else 24),
        cost_estimate=cost(3.2 * count),
        name="attend_fwd",
    )(*args)


def gelu_parts(v):
    half = 0.5 * (1.0 + lax.erf(v * ROOT_HALF))
    return v * half, half + v * jnp.exp(-0.5 * v * v) * INV_ROOT_TAU


def by_rows(total, step, body, carry):
    def one(i, c):
        return body(pl.ds(pl.multiple_of(i * step, step), step), c)

    return lax.fori_loop(0, total // step, one, carry, unroll=2)


def fold(a):
    return jnp.sum(a.reshape(a.shape[0] // 8, 8, a.shape[1]), axis=0)


def up_kernel(
    idx, x_ref, pa, pb, pc, ob, gain, shift, u0, u1, u2, u3, b0, b1, b2, b3,
    hid, nrm, inv, low, act, slope,
):
    @pl.when(pl.program_id(0) == 0)
    def _():
        def body(rows, carry):
            middle = (
                pa[rows, :].astype(F32)
                + pb[rows, :].astype(F32)
                + pc[rows, :].astype(F32)
                + ob[...]
                + x_ref[rows, :].astype(F32)
            )
            centred = middle - jnp.mean(middle, axis=-1, keepdims=True)
            r = lax.rsqrt(jnp.mean(centred * centred, axis=-1, keepdims=True) + EPSILON)
            normed = centred * r
            hidden = normed * gain[...] + shift[...]
            nrm[rows, :] = normed
            inv[rows, :] = jnp.broadcast_to(r, (r.shape[0], 128))
            hid[rows, :] = hidden
            low[rows, :] = hidden.astype(BF16)
            return carry

        by_rows(low.shape[0], 64, body, 0)

    for r, (u, b) in enumerate(((u0, b0), (u1, b1), (u2, b2), (u3, b3))):
        value, deriv = gelu_parts(nn(low[...], u[...]) + b[...])
        act[r] = value.astype(BF16)
        slope[r] = deriv.astype(BF16)


def up(idx, x, own, recv, other, ob, gain, shift, us, bs):
    seq, d = other.shape
    units = us[0].shape[1]
    tile = 256
    row = pl.BlockSpec((seq, d), lambda n, s: (s[0], 0), pipeline_mode=pl.Buffered(1))
    wide = pl.BlockSpec((d, tile), lambda n, s: (0, n))
    bias = pl.BlockSpec((1, tile), lambda n, s: (0, n))
    out = pl.BlockSpec((4, seq, tile), lambda n, s: (0, 0, n))
    return pl.pallas_call(
        up_kernel,
        out_shape=(
            jax.ShapeDtypeStruct((seq, d), F32),
            jax.ShapeDtypeStruct((seq, d), F32),
            jax.ShapeDtypeStruct((seq, 128), F32),
            jax.ShapeDtypeStruct((seq, d), BF16),
            jax.ShapeDtypeStruct((4, seq, units), BF16),
            jax.ShapeDtypeStruct((4, seq, units), BF16),
        ),
        grid_spec=pltpu.PrefetchScalarGridSpec(
            num_scalar_prefetch=1,
            grid=(units // tile,),
            in_specs=[row] + [whole(seq, d)] * 3 + [whole(1, d)] * 3 + [wide] * 4 + [bias] * 4,
            out_specs=[held(seq, d), held(seq, d), held(seq, 128), held(seq, d), out, out],
        ),
        compiler_params=params(28),
        cost_estimate=cost(7.3),
        name="up",
    )(idx, x, own, recv, other, ob, gain, shift, *us, *bs)


def down_kernel(idx, act, d0, d1, d2, d3, hid, cot, db, gain, shift, out_ref, gf_ref, gl_ref, vec, acc):
    step = pl.program_id(0)
    total = None
    for r, w in enumerate((d0, d1, d2, d3)):
        term = nn(act[r], w[...])
        total = term if total is None else total + term
    acc[step] = total

    @pl.when(step == pl.num_programs(0) - 1)
    def _():
        def body(rows, carry):
            parts = [acc[n, rows, :] for n in range(acc.shape[0])]
            final = jnp.concatenate(parts, axis=1) + db[...] + hid[rows, :]
            centred = final - jnp.mean(final, axis=-1, keepdims=True)
            r = lax.rsqrt(jnp.mean(centred * centred, axis=-1, keepdims=True) + EPSILON)
            normed = centred * r
            out_ref[rows, :] = (normed * gain[...] + shift[...]).astype(BF16)
            cv = cot[rows, :].astype(F32)
            c = cv * gain[...]
            grad = r * (
                c
                - jnp.mean(c, axis=-1, keepdims=True)
                - normed * jnp.mean(c * normed, axis=-1, keepdims=True)
            )
            gf_ref[rows, :] = grad
            gl_ref[rows, :] = grad.astype(BF16)
            return tuple(a + b for a, b in zip(carry, (fold(cv * normed), fold(cv), fold(grad))))

        zero = jnp.zeros((8, hid.shape[1]), F32)
        sums = by_rows(hid.shape[0], 64, body, (zero, zero, zero))
        vec[...] = jnp.zeros_like(vec)
        for j, total in enumerate(sums):
            vec[j : j + 1, :] = jnp.sum(total, axis=0, keepdims=True)


def down(idx, act, ds, hid, cot, db, gain, shift):
    seq, d = hid.shape
    units = act.shape[2]
    tile = 256
    wide = pl.BlockSpec((units, tile), lambda n, s: (0, n))
    row = pl.BlockSpec((seq, d), lambda n, s: (s[0], 0), pipeline_mode=pl.Buffered(1))
    return pl.pallas_call(
        down_kernel,
        out_shape=(
            jax.ShapeDtypeStruct((seq, d), BF16),
            jax.ShapeDtypeStruct((seq, d), F32),
            jax.ShapeDtypeStruct((seq, d), BF16),
            jax.ShapeDtypeStruct((8, d), F32),
        ),
        grid_spec=pltpu.PrefetchScalarGridSpec(
            num_scalar_prefetch=1,
            grid=(d // tile,),
            in_specs=[whole(4, seq, units)] + [wide] * 4 + [whole(seq, d), row] + [whole(1, d)] * 3,
            out_specs=[held(seq, d), held(seq, d), held(seq, d), held(8, d)],
            scratch_shapes=[pltpu.VMEM((d // tile, seq, tile), F32)],
        ),
        compiler_params=params(24),
        cost_estimate=cost(6.2),
        name="down",
    )(idx, act, *ds, hid, cot, db, gain, shift)


def back_kernel(
    gl, slope, d0, d1, d2, d3, u0, u1, u2, u3, gf, nrm, inv, gain, vecf, gp, gm_ref, gml_ref, vec, acc
):
    step = pl.program_id(0)
    tile = slope.shape[2]
    total = None
    for r, (w_d, w_u) in enumerate(((d0, u0), (d1, u1), (d2, u2), (d3, u3))):
        pre = (nt(gl[...], w_d[...]) * slope[r].astype(F32)).astype(BF16)
        gp[r] = pre
        sums = jnp.sum(pre.astype(F32), axis=0, keepdims=True)
        vec[r : r + 1, pl.ds(pl.multiple_of(step * tile, tile), tile)] = sums
        term = nt(pre, w_u[...])
        total = term if total is None else total + term

    @pl.when(step == 0)
    def _():
        acc[...] = total

    @pl.when(step > 0)
    def _():
        acc[...] += total

    @pl.when(step == pl.num_programs(0) - 1)
    def _():
        def body(rows, carry):
            grad = acc[rows, :] + gf[rows, :]
            normed = nrm[rows, :]
            c = grad * gain[...]
            gm = inv[rows, 0:1] * (
                c
                - jnp.mean(c, axis=-1, keepdims=True)
                - normed * jnp.mean(c * normed, axis=-1, keepdims=True)
            )
            gm_ref[rows, :] = gm
            gml_ref[rows, :] = gm.astype(BF16)
            return tuple(a + b for a, b in zip(carry, (fold(grad * normed), fold(grad), fold(gm))))

        zero = jnp.zeros((8, gf.shape[1]), F32)
        sums = by_rows(gf.shape[0], 64, body, (zero, zero, zero))
        for j, total in enumerate(sums):
            vec[4 + j : 5 + j, :] = jnp.sum(total, axis=0, keepdims=True)
        vec[7:10, :] = vecf[0:3, :]
        vec[10:16, :] = jnp.zeros((6, gf.shape[1]), F32)


def back(gl, slope, ds, us, gf, nrm, inv, gain, vecf):
    seq, d = gf.shape
    units = slope.shape[2]
    tile = 256
    tall = pl.BlockSpec((4, seq, tile), lambda n: (0, 0, n))
    w_d = pl.BlockSpec((tile, d), lambda n: (n, 0))
    w_u = pl.BlockSpec((d, tile), lambda n: (0, n))
    return pl.pallas_call(
        back_kernel,
        out_shape=(
            jax.ShapeDtypeStruct((4, seq, units), BF16),
            jax.ShapeDtypeStruct((seq, d), F32),
            jax.ShapeDtypeStruct((seq, d), BF16),
            jax.ShapeDtypeStruct((16, d), F32),
        ),
        grid=(units // tile,),
        in_specs=[whole(seq, d), tall]
        + [w_d] * 4
        + [w_u] * 4
        + [whole(seq, d), whole(seq, d), whole(seq, 128), whole(1, d), whole(8, d)],
        out_specs=[tall, held(seq, d), held(seq, d), held(16, d)],
        scratch_shapes=[pltpu.VMEM((seq, d), F32)],
        compiler_params=params(28),
        cost_estimate=cost(10.8),
        name="back",
    )(gl, slope, *ds, *us, gf, nrm, inv, gain, vecf)


def place(idx, e, z_major=False):
    first, second = (idx[2], idx[1]) if z_major else (idx[1], idx[2])
    return jnp.bitwise_xor(e // 2, first) * 2 + jnp.bitwise_xor(e % 2, second)


def spread(idx, value, put, z_major=False):
    size = value.shape[0] // 4
    for e in range(4):
        put(place(idx, e, z_major), size, value[e * size : (e + 1) * size])


def slot_rows(slot, size):
    return pl.ds(pl.multiple_of(slot * size, 8), size)


def put_halves(first, second):
    def put(slot, size, piece):
        @pl.when(slot < 2)
        def _():
            first[slot_rows(slot, size), :] = piece.astype(BF16)

        @pl.when(slot >= 2)
        def _():
            second[slot_rows(slot - 2, size), :] = piece.astype(BF16)

    return put


def outer_kernel(flip, z_major, halves, idx, left, varied, out, *kept):
    step = pl.program_id(0)
    value = tn(varied[0], left[...]) if flip else tn(left[...], varied[0])

    def whole_to(ref):
        def put(slot, size, piece):
            ref[slot_rows(slot, size), :] = piece.astype(BF16)

        return put

    @pl.when(step < 2)
    def _():
        spread(idx, value, whole_to(out.at[step]), z_major)

    if not halves:
        first, second = kept

        @pl.when(step >= 2)
        def _():
            spread(idx, value, put_halves(first.at[step - 2], second.at[step - 2]), z_major)

    else:
        far_left, near_first, near_second, first, second = kept
        n = far_left.shape[1]

        @pl.when(step >= 2)
        def _():
            spread(idx, value[:, n:], put_halves(first.at[step - 2], second.at[step - 2]), z_major)

        @pl.when(step == 2)
        def _():
            spread(idx, value[:, :n], whole_to(far_left), z_major)

        @pl.when(step == 3)
        def _():
            spread(idx, value[:, :n], put_halves(near_first, near_second), z_major)


def outer(flip, z_major, halves, idx, left, varied):
    seq, d = left.shape
    units = varied.shape[2]
    rows, cols = (units, d) if flip else (d, units)
    shapes = [(2, rows, cols)]
    if halves:
        cols = cols // 2
        shapes += [(rows, cols), (rows // 2, cols), (rows // 2, cols)]
    shapes += [(2, rows // 2, cols), (2, rows // 2, cols)]
    member = lambda g, s: (jnp.where(g < 2, 3 - 2 * g, 6 - 2 * g), 0, 0)
    return pl.pallas_call(
        partial(outer_kernel, flip, z_major, halves),
        out_shape=[jax.ShapeDtypeStruct(a, BF16) for a in shapes],
        grid_spec=pltpu.PrefetchScalarGridSpec(
            num_scalar_prefetch=1,
            grid=(4,),
            in_specs=[whole(seq, d), pl.BlockSpec((1, seq, units), member)],
            out_specs=[whole(*a) for a in shapes],
        ),
        compiler_params=params(20),
        cost_estimate=cost(5.5),
        name="outer",
    )(idx, left, varied)


def attend_bwd_kernel(count, later, last, idx, x_ref, *rest):
    gmls, rest = rest[:count], rest[count:]
    q_ref, k_ref, v_ref, p_ref, ctx_ref, wq, wk, wv, wo = rest[:9]
    rest = rest[9:]
    if later:
        before, vec_before = rest[:2]
        rest = rest[2:]
    if last:
        shared, shared_y = rest[:2]
        rest = rest[2:]
    parts, rest = rest[:count], rest[count:]
    if last:
        first, second, tail, vec, grads, gq_s, gk_s, gv_s = rest
    else:
        grads, vec, gq_s, gk_s, gv_s = rest
    step = pl.program_id(0)
    seq = x_ref.shape[0]
    width = wq.shape[0]
    blocks = seq // BAND

    @pl.when(step == 0)
    def _():
        if later:
            grads[...] = before[...]
            vec[...] = vec_before[...]
        else:
            grads[...] = jnp.zeros_like(grads)
            vec[...] = jnp.zeros_like(vec)

    gml = gmls[0][...] if count == 1 else jnp.where(step == 0, gmls[0][...], gmls[1][...])
    x, ctx, q_t, k = x_ref[...], ctx_ref[0], q_ref[0], k_ref[0]
    gctx = nt(gml, wo[...]).astype(BF16)
    gctx_t = jnp.transpose(gctx)
    g_tiles, v_rows, k_cols = tiles_of_heads(gctx), rows_of_heads(v_ref[0]), columns_of_heads(k)
    heads = range(len(g_tiles))
    gk = [[None] * blocks for _ in heads]
    gv = [[None] * blocks for _ in heads]
    for i in range(blocks):
        lo, hi = window(i, seq)
        rows = slice(i * BAND, (i + 1) * BAND)
        probs_low = [p_ref[0, h, rows, 0 : hi - lo] for h in heads]
        gprobs = [nn(g_tiles[h][rows], v_rows[h][:, lo:hi]) for h in heads]
        probs = [p.astype(F32) for p in probs_low]
        dots = [jnp.sum(a * b, axis=-1, keepdims=True) for a, b in zip(gprobs, probs)]
        gscores = [(p * (g - t)).astype(BF16) for g, p, t in zip(gprobs, probs, dots)]
        store_tiles(gq_s, rows, [nn(gscores[h], k_cols[h][lo:hi]) for h in heads], HEAD**-0.5)
        for h in heads:
            mine = slice(h * HEAD, (h + 1) * HEAD)
            gk_i = nn(q_t[mine, rows], gscores[h])
            gv_i = nn(gctx_t[mine, rows], probs_low[h])
            for j in range(lo // BAND, hi // BAND):
                at = slice(j * BAND - lo, (j + 1) * BAND - lo)
                gk[h][j] = gk_i[:, at] if gk[h][j] is None else gk[h][j] + gk_i[:, at]
                gv[h][j] = gv_i[:, at] if gv[h][j] is None else gv[h][j] + gv_i[:, at]
    for h in heads:
        mine = slice(h * HEAD, (h + 1) * HEAD)
        for j in range(blocks):
            cols = slice(j * BAND, (j + 1) * BAND)
            gk_s[mine, cols] = gk[h][j].astype(BF16)
            gv_s[mine, cols] = gv[h][j].astype(BF16)
    gq, gk_t, gv_t = gq_s[...], gk_s[...], gv_s[...]
    gv_n = jnp.transpose(gv_t)
    grads[0:width] += tn(gq, x)
    grads[width : 2 * width] += nn(gk_t, x)
    grads[2 * width : 3 * width] += nn(gv_t, x)
    grads[3 * width : 4 * width] += tn(ctx, gml)
    vec[0:1, 0:width] += jnp.sum(gq.astype(F32), axis=0, keepdims=True)
    vec[1:2, 0:width] += jnp.sum(gv_n.astype(F32), axis=0, keepdims=True)
    part = (nn(gq, wq[...]) + nn(jnp.transpose(gk_t), wk[...]) + nn(gv_n, wv[...])).astype(BF16)

    for j, ref in enumerate(parts):

        @pl.when(step == j)
        def _():
            ref[...] = part

    if last:

        @pl.when(step == count - 1)
        def _():
            tail[...] = jnp.zeros_like(tail)
            tail[0:1, :] = shared[0:1, :] + shared_y[2:3, :]
            for j in range(6):
                at = TAIL * ((j + 1) // 3) + (j + 1) % 3
                tail[at : at + 1, :] = shared[4 + j : 5 + j, :] + shared_y[4 + j : 5 + j, :]
            tail[2 * TAIL + 1 : 2 * TAIL + 3, :] = vec[0:2, :]
            for e in range(4):
                body = grads[e * width : (e + 1) * width]
                both = jnp.concatenate([body, tail[e * TAIL : (e + 1) * TAIL]], axis=0)
                put_halves(first, second)(place(idx, e), width + TAIL, both)


def attend_bwd(base, last, idx, x, gmls, kept, wq, wk, wv, wo, before=None, shared=()):
    q, k, v, p, ctx = kept
    width, d = wq.shape
    seq = gmls[0].shape[0]
    heads = width // HEAD
    count = len(gmls)
    later = before is not None
    slot = lambda g, s: (count - 1 - g, 0, 0)
    natural = pl.BlockSpec((1, seq, width), slot)
    turned = pl.BlockSpec((1, width, seq), slot)
    specs = [
        pl.BlockSpec((seq, d), lambda g, s: (jnp.bitwise_xor(s[0], base + g), 0)),
    ] + [whole(seq, d)] * count + [
        turned,
        natural,
        turned,
        pl.BlockSpec((1, heads, seq, 3 * BAND), lambda g, s: (count - 1 - g, 0, 0, 0)),
        natural,
    ] + [whole(width, d)] * 4
    args = (idx, x, *gmls, q, k, v, p, ctx, wq, wk, wv, wo)
    part = jax.ShapeDtypeStruct((seq, d), BF16)
    small = jax.ShapeDtypeStruct((8, d), F32)
    scratch = [
        pltpu.VMEM((seq, width), BF16),
        pltpu.VMEM((width, seq), BF16),
        pltpu.VMEM((width, seq), BF16),
    ]
    if later:
        specs += [whole(4 * width, d), whole(8, d)]
        args += tuple(before)
    if last:
        specs += [whole(16, d)] * 2
        args += tuple(shared)
        half = 2 * (width + TAIL)
        shapes = (part,) * count + (jax.ShapeDtypeStruct((half, d), BF16),) * 2
        outs = [held(seq, d)] * count + [held(half, d)] * 2
        scratch = [
            pltpu.VMEM((4 * TAIL, d), F32), pltpu.VMEM((8, d), F32), pltpu.VMEM((4 * width, d), F32)
        ] + scratch
    else:
        shapes = (part,) * count + (jax.ShapeDtypeStruct((4 * width, d), F32), small)
        outs = [held(seq, d)] * count + [held(4 * width, d), held(8, d)]
    return pl.pallas_call(
        partial(attend_bwd_kernel, count, later, last),
        out_shape=shapes,
        grid_spec=pltpu.PrefetchScalarGridSpec(
            num_scalar_prefetch=1, grid=(count,), in_specs=specs, out_specs=outs, scratch_shapes=scratch
        ),
        compiler_params=params(28),
        cost_estimate=cost(5.0 if later else 10.0),
        name="attend_bwd",
    )(*args)


def join_kernel(idx, *refs):
    pieces, outs = refs[:-2], refs[-2:]
    rows = pieces[0].shape[0]
    for j, piece in enumerate(pieces):
        at = place(idx, j % 4)
        outs[j // 4][slot_rows(at, rows), :] = piece[...]


def join(idx, *pieces):
    rows, d = pieces[0].shape
    return pl.pallas_call(
        join_kernel,
        out_shape=[jax.ShapeDtypeStruct((4 * rows, d), BF16)] * 2,
        grid_spec=pltpu.PrefetchScalarGridSpec(
            num_scalar_prefetch=1,
            grid=(1,),
            in_specs=[whole(rows, d)] * 8,
            out_specs=[whole(4 * rows, d)] * 2,
        ),
        compiler_params=params(8),
        cost_estimate=cost(1.0),
        name="join",
    )(idx, *pieces)


def unpack_kernel(z_major, given, tail, idx, *refs):
    pieces, outs = refs[:given], refs[given:]
    size = pieces[0].shape[0] * given // 4
    body = size - tail
    for slot in range(4):
        piece = pieces[slot][...] if given == 4 else pieces[0][slot * size : (slot + 1) * size]
        at = place(idx, slot, z_major)
        if not tail:
            outs[0][slot_rows(at, size), :] = piece.astype(F32)
        else:
            outs[4][slot_rows(at, tail), :] = piece[body:].astype(F32)
            for j in range(4):

                @pl.when(at == j)
                def _():
                    outs[j][...] = piece[:body].astype(F32)


def unpack(idx, z_major, tail, pieces):
    d = pieces[0].shape[1]
    total = sum(p.shape[0] for p in pieces)
    shapes = [(total // 4 - tail, d)] * 4 + [(4 * tail, d)] if tail else [(total, d)]
    return pl.pallas_call(
        partial(unpack_kernel, z_major, len(pieces), tail),
        out_shape=[jax.ShapeDtypeStruct(a, F32) for a in shapes],
        grid_spec=pltpu.PrefetchScalarGridSpec(
            num_scalar_prefetch=1,
            grid=(1,),
            in_specs=[whole(*p.shape) for p in pieces],
            out_specs=[whole(*a) for a in shapes],
        ),
        compiler_params=params(10),
        cost_estimate=cost(0.0),
        name="unpack",
    )(idx, *pieces)


def mix_kernel(order, v, r, out):
    for j, other in enumerate(order):
        out[j : j + 1, :] = v[j : j + 1, :] + r[other : other + 1, :]
    out[len(order) :, :] = v[len(order) :, :] + r[len(order) :, :]


def small(kernel, *arrays):
    return pl.pallas_call(
        kernel,
        out_shape=jax.ShapeDtypeStruct(arrays[0].shape, F32),
        compiler_params=params(4),
        cost_estimate=cost(0.5),
        name="small",
    )(*arrays)


def block(array, *index, rows=None, cols=None):
    (r, n_r), (c, n_c) = rows or (0, 1), cols or (0, 1)
    shape = (1,) * len(index) + (array.shape[-2] // n_r, array.shape[-1] // n_c)
    return array, shape, index + (r, c)


def add_up_kernel(sizes, idx, *refs):
    outs = refs[sum(sizes) :]
    col = 0
    for size in sizes:
        total = None
        for ref in refs[:size]:
            piece = ref[...]
            piece = piece.reshape(piece.shape[-2:]).astype(F32)
            total = piece if total is None else total + piece
        refs = refs[size:]
        cols = slice(col, col + total.shape[1])
        col += total.shape[1]
        n = outs[0].shape[0]
        for j, out in enumerate(outs):
            out[:, cols] = total[j * n : (j + 1) * n].astype(BF16)


def add_up(idx, pieces, *parts):
    blocks = [b for part in parts for b in part]
    rows = blocks[0][1][-2] // pieces
    cols = sum(part[0][1][-1] for part in parts)
    out = pl.pallas_call(
        partial(add_up_kernel, tuple(len(part) for part in parts)),
        out_shape=[jax.ShapeDtypeStruct((rows, cols), BF16)] * pieces,
        grid_spec=pltpu.PrefetchScalarGridSpec(
            num_scalar_prefetch=1,
            grid=(1,),
            in_specs=[
                pl.BlockSpec(b[1], partial(lambda at, g, s: at, b[2]), pipeline_mode=pl.Buffered(1))
                for b in blocks
            ],
            out_specs=[whole(rows, cols)] * pieces,
        ),
        compiler_params=params(12),
        cost_estimate=cost(0.02),
        name="add_up",
    )(idx, *(b[0] for b in blocks))
    return out if pieces > 1 else out[0]


def finish_kernel(idx, a, b, c, gm, out):
    total = a[...].astype(F32) + b[...].astype(F32) + c[...].astype(F32) + gm[...]
    out[...] = total.astype(BF16)


def finish(idx, a, b, c, gm):
    seq, d = a.shape
    part = pl.BlockSpec((seq // 4, d), lambda n, s: (n, 0))
    return pl.pallas_call(
        finish_kernel,
        out_shape=jax.ShapeDtypeStruct((seq, d), BF16),
        grid_spec=pltpu.PrefetchScalarGridSpec(
            num_scalar_prefetch=1, grid=(4,), in_specs=[part] * 4, out_specs=part
        ),
        compiler_params=params(8),
        cost_estimate=cost(0.0),
        name="finish",
    )(idx, a, b, c, gm)


def over(name, bit):
    size = lax.axis_size(name)
    pairs = [(i, i ^ bit) for i in range(size)]
    return lambda a: lax.ppermute(a, name, pairs)


class Order:
    def __init__(self):
        self.last = ()

    def then(self, a):
        return lax.optimization_barrier((a, self.last))[0]

    def done(self, out):
        self.last = (jax.tree.leaves(out)[-1],)
        return out

    def wait(self, *arrays):
        arrays = self.then(arrays)
        self.last = self.last + tuple(arrays)
        return arrays


def local(
    inputs, segment_ids, cotangent, query_weight, key_weight, value_weight, query_bias, value_bias,
    output_weight, output_bias, middle_gain, middle_shift, up_weight, up_bias, down_weight, down_bias,
    final_gain, final_shift,
):
    rows_here, seq = segment_ids.shape
    members = lax.axis_size("mp")
    assert members == 4 and rows_here == 4
    staged = lax.axis_size("dp") == 8
    me = lax.axis_index("mp")
    spot = lax.axis_index("dp")
    x_bit = jnp.bitwise_and(spot, 1) if staged else 0 * spot
    z_bit = jnp.bitwise_and(jnp.right_shift(spot, 1), 1) if staged else 0 * spot
    idx = jnp.stack([me, x_bit, z_bit]).astype(jnp.int32)
    core, y, both = over("mp", 1), over("mp", 2), over("mp", 3)
    x, z1, z2 = over("dp", 1), over("dp", 2), over("dp", 4)
    line = lambda v: v.reshape(1, -1)
    in_hbm = lambda a: pltpu.with_memory_space_constraint(a, pltpu.HBM)
    inputs, cotangent = in_hbm(inputs), in_hbm(cotangent)
    order = Order()
    then, done, wait = order.then, order.done, order.wait
    kernel = lambda f, *a: done(f(then(idx), *a))

    if staged:
        quarter = up_weight.shape[0] // 4
        at = (x_bit * 2 + z_bit) * quarter
        mine = [lax.dynamic_slice_in_dim(w, at, quarter, 0) for w in (up_weight, down_weight)]
        mine = done(mine)
        near_u, near_d = y(mine[0]), y(mine[1])
    u1, d1 = core(up_weight), core(down_weight)
    ub = line(up_bias)
    ub1, ub2 = core(ub), y(ub)

    weights = (query_weight.T, key_weight.T, value_weight.T, output_weight)
    fwd = (inputs, segment_ids) + weights + (line(query_bias), line(value_bias))
    *kept3, part3 = kernel(partial(attend_fwd, 3, 1), *fwd)
    from3 = core(part3)
    if staged:
        (near_u,) = wait(near_u)
        x_u, z_u = x(near_u), z1(near_u)
    *kept2, part2 = kernel(partial(attend_fwd, 2, 1), *fwd)
    if staged:
        (near_d,) = wait(near_d)
        x_d, z_d = x(near_d), z1(near_d)
    u1, d1, ub1, ub2 = wait(u1, d1, ub1, ub2)
    ub3 = core(ub2)
    other = y(done(part2 + then(from3)))
    if staged:
        x_u, z_u = wait(x_u, z_u)
        far_u = z1(x_u)
    *kept10, part1, part0 = kernel(partial(attend_fwd, 1, 2), *fwd)
    from1 = core(part1)
    if staged:
        z_d, x_d, ub3 = wait(z_d, x_d, ub3)
        far_d = x(z_d)
        (other,) = wait(other)
        far_u, far_d = wait(far_u, far_d)
        u2, d2 = kernel(join, near_u, z_u, x_u, far_u, near_d, z_d, x_d, far_d)
        u3, d3 = core(u2), core(d2)
    else:
        u2, u3, d2, d3 = y(up_weight), both(up_weight), y(down_weight), both(down_weight)
    us = (up_weight, u1, u2, u3)
    ds = (down_weight, d1, d2, d3)
    hidden, normed, inverse, low, act, slope = kernel(
        up, inputs, part0, from1, other, line(output_bias), line(middle_gain), line(middle_shift),
        us, (ub, ub1, ub2, ub3),
    )
    layer_out, grad_final, grad_low, vec_fin = kernel(
        down, act, ds, hidden, cotangent, line(down_bias), line(final_gain), line(final_shift)
    )

    gd31, first_d, second_d = kernel(partial(outer, True, False, False), grad_low, act)
    rd = core(gd31)
    gp, grad_mid, mid0, vec = done(
        back(grad_low, slope, ds, us, grad_final, normed, inverse, then(line(middle_gain)), vec_fin)
    )
    mid2, mid1 = y(mid0), core(mid0)
    vec_core = core(vec)
    half = first_d.shape[1]
    rd = then(rd)
    second_d = done(second_d + rd[:, half:])
    got_d = x(second_d) if staged else None
    gu31, far_l, near_l1, near_l2, first_r, second_r = kernel(
        partial(outer, False, True, True), low, gp
    )
    ru = core(gu31)
    in0, in1, *before = kernel(partial(attend_bwd, 0, False), inputs, (mid0, mid1), kept10, *weights)
    from_in1 = core(in1)
    n = far_l.shape[1]
    ru = then(ru)
    second_r = second_r + ru[:, half:, n:]
    far_l = done(far_l + ru[0, :, :n])
    got_r = z1(second_r) if staged else None
    got_l = y(far_l)
    (mid2,) = wait(mid2)
    mid3 = core(mid2)
    vec = done(small(partial(mix_kernel, (1, 0, 3, 2)), vec, then(vec_core)))
    vec_y = y(vec)
    in2, *before = kernel(partial(attend_bwd, 2, False), inputs, (mid2,), kept2, *weights, before)
    (vec_y,) = wait(vec_y)
    in3, first_a, second_a = kernel(
        partial(attend_bwd, 3, True), inputs, (mid3,), kept3, *weights, before, (vec, vec_y)
    )
    width = query_bias.shape[0]

    if staged:
        top = dict(rows=(0, 2))
        left, right = dict(cols=(0, 2)), dict(cols=(1, 2))
        got_a = x(second_a)
        from_in3 = core(in3)
        more_d = y(
            kernel(add_up, 1, [block(first_d, 0), block(rd, 0, **top), block(got_d, 0)])
        )
        more_r = y(
            kernel(add_up, 1, [block(first_r, 0), block(ru, 0, **top, **right), block(got_r, 0)])
        )
        more_l = z1(
            kernel(
                add_up, 1,
                [block(near_l2), block(ru, 1, rows=(1, 2), **left), block(got_l, rows=(1, 2))],
            )
        )
        keep_a, send_a = kernel(add_up, 2, [block(first_a), block(got_a)])
        got_a = z1(send_a)
        keep_d, send_d = kernel(
            add_up, 2, [block(first_d, 1), block(rd, 1, **top), block(got_d, 1), block(more_d)]
        )
        got_d = z1(send_d)
        keep_u, send_u = kernel(
            add_up, 2,
            [block(near_l1), block(ru, 1, **top, **left), block(got_l, **top), block(more_l)],
            [block(first_r, 1), block(ru, 1, **top, **right), block(got_r, 1), block(more_r)],
        )
        got_u = x(send_u)
        from_in2 = y(kernel(add_up, 1, [block(in2), block(from_in3)]))
        s_a = kernel(add_up, 1, [block(keep_a), block(got_a)])
        got_a = z2(s_a)
        s_d = kernel(add_up, 1, [block(keep_d), block(got_d)])
        got_d = z2(s_d)
        s_u = kernel(add_up, 1, [block(keep_u), block(got_u)])
        got_u = z2(s_u)
        s_a = kernel(add_up, 1, [block(s_a), block(got_a)])
        q_a, p_a = z1(s_a), x(s_a)
        input_grad = kernel(finish, in0, from_in1, from_in2, grad_mid)
        (q_a,) = wait(q_a)
        r_a = x(q_a)
        s_d = kernel(add_up, 1, [block(s_d), block(got_d)])
        q_d, p_d = z1(s_d), x(s_d)
        s_u = kernel(add_up, 1, [block(s_u), block(got_u)])
        q_u, p_u = x(s_u), z1(s_u)
        (q_d,) = wait(q_d)
        r_d = x(q_d)
        grad_q, grad_k, grad_v, grad_o, vecs = kernel(unpack, False, TAIL, (s_a, q_a, p_a, r_a))
        (q_u,) = wait(q_u)
        r_u = z1(q_u)
        (grad_down,) = kernel(unpack, False, 0, (s_d, q_d, p_d, r_d))
        (grad_up,) = kernel(unpack, True, 0, (s_u, q_u, p_u, r_u))
    else:
        input_grad = finish(idx, in0, from_in1, y(in2 + core(in3)), grad_mid)
        td = jnp.concatenate([first_d[1] + rd[1, :half], second_d[1]]) + y(
            jnp.concatenate([first_d[0] + rd[0, :half], second_d[0]])
        )
        tl = jnp.concatenate([near_l1, near_l2]) + ru[1, :, :n] + got_l
        tr = jnp.concatenate([first_r[1] + ru[1, :half, n:], second_r[1]]) + y(
            jnp.concatenate([first_r[0] + ru[0, :half, n:], second_r[0]])
        )
        tu = jnp.concatenate([tl, tr], axis=1)
        ta = jnp.concatenate([first_a, second_a])
        td, tu, ta = lax.psum((td, tu, ta), "dp")
        (grad_down,) = unpack(idx, False, 0, (td,))
        (grad_up,) = unpack(idx, True, 0, (tu,))
        grad_q, grad_k, grad_v, grad_o, vecs = unpack(idx, False, TAIL, (ta,))

    bias_up, gain_mid, shift_mid, bias_out, gain_fin, shift_fin, bias_down, bias_q, bias_v = (
        vecs[TAIL * (j // 3) + j % 3] for j in range(9)
    )
    return (
        layer_out, input_grad, grad_q.T, grad_k.T, grad_v.T, bias_q[:width], bias_v[:width], grad_o,
        bias_out, gain_mid, shift_mid, grad_up, bias_up, grad_down, bias_down, gain_fin, shift_fin,
    )


def solution(mesh):
    tokens = P("dp", None)
    columns, units, stacked, full = P(None, "mp"), P("mp"), P("mp", None), P()
    shared = P(("dp", "mp"), None)
    placed = (
        tokens, tokens, tokens, columns, columns, columns, units, units, stacked, full, full, full,
        columns, units, stacked, full, full, full,
    )
    given = (
        shared, shared, columns, columns, columns, units, units, stacked, full, full, full,
        columns, units, stacked, full, full, full,
    )
    return jax.shard_map(local, mesh=mesh, in_specs=placed, out_specs=given, check_vma=False)
```

```python
from functools import partial

import jax
import jax.numpy as jnp
from jax import lax
from jax.experimental import pallas as pl
from jax.experimental.pallas import tpu as pltpu
from jax.sharding import PartitionSpec as P

HEAD = 64
BAND = 128
EPSILON = 1e-12
ROOT_HALF = 0.7071067811865476
INV_ROOT_TAU = 0.3989422804014327
MASKED = -1e30
TAIL = 8
F32 = jnp.float32
BF16 = jnp.bfloat16
MIB = 1024 * 1024
SCALE = 4.0


def nn(a, b):
    return lax.dot_general(a, b, (((1,), (0,)), ((), ())), preferred_element_type=F32)


def nt(a, b):
    return lax.dot_general(a, b, (((1,), (1,)), ((), ())), preferred_element_type=F32)


def tn(a, b):
    return lax.dot_general(a, b, (((0,), (0,)), ((), ())), preferred_element_type=F32)


def window(block, seq):
    lo = max(block * BAND - BAND, 0)
    hi = min(block * BAND + 2 * BAND, seq)
    return lo, hi


def params(mib):
    return pltpu.CompilerParams(vmem_limit_bytes=mib * MIB)


def cost(us):
    return pl.CostEstimate(
        flops=int(us * SCALE * 1.15e9), bytes_accessed=int(us * SCALE * 3.6e6), transcendentals=0
    )


def whole(*shape):
    return pl.BlockSpec(shape, lambda *_: (0,) * len(shape), pipeline_mode=pl.Buffered(1))


def held(*shape):
    return pl.BlockSpec(shape, lambda *_: (0,) * len(shape))


def rows_of_heads(a):
    zero = jnp.zeros((HEAD, a.shape[1]), a.dtype)
    tiles = []
    for h in range(a.shape[0] // HEAD):
        mine = a[h * HEAD : (h + 1) * HEAD]
        if h % 2 == 0 and (h + 1) * HEAD == a.shape[0]:
            tiles.append(mine)
        else:
            tiles.append(jnp.concatenate([mine, zero] if h % 2 == 0 else [zero, mine], axis=0))
    return tiles


def tiles_of_heads(a):
    width = a.shape[1]
    return [a[:, h // 2 * 128 : min(h // 2 * 128 + 128, width)] for h in range(width // HEAD)]


def columns_of_heads(a):
    masked = []
    for h, tile in enumerate(tiles_of_heads(a)):
        if tile.shape[1] == HEAD:
            masked.append(tile)
        else:
            lane = lax.broadcasted_iota(jnp.int32, tile.shape, 1)
            masked.append(jnp.where((lane < HEAD) == (h % 2 == 0), tile, jnp.zeros_like(tile)))
    return masked


def store_tiles(ref, rows, per_head, scale=None):
    for at in range(0, len(per_head), 2):
        total = per_head[at] if at + 1 == len(per_head) else per_head[at] + per_head[at + 1]
        if scale is not None:
            total = total * scale
        lo = at * HEAD
        ref[rows, lo : lo + total.shape[1]] = total.astype(ref.dtype)


def attend_fwd_kernel(base, idx, x_ref, seg_ref, wq, wk, wv, wo, qb, vb,
                      q_ref, k_ref, v_ref, p_ref, ctx_ref, *parts):
    step = pl.program_id(0)
    seq = x_ref.shape[0]
    row = jnp.bitwise_xor(idx[0], base - step)
    x = x_ref[...]
    q = ((nt(x, wq[...]) + qb[...]).astype(BF16) * (HEAD**-0.5)).astype(BF16)
    k_t = nt(wk[...], x).astype(BF16)
    v = (nt(x, wv[...]) + vb[...]).astype(BF16)
    q_ref[0] = jnp.transpose(q)
    k_ref[0] = jnp.transpose(k_t)
    v_ref[0] = jnp.transpose(v)
    q_tiles, k_rows, v_cols = tiles_of_heads(q), rows_of_heads(k_t), columns_of_heads(v)
    heads = range(len(q_tiles))
    seg_row = seg_ref[pl.ds(row, 1), :]
    for i in range(seq // BAND):
        lo, hi = window(i, seq)
        rows = slice(i * BAND, (i + 1) * BAND)
        seg_k = jnp.broadcast_to(seg_row[:, lo:hi], (BAND, hi - lo))
        seg_q = jnp.transpose(jnp.broadcast_to(seg_row[:, rows], (BAND, BAND)))
        same = jnp.concatenate([seg_q] * ((hi - lo) // BAND), axis=1) == seg_k
        scores = [jnp.where(same, nn(q_tiles[h][rows], k_rows[h][:, lo:hi]), MASKED) for h in heads]
        tops = [jnp.max(a, axis=-1, keepdims=True) for a in scores]
        expos = [jnp.exp(a - m) for a, m in zip(scores, tops)]
        scales = [1.0 / jnp.sum(e, axis=-1, keepdims=True) for e in expos]
        probs = [(e * t).astype(BF16) for e, t in zip(expos, scales)]
        for h in heads:
            p_ref[0, h, rows, 0 : hi - lo] = probs[h]
        store_tiles(ctx_ref.at[0], rows, [nn(probs[h], v_cols[h][lo:hi]) for h in heads])
    part = nn(ctx_ref[0], wo[...]).astype(BF16)
    for j, ref in enumerate(parts):

        @pl.when(step == j)
        def _():
            ref[...] = part


def attend_fwd(base, count, idx, x, seg, wq, wk, wv, wo, qb, vb):
    seq = seg.shape[1]
    width, d = wq.shape
    heads = width // HEAD
    slot = lambda g, s: (g, 0, 0)
    natural = pl.BlockSpec((1, seq, width), slot)
    turned = pl.BlockSpec((1, width, seq), slot)
    saved = (
        jax.ShapeDtypeStruct((count, width, seq), BF16),
        jax.ShapeDtypeStruct((count, seq, width), BF16),
        jax.ShapeDtypeStruct((count, width, seq), BF16),
        jax.ShapeDtypeStruct((count, heads, seq, 3 * BAND), BF16),
        jax.ShapeDtypeStruct((count, seq, width), BF16),
    )
    args = (idx, x, seg, wq, wk, wv, wo, qb, vb)
    specs = [
        pl.BlockSpec((seq, d), lambda g, s: (jnp.bitwise_xor(s[0], base - g), 0)),
        whole(*seg.shape),
        whole(width, d),
        whole(width, d),
        whole(width, d),
        whole(width, d),
        whole(1, width),
        whole(1, width),
    ]
    return pl.pallas_call(
        partial(attend_fwd_kernel, base),
        out_shape=saved + (jax.ShapeDtypeStruct((seq, d), BF16),) * count,
        grid_spec=pltpu.PrefetchScalarGridSpec(
            num_scalar_prefetch=1,
            grid=(count,),
            in_specs=specs,
            out_specs=[
                turned,
                natural,
                turned,
                pl.BlockSpec((1, heads, seq, 3 * BAND), lambda g, s: (g, 0, 0, 0)),
                natural,
            ]
            + [held(seq, d)] * count,
        ),
        compiler_params=params(60 if base == 3 else 24),
        cost_estimate=cost(3.2 * count),
        name="attend_fwd",
    )(*args)


def gelu_parts(v):
    half = 0.5 * (1.0 + lax.erf(v * ROOT_HALF))
    return v * half, half + v * jnp.exp(-0.5 * v * v) * INV_ROOT_TAU


def by_rows(total, step, body, carry):
    def one(i, c):
        return body(pl.ds(pl.multiple_of(i * step, step), step), c)

    return lax.fori_loop(0, total // step, one, carry, unroll=4)


def fold(a):
    return jnp.sum(a.reshape(a.shape[0] // 8, 8, a.shape[1]), axis=0)


def up_kernel(
    idx, x_ref, pa, pb, pc, ob, gain, shift, u0, u1, u2, u3, b0, b1, b2, b3,
    hid, nrm, inv, low, act, slope,
):
    @pl.when(pl.program_id(0) == 0)
    def _():
        def body(rows, carry):
            middle = (
                pa[rows, :].astype(F32)
                + pb[rows, :].astype(F32)
                + pc[rows, :].astype(F32)
                + ob[...]
                + x_ref[rows, :].astype(F32)
            )
            centred = middle - jnp.mean(middle, axis=-1, keepdims=True)
            r = lax.rsqrt(jnp.mean(centred * centred, axis=-1, keepdims=True) + EPSILON)
            normed = centred * r
            hidden = normed * gain[...] + shift[...]
            nrm[rows, :] = normed
            inv[rows, :] = jnp.broadcast_to(r, (r.shape[0], 128))
            hid[rows, :] = hidden
            low[rows, :] = hidden.astype(BF16)
            return carry

        by_rows(low.shape[0], 64, body, 0)

    for r, (u, b) in enumerate(((u0, b0), (u1, b1), (u2, b2), (u3, b3))):
        value, deriv = gelu_parts(nn(low[...], u[...]) + b[...])
        act[r] = value.astype(BF16)
        slope[r] = deriv.astype(BF16)


def up(idx, x, own, recv, other, ob, gain, shift, us, bs):
    seq, d = other.shape
    units = us[0].shape[1]
    tile = 256
    row = pl.BlockSpec((seq, d), lambda n, s: (s[0], 0), pipeline_mode=pl.Buffered(1))
    wide = pl.BlockSpec((d, tile), lambda n, s: (0, n))
    bias = pl.BlockSpec((1, tile), lambda n, s: (0, n))
    out = pl.BlockSpec((4, seq, tile), lambda n, s: (0, 0, n))
    return pl.pallas_call(
        up_kernel,
        out_shape=(
            jax.ShapeDtypeStruct((seq, d), F32),
            jax.ShapeDtypeStruct((seq, d), F32),
            jax.ShapeDtypeStruct((seq, 128), F32),
            jax.ShapeDtypeStruct((seq, d), BF16),
            jax.ShapeDtypeStruct((4, seq, units), BF16),
            jax.ShapeDtypeStruct((4, seq, units), BF16),
        ),
        grid_spec=pltpu.PrefetchScalarGridSpec(
            num_scalar_prefetch=1,
            grid=(units // tile,),
            in_specs=[row] + [whole(seq, d)] * 3 + [whole(1, d)] * 3 + [wide] * 4 + [bias] * 4,
            out_specs=[held(seq, d), held(seq, d), held(seq, 128), held(seq, d), out, out],
        ),
        compiler_params=params(28),
        cost_estimate=cost(7.3),
        name="up",
    )(idx, x, own, recv, other, ob, gain, shift, *us, *bs)


def down_kernel(idx, act, d0, d1, d2, d3, hid, cot, db, gain, shift, out_ref, gf_ref, gl_ref, vec, acc):
    step = pl.program_id(0)
    total = None
    for r, w in enumerate((d0, d1, d2, d3)):
        term = nn(act[r], w[...])
        total = term if total is None else total + term
    acc[step] = total

    @pl.when(step == pl.num_programs(0) - 1)
    def _():
        def body(rows, carry):
            parts = [acc[n, rows, :] for n in range(acc.shape[0])]
            final = jnp.concatenate(parts, axis=1) + db[...] + hid[rows, :]
            centred = final - jnp.mean(final, axis=-1, keepdims=True)
            r = lax.rsqrt(jnp.mean(centred * centred, axis=-1, keepdims=True) + EPSILON)
            normed = centred * r
            out_ref[rows, :] = (normed * gain[...] + shift[...]).astype(BF16)
            cv = cot[rows, :].astype(F32)
            c = cv * gain[...]
            grad = r * (
                c
                - jnp.mean(c, axis=-1, keepdims=True)
                - normed * jnp.mean(c * normed, axis=-1, keepdims=True)
            )
            gf_ref[rows, :] = grad
            gl_ref[rows, :] = grad.astype(BF16)
            return tuple(a + b for a, b in zip(carry, (fold(cv * normed), fold(cv), fold(grad))))

        zero = jnp.zeros((8, hid.shape[1]), F32)
        sums = by_rows(hid.shape[0], 64, body, (zero, zero, zero))
        vec[...] = jnp.zeros_like(vec)
        for j, total in enumerate(sums):
            vec[j : j + 1, :] = jnp.sum(total, axis=0, keepdims=True)


def down(idx, act, ds, hid, cot, db, gain, shift):
    seq, d = hid.shape
    units = act.shape[2]
    tile = 256
    wide = pl.BlockSpec((units, tile), lambda n, s: (0, n))
    row = pl.BlockSpec((seq, d), lambda n, s: (s[0], 0), pipeline_mode=pl.Buffered(1))
    return pl.pallas_call(
        down_kernel,
        out_shape=(
            jax.ShapeDtypeStruct((seq, d), BF16),
            jax.ShapeDtypeStruct((seq, d), F32),
            jax.ShapeDtypeStruct((seq, d), BF16),
            jax.ShapeDtypeStruct((8, d), F32),
        ),
        grid_spec=pltpu.PrefetchScalarGridSpec(
            num_scalar_prefetch=1,
            grid=(d // tile,),
            in_specs=[whole(4, seq, units)] + [wide] * 4 + [whole(seq, d), row] + [whole(1, d)] * 3,
            out_specs=[held(seq, d), held(seq, d), held(seq, d), held(8, d)],
            scratch_shapes=[pltpu.VMEM((d // tile, seq, tile), F32)],
        ),
        compiler_params=params(24),
        cost_estimate=cost(6.2),
        name="down",
    )(idx, act, *ds, hid, cot, db, gain, shift)


def back_kernel(
    gl, slope, d0, d1, d2, d3, u0, u1, u2, u3, gf, nrm, inv, gain, vecf, gp, gm_ref, gml_ref, vec, acc
):
    step = pl.program_id(0)
    tile = slope.shape[2]
    total = None
    for r, (w_d, w_u) in enumerate(((d0, u0), (d1, u1), (d2, u2), (d3, u3))):
        pre = (nt(gl[...], w_d[...]) * slope[r].astype(F32)).astype(BF16)
        gp[r] = pre
        sums = jnp.sum(pre.astype(F32), axis=0, keepdims=True)
        vec[r : r + 1, pl.ds(pl.multiple_of(step * tile, tile), tile)] = sums
        term = nt(pre, w_u[...])
        total = term if total is None else total + term

    @pl.when(step == 0)
    def _():
        acc[...] = total

    @pl.when(step > 0)
    def _():
        acc[...] += total

    @pl.when(step == pl.num_programs(0) - 1)
    def _():
        def body(rows, carry):
            grad = acc[rows, :] + gf[rows, :]
            normed = nrm[rows, :]
            c = grad * gain[...]
            gm = inv[rows, 0:1] * (
                c
                - jnp.mean(c, axis=-1, keepdims=True)
                - normed * jnp.mean(c * normed, axis=-1, keepdims=True)
            )
            gm_ref[rows, :] = gm
            gml_ref[rows, :] = gm.astype(BF16)
            return tuple(a + b for a, b in zip(carry, (fold(grad * normed), fold(grad), fold(gm))))

        zero = jnp.zeros((8, gf.shape[1]), F32)
        sums = by_rows(gf.shape[0], 64, body, (zero, zero, zero))
        for j, total in enumerate(sums):
            vec[4 + j : 5 + j, :] = jnp.sum(total, axis=0, keepdims=True)
        vec[7:10, :] = vecf[0:3, :]
        vec[10:16, :] = jnp.zeros((6, gf.shape[1]), F32)


def back(gl, slope, ds, us, gf, nrm, inv, gain, vecf):
    seq, d = gf.shape
    units = slope.shape[2]
    tile = 256
    tall = pl.BlockSpec((4, seq, tile), lambda n: (0, 0, n))
    w_d = pl.BlockSpec((tile, d), lambda n: (n, 0))
    w_u = pl.BlockSpec((d, tile), lambda n: (0, n))
    return pl.pallas_call(
        back_kernel,
        out_shape=(
            jax.ShapeDtypeStruct((4, seq, units), BF16),
            jax.ShapeDtypeStruct((seq, d), F32),
            jax.ShapeDtypeStruct((seq, d), BF16),
            jax.ShapeDtypeStruct((16, d), F32),
        ),
        grid=(units // tile,),
        in_specs=[whole(seq, d), tall]
        + [w_d] * 4
        + [w_u] * 4
        + [whole(seq, d), whole(seq, d), whole(seq, 128), whole(1, d), whole(8, d)],
        out_specs=[tall, held(seq, d), held(seq, d), held(16, d)],
        scratch_shapes=[pltpu.VMEM((seq, d), F32)],
        compiler_params=params(28),
        cost_estimate=cost(10.8),
        name="back",
    )(gl, slope, *ds, *us, gf, nrm, inv, gain, vecf)


def place(idx, e, z_major=False):
    first, second = (idx[2], idx[1]) if z_major else (idx[1], idx[2])
    return jnp.bitwise_xor(e // 2, first) * 2 + jnp.bitwise_xor(e % 2, second)


def spread(idx, value, put, z_major=False):
    size = value.shape[0] // 4
    for e in range(4):
        put(place(idx, e, z_major), size, value[e * size : (e + 1) * size])


def slot_rows(slot, size):
    return pl.ds(pl.multiple_of(slot * size, 8), size)


def put_halves(first, second):
    def put(slot, size, piece):
        @pl.when(slot < 2)
        def _():
            first[slot_rows(slot, size), :] = piece.astype(BF16)

        @pl.when(slot >= 2)
        def _():
            second[slot_rows(slot - 2, size), :] = piece.astype(BF16)

    return put


def outer_kernel(flip, z_major, halves, idx, left, varied, out, *kept):
    step = pl.program_id(0)
    value = tn(varied[0], left[...]) if flip else tn(left[...], varied[0])

    def whole_to(ref):
        def put(slot, size, piece):
            ref[slot_rows(slot, size), :] = piece.astype(BF16)

        return put

    @pl.when(step < 2)
    def _():
        spread(idx, value, whole_to(out.at[step]), z_major)

    if not halves:
        first, second = kept

        @pl.when(step >= 2)
        def _():
            spread(idx, value, put_halves(first.at[step - 2], second.at[step - 2]), z_major)

    else:
        far_left, near_first, near_second, first, second = kept
        n = far_left.shape[1]

        @pl.when(step >= 2)
        def _():
            spread(idx, value[:, n:], put_halves(first.at[step - 2], second.at[step - 2]), z_major)

        @pl.when(step == 2)
        def _():
            spread(idx, value[:, :n], whole_to(far_left), z_major)

        @pl.when(step == 3)
        def _():
            spread(idx, value[:, :n], put_halves(near_first, near_second), z_major)


def outer(flip, z_major, halves, idx, left, varied):
    seq, d = left.shape
    units = varied.shape[2]
    rows, cols = (units, d) if flip else (d, units)
    shapes = [(2, rows, cols)]
    if halves:
        cols = cols // 2
        shapes += [(rows, cols), (rows // 2, cols), (rows // 2, cols)]
    shapes += [(2, rows // 2, cols), (2, rows // 2, cols)]
    member = lambda g, s: (jnp.where(g < 2, 3 - 2 * g, 6 - 2 * g), 0, 0)
    return pl.pallas_call(
        partial(outer_kernel, flip, z_major, halves),
        out_shape=[jax.ShapeDtypeStruct(a, BF16) for a in shapes],
        grid_spec=pltpu.PrefetchScalarGridSpec(
            num_scalar_prefetch=1,
            grid=(4,),
            in_specs=[whole(seq, d), pl.BlockSpec((1, seq, units), member)],
            out_specs=[whole(*a) for a in shapes],
        ),
        compiler_params=params(20),
        cost_estimate=cost(5.5),
        name="outer",
    )(idx, left, varied)


def attend_bwd_kernel(count, later, last, idx, x_ref, *rest):
    gmls, rest = rest[:count], rest[count:]
    q_ref, k_ref, v_ref, p_ref, ctx_ref, wq, wk, wv, wo = rest[:9]
    rest = rest[9:]
    if later:
        before, vec_before = rest[:2]
        rest = rest[2:]
    if last:
        shared, shared_y = rest[:2]
        rest = rest[2:]
    parts, rest = rest[:count], rest[count:]
    if last:
        first, second, tail, vec, grads, gq_s, gk_s, gv_s = rest
    else:
        grads, vec, gq_s, gk_s, gv_s = rest
    step = pl.program_id(0)
    seq = x_ref.shape[0]
    width = wq.shape[0]
    blocks = seq // BAND

    @pl.when(step == 0)
    def _():
        if later:
            grads[...] = before[...]
            vec[...] = vec_before[...]
        else:
            grads[...] = jnp.zeros_like(grads)
            vec[...] = jnp.zeros_like(vec)

    gml = gmls[0][...] if count == 1 else jnp.where(step == 0, gmls[0][...], gmls[1][...])
    x, ctx, q_t, k = x_ref[...], ctx_ref[0], q_ref[0], k_ref[0]
    gctx = nt(gml, wo[...]).astype(BF16)
    gctx_t = jnp.transpose(gctx)
    g_tiles, v_rows, k_cols = tiles_of_heads(gctx), rows_of_heads(v_ref[0]), columns_of_heads(k)
    heads = range(len(g_tiles))
    gk = [[None] * blocks for _ in heads]
    gv = [[None] * blocks for _ in heads]
    for i in range(blocks):
        lo, hi = window(i, seq)
        rows = slice(i * BAND, (i + 1) * BAND)
        probs_low = [p_ref[0, h, rows, 0 : hi - lo] for h in heads]
        gprobs = [nn(g_tiles[h][rows], v_rows[h][:, lo:hi]) for h in heads]
        probs = [p.astype(F32) for p in probs_low]
        dots = [jnp.sum(a * b, axis=-1, keepdims=True) for a, b in zip(gprobs, probs)]
        gscores = [(p * (g - t)).astype(BF16) for g, p, t in zip(gprobs, probs, dots)]
        store_tiles(gq_s, rows, [nn(gscores[h], k_cols[h][lo:hi]) for h in heads], HEAD**-0.5)
        for h in heads:
            mine = slice(h * HEAD, (h + 1) * HEAD)
            gk_i = nn(q_t[mine, rows], gscores[h])
            gv_i = nn(gctx_t[mine, rows], probs_low[h])
            for j in range(lo // BAND, hi // BAND):
                at = slice(j * BAND - lo, (j + 1) * BAND - lo)
                gk[h][j] = gk_i[:, at] if gk[h][j] is None else gk[h][j] + gk_i[:, at]
                gv[h][j] = gv_i[:, at] if gv[h][j] is None else gv[h][j] + gv_i[:, at]
    for h in heads:
        mine = slice(h * HEAD, (h + 1) * HEAD)
        for j in range(blocks):
            cols = slice(j * BAND, (j + 1) * BAND)
            gk_s[mine, cols] = gk[h][j].astype(BF16)
            gv_s[mine, cols] = gv[h][j].astype(BF16)
    gq, gk_t, gv_t = gq_s[...], gk_s[...], gv_s[...]
    gv_n = jnp.transpose(gv_t)
    grads[0:width] += tn(gq, x)
    grads[width : 2 * width] += nn(gk_t, x)
    grads[2 * width : 3 * width] += nn(gv_t, x)
    grads[3 * width : 4 * width] += tn(ctx, gml)
    vec[0:1, 0:width] += jnp.sum(gq.astype(F32), axis=0, keepdims=True)
    vec[1:2, 0:width] += jnp.sum(gv_n.astype(F32), axis=0, keepdims=True)
    part = (nn(gq, wq[...]) + nn(jnp.transpose(gk_t), wk[...]) + nn(gv_n, wv[...])).astype(BF16)

    for j, ref in enumerate(parts):

        @pl.when(step == j)
        def _():
            ref[...] = part

    if last:

        @pl.when(step == count - 1)
        def _():
            tail[...] = jnp.zeros_like(tail)
            tail[0:1, :] = shared[0:1, :] + shared_y[2:3, :]
            for j in range(6):
                at = TAIL * ((j + 1) // 3) + (j + 1) % 3
                tail[at : at + 1, :] = shared[4 + j : 5 + j, :] + shared_y[4 + j : 5 + j, :]
            tail[2 * TAIL + 1 : 2 * TAIL + 3, :] = vec[0:2, :]
            for e in range(4):
                body = grads[e * width : (e + 1) * width]
                both = jnp.concatenate([body, tail[e * TAIL : (e + 1) * TAIL]], axis=0)
                put_halves(first, second)(place(idx, e), width + TAIL, both)


def attend_bwd(base, last, idx, x, gmls, kept, wq, wk, wv, wo, before=None, shared=()):
    q, k, v, p, ctx = kept
    width, d = wq.shape
    seq = gmls[0].shape[0]
    heads = width // HEAD
    count = len(gmls)
    later = before is not None
    slot = lambda g, s: (count - 1 - g, 0, 0)
    natural = pl.BlockSpec((1, seq, width), slot)
    turned = pl.BlockSpec((1, width, seq), slot)
    specs = [
        pl.BlockSpec((seq, d), lambda g, s: (jnp.bitwise_xor(s[0], base + g), 0)),
    ] + [whole(seq, d)] * count + [
        turned,
        natural,
        turned,
        pl.BlockSpec((1, heads, seq, 3 * BAND), lambda g, s: (count - 1 - g, 0, 0, 0)),
        natural,
    ] + [whole(width, d)] * 4
    args = (idx, x, *gmls, q, k, v, p, ctx, wq, wk, wv, wo)
    part = jax.ShapeDtypeStruct((seq, d), BF16)
    small = jax.ShapeDtypeStruct((8, d), F32)
    scratch = [
        pltpu.VMEM((seq, width), BF16),
        pltpu.VMEM((width, seq), BF16),
        pltpu.VMEM((width, seq), BF16),
    ]
    if later:
        specs += [whole(4 * width, d), whole(8, d)]
        args += tuple(before)
    if last:
        specs += [whole(16, d)] * 2
        args += tuple(shared)
        half = 2 * (width + TAIL)
        shapes = (part,) * count + (jax.ShapeDtypeStruct((half, d), BF16),) * 2
        outs = [held(seq, d)] * count + [held(half, d)] * 2
        scratch = [
            pltpu.VMEM((4 * TAIL, d), F32), pltpu.VMEM((8, d), F32), pltpu.VMEM((4 * width, d), F32)
        ] + scratch
    else:
        shapes = (part,) * count + (jax.ShapeDtypeStruct((4 * width, d), F32), small)
        outs = [held(seq, d)] * count + [held(4 * width, d), held(8, d)]
    return pl.pallas_call(
        partial(attend_bwd_kernel, count, later, last),
        out_shape=shapes,
        grid_spec=pltpu.PrefetchScalarGridSpec(
            num_scalar_prefetch=1, grid=(count,), in_specs=specs, out_specs=outs, scratch_shapes=scratch
        ),
        compiler_params=params(28),
        cost_estimate=cost(5.0 if later else 10.0),
        name="attend_bwd",
    )(*args)


def join_kernel(idx, *refs):
    pieces, outs = refs[:-2], refs[-2:]
    rows = pieces[0].shape[0]
    for j, piece in enumerate(pieces):
        at = place(idx, j % 4)
        outs[j // 4][slot_rows(at, rows), :] = piece[...]


def join(idx, *pieces):
    rows, d = pieces[0].shape
    return pl.pallas_call(
        join_kernel,
        out_shape=[jax.ShapeDtypeStruct((4 * rows, d), BF16)] * 2,
        grid_spec=pltpu.PrefetchScalarGridSpec(
            num_scalar_prefetch=1,
            grid=(1,),
            in_specs=[whole(rows, d)] * 8,
            out_specs=[whole(4 * rows, d)] * 2,
        ),
        compiler_params=params(8),
        cost_estimate=cost(1.0),
        name="join",
    )(idx, *pieces)


def unpack_kernel(z_major, given, tail, idx, *refs):
    pieces, outs = refs[:given], refs[given:]
    size = pieces[0].shape[0] * given // 4
    body = size - tail
    for slot in range(4):
        piece = pieces[slot][...] if given == 4 else pieces[0][slot * size : (slot + 1) * size]
        at = place(idx, slot, z_major)
        if not tail:
            outs[0][slot_rows(at, size), :] = piece.astype(F32)
        else:
            outs[4][slot_rows(at, tail), :] = piece[body:].astype(F32)
            for j in range(4):

                @pl.when(at == j)
                def _():
                    outs[j][...] = piece[:body].astype(F32)


def unpack(idx, z_major, tail, pieces):
    d = pieces[0].shape[1]
    total = sum(p.shape[0] for p in pieces)
    shapes = [(total // 4 - tail, d)] * 4 + [(4 * tail, d)] if tail else [(total, d)]
    return pl.pallas_call(
        partial(unpack_kernel, z_major, len(pieces), tail),
        out_shape=[jax.ShapeDtypeStruct(a, F32) for a in shapes],
        grid_spec=pltpu.PrefetchScalarGridSpec(
            num_scalar_prefetch=1,
            grid=(1,),
            in_specs=[whole(*p.shape) for p in pieces],
            out_specs=[whole(*a) for a in shapes],
        ),
        compiler_params=params(10),
        cost_estimate=cost(0.0),
        name="unpack",
    )(idx, *pieces)


def mix_kernel(order, v, r, out):
    for j, other in enumerate(order):
        out[j : j + 1, :] = v[j : j + 1, :] + r[other : other + 1, :]
    out[len(order) :, :] = v[len(order) :, :] + r[len(order) :, :]


def small(kernel, *arrays):
    return pl.pallas_call(
        kernel,
        out_shape=jax.ShapeDtypeStruct(arrays[0].shape, F32),
        compiler_params=params(4),
        cost_estimate=cost(0.5),
        name="small",
    )(*arrays)


def block(array, *index, rows=None, cols=None):
    (r, n_r), (c, n_c) = rows or (0, 1), cols or (0, 1)
    shape = (1,) * len(index) + (array.shape[-2] // n_r, array.shape[-1] // n_c)
    return array, shape, index + (r, c)


def add_up_kernel(sizes, idx, *refs):
    outs = refs[sum(sizes) :]
    col = 0
    for size in sizes:
        total = None
        for ref in refs[:size]:
            piece = ref[...]
            piece = piece.reshape(piece.shape[-2:]).astype(F32)
            total = piece if total is None else total + piece
        refs = refs[size:]
        cols = slice(col, col + total.shape[1])
        col += total.shape[1]
        n = outs[0].shape[0]
        for j, out in enumerate(outs):
            out[:, cols] = total[j * n : (j + 1) * n].astype(BF16)


def add_up(idx, pieces, *parts):
    blocks = [b for part in parts for b in part]
    rows = blocks[0][1][-2] // pieces
    cols = sum(part[0][1][-1] for part in parts)
    out = pl.pallas_call(
        partial(add_up_kernel, tuple(len(part) for part in parts)),
        out_shape=[jax.ShapeDtypeStruct((rows, cols), BF16)] * pieces,
        grid_spec=pltpu.PrefetchScalarGridSpec(
            num_scalar_prefetch=1,
            grid=(1,),
            in_specs=[
                pl.BlockSpec(b[1], partial(lambda at, g, s: at, b[2]), pipeline_mode=pl.Buffered(1))
                for b in blocks
            ],
            out_specs=[whole(rows, cols)] * pieces,
        ),
        compiler_params=params(12),
        cost_estimate=cost(0.02),
        name="add_up",
    )(idx, *(b[0] for b in blocks))
    return out if pieces > 1 else out[0]


def finish_kernel(idx, a, b, c, gm, out):
    total = a[...].astype(F32) + b[...].astype(F32) + c[...].astype(F32) + gm[...]
    out[...] = total.astype(BF16)


def finish(idx, a, b, c, gm):
    seq, d = a.shape
    part = pl.BlockSpec((seq // 4, d), lambda n, s: (n, 0))
    return pl.pallas_call(
        finish_kernel,
        out_shape=jax.ShapeDtypeStruct((seq, d), BF16),
        grid_spec=pltpu.PrefetchScalarGridSpec(
            num_scalar_prefetch=1, grid=(4,), in_specs=[part] * 4, out_specs=part
        ),
        compiler_params=params(8),
        cost_estimate=cost(0.0),
        name="finish",
    )(idx, a, b, c, gm)


def over(name, bit):
    size = lax.axis_size(name)
    pairs = [(i, i ^ bit) for i in range(size)]
    return lambda a: lax.ppermute(a, name, pairs)


class Order:
    def __init__(self):
        self.last = ()

    def then(self, a):
        return lax.optimization_barrier((a, self.last))[0]

    def done(self, out):
        self.last = (jax.tree.leaves(out)[-1],)
        return out

    def wait(self, *arrays):
        arrays = self.then(arrays)
        self.last = self.last + tuple(arrays)
        return arrays


def local(
    inputs, segment_ids, cotangent, query_weight, key_weight, value_weight, query_bias, value_bias,
    output_weight, output_bias, middle_gain, middle_shift, up_weight, up_bias, down_weight, down_bias,
    final_gain, final_shift,
):
    rows_here, seq = segment_ids.shape
    members = lax.axis_size("mp")
    assert members == 4 and rows_here == 4
    staged = lax.axis_size("dp") == 8
    me = lax.axis_index("mp")
    spot = lax.axis_index("dp")
    x_bit = jnp.bitwise_and(spot, 1) if staged else 0 * spot
    z_bit = jnp.bitwise_and(jnp.right_shift(spot, 1), 1) if staged else 0 * spot
    idx = jnp.stack([me, x_bit, z_bit]).astype(jnp.int32)
    core, y, both = over("mp", 1), over("mp", 2), over("mp", 3)
    x, z1, z2 = over("dp", 1), over("dp", 2), over("dp", 4)
    line = lambda v: v.reshape(1, -1)
    in_hbm = lambda a: pltpu.with_memory_space_constraint(a, pltpu.HBM)
    inputs, cotangent = in_hbm(inputs), in_hbm(cotangent)
    order = Order()
    then, done, wait = order.then, order.done, order.wait
    kernel = lambda f, *a: done(f(then(idx), *a))

    if staged:
        quarter = up_weight.shape[0] // 4
        at = (x_bit * 2 + z_bit) * quarter
        mine = [lax.dynamic_slice_in_dim(w, at, quarter, 0) for w in (up_weight, down_weight)]
        mine = done(mine)
        near_u, near_d = y(mine[0]), y(mine[1])
    u1, d1 = core(up_weight), core(down_weight)
    ub = line(up_bias)
    ub1, ub2 = core(ub), y(ub)

    weights = (query_weight.T, key_weight.T, value_weight.T, output_weight)
    fwd = (inputs, segment_ids) + weights + (line(query_bias), line(value_bias))
    *kept3, part3 = kernel(partial(attend_fwd, 3, 1), *fwd)
    from3 = core(part3)
    if staged:
        (near_u,) = wait(near_u)
        x_u, z_u = x(near_u), z1(near_u)
    *kept2, part2 = kernel(partial(attend_fwd, 2, 1), *fwd)
    if staged:
        (near_d,) = wait(near_d)
        x_d, z_d = x(near_d), z1(near_d)
    u1, d1, ub1, ub2 = wait(u1, d1, ub1, ub2)
    ub3 = core(ub2)
    other = y(done(part2 + then(from3)))
    if staged:
        x_u, z_u = wait(x_u, z_u)
        far_u = z1(x_u)
    *kept10, part1, part0 = kernel(partial(attend_fwd, 1, 2), *fwd)
    from1 = core(part1)
    if staged:
        z_d, x_d, ub3 = wait(z_d, x_d, ub3)
        far_d = x(z_d)
        (other,) = wait(other)
        far_u, far_d = wait(far_u, far_d)
        u2, d2 = kernel(join, near_u, z_u, x_u, far_u, near_d, z_d, x_d, far_d)
        u3, d3 = core(u2), core(d2)
    else:
        u2, u3, d2, d3 = y(up_weight), both(up_weight), y(down_weight), both(down_weight)
    us = (up_weight, u1, u2, u3)
    ds = (down_weight, d1, d2, d3)
    hidden, normed, inverse, low, act, slope = kernel(
        up, inputs, part0, from1, other, line(output_bias), line(middle_gain), line(middle_shift),
        us, (ub, ub1, ub2, ub3),
    )
    layer_out, grad_final, grad_low, vec_fin = kernel(
        down, act, ds, hidden, cotangent, line(down_bias), line(final_gain), line(final_shift)
    )

    gd31, first_d, second_d = kernel(partial(outer, True, False, False), grad_low, act)
    rd = core(gd31)
    gp, grad_mid, mid0, vec = done(
        back(grad_low, slope, ds, us, grad_final, normed, inverse, then(line(middle_gain)), vec_fin)
    )
    mid2, mid1 = y(mid0), core(mid0)
    vec_core = core(vec)
    half = first_d.shape[1]
    rd = then(rd)
    second_d = done(second_d + rd[:, half:])
    got_d = x(second_d) if staged else None
    gu31, far_l, near_l1, near_l2, first_r, second_r = kernel(
        partial(outer, False, True, True), low, gp
    )
    ru = core(gu31)
    in0, in1, *before = kernel(partial(attend_bwd, 0, False), inputs, (mid0, mid1), kept10, *weights)
    from_in1 = core(in1)
    n = far_l.shape[1]
    ru = then(ru)
    second_r = second_r + ru[:, half:, n:]
    far_l = done(far_l + ru[0, :, :n])
    got_r = z1(second_r) if staged else None
    got_l = y(far_l)
    (mid2,) = wait(mid2)
    mid3 = core(mid2)
    vec = done(small(partial(mix_kernel, (1, 0, 3, 2)), vec, then(vec_core)))
    vec_y = y(vec)
    in2, *before = kernel(partial(attend_bwd, 2, False), inputs, (mid2,), kept2, *weights, before)
    (vec_y,) = wait(vec_y)
    in3, first_a, second_a = kernel(
        partial(attend_bwd, 3, True), inputs, (mid3,), kept3, *weights, before, (vec, vec_y)
    )
    width = query_bias.shape[0]

    if staged:
        top = dict(rows=(0, 2))
        left, right = dict(cols=(0, 2)), dict(cols=(1, 2))
        got_a = x(second_a)
        from_in3 = core(in3)
        more_d = y(
            kernel(add_up, 1, [block(first_d, 0), block(rd, 0, **top), block(got_d, 0)])
        )
        more_r = y(
            kernel(add_up, 1, [block(first_r, 0), block(ru, 0, **top, **right), block(got_r, 0)])
        )
        more_l = z1(
            kernel(
                add_up, 1,
                [block(near_l2), block(ru, 1, rows=(1, 2), **left), block(got_l, rows=(1, 2))],
            )
        )
        keep_a, send_a = kernel(add_up, 2, [block(first_a), block(got_a)])
        got_a = z1(send_a)
        keep_d, send_d = kernel(
            add_up, 2, [block(first_d, 1), block(rd, 1, **top), block(got_d, 1), block(more_d)]
        )
        got_d = z1(send_d)
        keep_u, send_u = kernel(
            add_up, 2,
            [block(near_l1), block(ru, 1, **top, **left), block(got_l, **top), block(more_l)],
            [block(first_r, 1), block(ru, 1, **top, **right), block(got_r, 1), block(more_r)],
        )
        got_u = x(send_u)
        from_in2 = y(kernel(add_up, 1, [block(in2), block(from_in3)]))
        s_a = kernel(add_up, 1, [block(keep_a), block(got_a)])
        got_a = z2(s_a)
        s_d = kernel(add_up, 1, [block(keep_d), block(got_d)])
        got_d = z2(s_d)
        s_u = kernel(add_up, 1, [block(keep_u), block(got_u)])
        got_u = z2(s_u)
        s_a = kernel(add_up, 1, [block(s_a), block(got_a)])
        q_a, p_a = z1(s_a), x(s_a)
        input_grad = kernel(finish, in0, from_in1, from_in2, grad_mid)
        (q_a,) = wait(q_a)
        r_a = x(q_a)
        s_d = kernel(add_up, 1, [block(s_d), block(got_d)])
        q_d, p_d = z1(s_d), x(s_d)
        s_u = kernel(add_up, 1, [block(s_u), block(got_u)])
        q_u, p_u = x(s_u), z1(s_u)
        (q_d,) = wait(q_d)
        r_d = x(q_d)
        grad_q, grad_k, grad_v, grad_o, vecs = kernel(unpack, False, TAIL, (s_a, q_a, p_a, r_a))
        (q_u,) = wait(q_u)
        r_u = z1(q_u)
        (grad_up,) = kernel(unpack, True, 0, (s_u, q_u, p_u, r_u))
        (grad_down,) = kernel(unpack, False, 0, (s_d, q_d, p_d, r_d))
    else:
        input_grad = finish(idx, in0, from_in1, y(in2 + core(in3)), grad_mid)
        td = jnp.concatenate([first_d[1] + rd[1, :half], second_d[1]]) + y(
            jnp.concatenate([first_d[0] + rd[0, :half], second_d[0]])
        )
        tl = jnp.concatenate([near_l1, near_l2]) + ru[1, :, :n] + got_l
        tr = jnp.concatenate([first_r[1] + ru[1, :half, n:], second_r[1]]) + y(
            jnp.concatenate([first_r[0] + ru[0, :half, n:], second_r[0]])
        )
        tu = jnp.concatenate([tl, tr], axis=1)
        ta = jnp.concatenate([first_a, second_a])
        td, tu, ta = lax.psum((td, tu, ta), "dp")
        (grad_down,) = unpack(idx, False, 0, (td,))
        (grad_up,) = unpack(idx, True, 0, (tu,))
        grad_q, grad_k, grad_v, grad_o, vecs = unpack(idx, False, TAIL, (ta,))

    bias_up, gain_mid, shift_mid, bias_out, gain_fin, shift_fin, bias_down, bias_q, bias_v = (
        vecs[TAIL * (j // 3) + j % 3] for j in range(9)
    )
    return (
        layer_out, input_grad, grad_q.T, grad_k.T, grad_v.T, bias_q[:width], bias_v[:width], grad_o,
        bias_out, gain_mid, shift_mid, grad_up, bias_up, grad_down, bias_down, gain_fin, shift_fin,
    )


def solution(mesh):
    tokens = P("dp", None)
    columns, units, stacked, full = P(None, "mp"), P("mp"), P("mp", None), P()
    shared = P(("dp", "mp"), None)
    placed = (
        tokens, tokens, tokens, columns, columns, columns, units, units, stacked, full, full, full,
        columns, units, stacked, full, full, full,
    )
    given = (
        shared, shared, columns, columns, columns, units, units, stacked, full, full, full,
        columns, units, stacked, full, full, full,
    )
    return jax.shard_map(local, mesh=mesh, in_specs=placed, out_specs=given, check_vma=False)
```
